32 devices in a mesh: grp: 4 (over z), seq: 8 (over y, x, core).
Axes of the slice: x: 2, y: 2, z: 4, core: 2. Of those that a mesh axis runs over, the one named last changes fastest.
Arguments:
- tokens: bfloat16 [128, 256, 768], P(('grp', 'seq')), may hold values from -6 to 6
- cotangent: bfloat16 [128, 256, 768], P(('grp', 'seq')), may hold values from -6 to 6
- frame_clip: int32 [128], P('grp'), may hold values from 0 to 15, as said below
- frame_valid: int32 [128], P('grp'), may hold values from 0 to 1, as said below
- place_valid: int32 [16, 256], P('grp'), may hold values from 0 to 1, as said below
- time_gain: float32 [768], P('seq'), may hold values from 0.5 to 1.5
- time_shift: float32 [768], P('seq'), may hold values from -1.75 to 1.75
- time_inward: float32 [768, 2304], P('grp', 'seq'), may hold values from -0.21875 to 0.21875
- time_inward_bias: float32 [1536], P('seq'), may hold values from -1.75 to 1.75
- time_outward: float32 [768, 768], P('grp', 'seq'), may hold values from -0.3125 to 0.3125
- time_outward_bias: float32 [768], P('seq'), may hold values from -1.75 to 1.75
- time_linear: float32 [768, 768], P('grp', 'seq'), may hold values from -0.21875 to 0.21875
- time_linear_bias: float32 [768], P('seq'), may hold values from -1.75 to 1.75
- space_gain: float32 [768], P('seq'), may hold values from 0.5 to 1.5
- space_shift: float32 [768], P('seq'), may hold values from -1.75 to 1.75
- space_inward: float32 [768, 2304], P('grp', 'seq'), may hold values from -0.21875 to 0.21875
- space_inward_bias: float32 [1536], P('seq'), may hold values from -1.75 to 1.75
- space_outward: float32 [768, 768], P('grp', 'seq'), may hold values from -0.875 to 0.875
- space_outward_bias: float32 [768], P('seq'), may hold values from -1.75 to 1.75
- feed_gain: float32 [768], P('seq'), may hold values from 0.5 to 1.5
- feed_shift: float32 [768], P('seq'), may hold values from -1.75 to 1.75
- feed_expand: float32 [768, 3072], P('grp', 'seq'), may hold values from -0.21875 to 0.21875
- feed_expand_bias: float32 [3072], P('seq'), may hold values from -1.75 to 1.75
- feed_reduce: float32 [3072, 768], P('grp', 'seq'), may hold values from -0.15625 to 0.15625
- feed_reduce_bias: float32 [768], P('seq'), may hold values from -1.75 to 1.75
Outputs:
- result: bfloat16 [128, 256, 768], P(('grp', 'seq'))
- input_gradient: float32 [128, 256, 768], P(('grp', 'seq'))
- gradient_time_gain: float32 [768], P('seq')
- gradient_time_shift: float32 [768], P('seq')
- gradient_time_inward: float32 [768, 2304], P('grp', 'seq')
- gradient_time_inward_bias: float32 [1536], P('seq')
- gradient_time_outward: float32 [768, 768], P('grp', 'seq')
- gradient_time_outward_bias: float32 [768], P('seq')
- gradient_time_linear: float32 [768, 768], P('grp', 'seq')
- gradient_time_linear_bias: float32 [768], P('seq')
- gradient_space_gain: float32 [768], P('seq')
- gradient_space_shift: float32 [768], P('seq')
- gradient_space_inward: float32 [768, 2304], P('grp', 'seq')
- gradient_space_inward_bias: float32 [1536], P('seq')
- gradient_space_outward: float32 [768, 768], P('grp', 'seq')
- gradient_space_outward_bias: float32 [768], P('seq')
- gradient_feed_gain: float32 [768], P('seq')
- gradient_feed_shift: float32 [768], P('seq')
- gradient_feed_expand: float32 [768, 3072], P('grp', 'seq')
- gradient_feed_expand_bias: float32 [3072], P('seq')
- gradient_feed_reduce: float32 [3072, 768], P('grp', 'seq')
- gradient_feed_reduce_bias: float32 [768], P('seq')
The draws below stay inside these ranges and needn't reach their ends.
Inputs may be any that keep to these rules, and one draw needn't show every extreme that they name: `frame_clip`: the g-th run of 32 consecutive frames belongs to the clips g * 4 to g * 4 + 3, each clip having exactly 8 of these frames, in any order. `frame_valid`: every clip has at least 4 valid frames. `place_valid`: in every clip the valid places are the first ones, at least 128 of them.
All inputs are finite; a program needn't handle non-finite values.
Results may differ from the reference program's by a relative error of at most 0.02.
Values may be sent and summed in bfloat16 or wider, within the bound.
A program may use at most 256 MiB of HBM per device.

```python
import jax
import jax.numpy as jnp
from jax import lax

D = 768
HEADS = 12
FF = 3072
HEAD_DIM = 64
PLACES = 256
FRAMES_CLIP = 8
CLIP_GRP = 4
CLIPS = 16
FRAMES = 128


def frame_layout(key, part):
    base = jax.random.fold_in(key, part)
    group_count = CLIPS // CLIP_GRP
    slot_count = CLIP_GRP * FRAMES_CLIP
    group_keys = jax.random.split(jax.random.fold_in(base, 101), group_count)
    orders = jax.vmap(lambda subkey: jax.random.permutation(subkey, slot_count))(group_keys).astype(jnp.int32)
    counts = jax.random.randint(jax.random.fold_in(base, 202), (group_count, CLIP_GRP), FRAMES_CLIP // 2, FRAMES_CLIP + 1).astype(jnp.int32)
    local_clip = orders // FRAMES_CLIP
    within = orders % FRAMES_CLIP
    first_clip = jnp.arange(group_count, dtype=jnp.int32)[:, None] * CLIP_GRP
    clip_ids = first_clip + local_clip
    count_of = jnp.take_along_axis(counts, local_clip, axis=1)
    validity = (within < count_of).astype(jnp.int32)
    return (clip_ids.reshape(-1).astype(jnp.int32), validity.reshape(-1))


def draw_frame_clip(key, part):
    return frame_layout(key, part)[0]


def draw_frame_valid(key, part):
    return frame_layout(key, part)[1]


def draw_place_valid(key, part):
    base = jax.random.fold_in(key, part)
    counts = jax.random.randint(jax.random.fold_in(base, 303), (CLIPS, 1), PLACES // 2, 7 * PLACES // 8 + 1)
    return (jnp.arange(PLACES, dtype=jnp.int32)[None, :] < counts.astype(jnp.int32)).astype(jnp.int32)


def block_scale(rng, extent, pieces, smallest, high):
    level, own = 1.0, jax.random.fold_in(rng, 6)
    for dim, shards_of in pieces:
        steps = jnp.exp(jax.random.uniform(jax.random.fold_in(own, dim), (shards_of,), jnp.float32, smallest / len(pieces), high / len(pieces)))
        level = level * jnp.repeat(steps, extent[dim] // shards_of).reshape([-1 if axis == dim else 1 for axis in range(len(extent))])
    return level


def centred(own_key, extent, scale, bound, pieces=(), held_as=jnp.bfloat16):
    result = jax.random.normal(own_key, extent, jnp.float32) * scale
    if len(pieces) > 0:
        result = block_scale(own_key, extent, pieces, -0.22, 0.18) * result
    return jnp.clip(result, min=-bound, max=bound).astype(held_as)


def setup_inputs(seed: int = 0) -> dict:
    key_of = jax.random.split(jax.random.key(seed), 26)
    return {
        "tokens": centred(key_of[0], (FRAMES, PLACES, D), 1.0, 6.0, ((0, 32),)),
        "cotangent": centred(key_of[1], (FRAMES, PLACES, D), 1.0, 6.0, ((0, 32),)),
        "frame_clip": draw_frame_clip(jax.random.fold_in(key_of[25], 71), 0),
        "frame_valid": draw_frame_valid(jax.random.fold_in(key_of[25], 71), 0),
        "place_valid": draw_place_valid(jax.random.fold_in(key_of[25], 71), 0),
        "time_gain": jnp.clip(1.0 + 0.1 * jax.random.normal(key_of[5], (D,), jnp.float32), 0.5, 1.5),
        "time_shift": centred(key_of[6], (D,), 0.3, 1.75, ((0, 8),), jnp.float32),
        "time_inward": centred(key_of[7], (D, 3 * D), D ** -0.5, 0.21875, ((0, 4), (1, 8)), jnp.float32),
        "time_inward_bias": centred(key_of[8], (2 * D,), 0.3, 1.75, ((0, 8),), jnp.float32),
        "time_outward": centred(key_of[9], (D, D), (D // 2) ** -0.5, 0.3125, ((0, 4), (1, 8)), jnp.float32),
        "time_outward_bias": centred(key_of[10], (D,), 0.3, 1.75, ((0, 8),), jnp.float32),
        "time_linear": centred(key_of[11], (D, D), D ** -0.5, 0.21875, ((0, 4), (1, 8)), jnp.float32),
        "time_linear_bias": centred(key_of[12], (D,), 0.3, 1.75, ((0, 8),), jnp.float32),
        "space_gain": jnp.clip(1.0 + 0.1 * jax.random.normal(key_of[13], (D,), jnp.float32), 0.5, 1.5),
        "space_shift": centred(key_of[14], (D,), 0.3, 1.75, ((0, 8),), jnp.float32),
        "space_inward": centred(key_of[15], (D, 3 * D), D ** -0.5, 0.21875, ((0, 4), (1, 8)), jnp.float32),
        "space_inward_bias": centred(key_of[16], (2 * D,), 0.3, 1.75, ((0, 8),), jnp.float32),
        "space_outward": centred(key_of[17], (D, D), (D // 16) ** -0.5, 0.875, ((0, 4), (1, 8)), jnp.float32),
        "space_outward_bias": centred(key_of[18], (D,), 0.3, 1.75, ((0, 8),), jnp.float32),
        "feed_gain": jnp.clip(1.0 + 0.1 * jax.random.normal(key_of[19], (D,), jnp.float32), 0.5, 1.5),
        "feed_shift": centred(key_of[20], (D,), 0.3, 1.75, ((0, 8),), jnp.float32),
        "feed_expand": centred(key_of[21], (D, FF), D ** -0.5, 0.21875, ((0, 4), (1, 8)), jnp.float32),
        "feed_expand_bias": centred(key_of[22], (FF,), 0.3, 1.75, ((0, 8),), jnp.float32),
        "feed_reduce": centred(key_of[23], (FF, D), (FF // 2) ** -0.5, 0.15625, ((0, 4), (1, 8)), jnp.float32),
        "feed_reduce_bias": centred(key_of[24], (D,), 0.3, 1.75, ((0, 8),), jnp.float32),
    }


EPSILON = 1e-06

@jax.custom_vjp
def low(v):
    return lax.optimization_barrier(v.astype(jnp.bfloat16)).astype(jnp.float32)

@jax.custom_vjp
def low_back(v):
    return v

def low_keep(v):
    return (low(v), None)

def low_pass(kept, grad):
    return (grad,)

def back_keep(v):
    return (v, None)

def back_low(kept, grad):
    return (low(grad),)
low.defvjp(low_keep, low_pass)
low_back.defvjp(back_keep, back_low)

def matmul(former, latter):
    return jnp.dot(former, latter, precision=lax.Precision.HIGHEST, preferred_element_type=jnp.float32)

def product(pattern, former, latter):
    return jnp.einsum(pattern, former, latter, precision=lax.Precision.HIGHEST, preferred_element_type=jnp.float32)

def normalize(inputs, scaling, offset):
    average = lax.optimization_barrier(jnp.mean(inputs, axis=-1, keepdims=True))
    centered = inputs - average
    variance = lax.optimization_barrier(jnp.mean(centered * centered, axis=-1, keepdims=True))
    return centered * lax.rsqrt(variance + EPSILON) * scaling + offset

def attention(normed, inward, inward_bias, allowed, score_form, mix_form, leading):
    padding = jnp.zeros((D,), jnp.float32)
    full_bias = jnp.concatenate([inward_bias[:D], padding, inward_bias[D:]])
    joined = low(low_back(matmul(low(normed), inward) + full_bias))
    joined = joined.reshape(leading + (3, HEADS, HEAD_DIM))
    queries = joined[:, :, 0]
    keys_in = joined[:, :, 1]
    values = joined[:, :, 2]
    scores = low_back(product(score_form, queries, keys_in) * HEAD_DIM ** (-0.5))
    chances = low(jax.nn.softmax(jnp.where(allowed, scores, -1e+30), axis=-1))
    return low(low_back(product(mix_form, chances, values).reshape(-1, D)))

def group_layer(rounded, grouped):
    time_gain, time_shift, time_inward, time_inward_bias, time_outward, time_outward_bias, time_linear, time_linear_bias, space_gain, space_shift, space_inward, space_inward_bias, space_outward, space_outward_bias, feed_gain, feed_shift, feed_expand, feed_expand_bias, feed_reduce, feed_reduce_bias = rounded
    rows_in, clip_ids, frame_flags, place_flags = grouped
    leading = (CLIP_GRP * FRAMES_CLIP, PLACES)
    flat_rows = rows_in.reshape(-1, D)
    time_allowed = ((clip_ids[:, None] == clip_ids[None, :]) & (frame_flags[None, :] == 1))[None, None]
    time_mixed = attention(normalize(flat_rows, time_gain, time_shift), time_inward, time_inward_bias, time_allowed, 'fphd,gphd->phfg', 'phfg,gphd->fphd', leading)
    time_proj = low(low_back(matmul(time_mixed, time_outward) + time_outward_bias))
    first_sum = flat_rows + low_back(matmul(time_proj, time_linear) + time_linear_bias)
    space_allowed = (place_flags == 1)[:, None, None, :]
    space_mixed = attention(normalize(first_sum, space_gain, space_shift), space_inward, space_inward_bias, space_allowed, 'fphd,fqhd->fhpq', 'fhpq,fqhd->fphd', leading)
    second_sum = first_sum + low_back(matmul(space_mixed, space_outward) + space_outward_bias)
    hidden = low_back(matmul(low(normalize(second_sum, feed_gain, feed_shift)), feed_expand) + feed_expand_bias)
    activated = low(jax.nn.gelu(hidden, approximate=False))
    final_sum = second_sum + low_back(matmul(activated, feed_reduce) + feed_reduce_bias)
    return final_sum.reshape(rows_in.shape)

def layer(inputs, parameters, frame_clip, frame_valid, key_places):
    rounded = tuple((low(member) for member in parameters))
    group_count = FRAMES // (CLIP_GRP * FRAMES_CLIP)
    single = jax.checkpoint(group_layer)
    stacked = (inputs.reshape(group_count, -1, PLACES, D), frame_clip.reshape(group_count, -1), frame_valid.reshape(group_count, -1), key_places.reshape(group_count, -1, PLACES))
    outputs = lax.map(lambda grouped: single(rounded, grouped), stacked)
    return outputs.reshape(FRAMES, PLACES, D)

def reference(tokens, cotangent, frame_clip, frame_valid, place_valid, time_gain, time_shift, time_inward, time_inward_bias, time_outward, time_outward_bias, time_linear, time_linear_bias, space_gain, space_shift, space_inward, space_inward_bias, space_outward, space_outward_bias, feed_gain, feed_shift, feed_expand, feed_expand_bias, feed_reduce, feed_reduce_bias):
    parameters = (time_gain, time_shift, time_inward, time_inward_bias, time_outward, time_outward_bias, time_linear, time_linear_bias, space_gain, space_shift, space_inward, space_inward_bias, space_outward, space_outward_bias, feed_gain, feed_shift, feed_expand, feed_expand_bias, feed_reduce, feed_reduce_bias)
    key_places = jnp.take(place_valid, frame_clip, axis=0)

    def forward(inputs, weights):
        return layer(inputs, weights, frame_clip, frame_valid, key_places)
    final_sum, pullback = jax.vjp(forward, tokens.astype(jnp.float32), parameters)
    input_gradient, slopes = pullback(cotangent.astype(jnp.float32))
    return (final_sum.astype(jnp.bfloat16), input_gradient, slopes[0], slopes[1], slopes[2], slopes[3], slopes[4], slopes[5], slopes[6], slopes[7], slopes[8], slopes[9], slopes[10], slopes[11], slopes[12], slopes[13], slopes[14], slopes[15], slopes[16], slopes[17], slopes[18], slopes[19])
```

```python
import jax
import jax.numpy as jnp
from jax import lax
from jax.experimental import pallas as pl
from jax.experimental.pallas import tpu as pltpu
from jax.sharding import PartitionSpec as P

MESH = pl.DeviceIdType.MESH
BF = jnp.bfloat16
F32 = jnp.float32
NN = (((1,), (0,)), ((), ()))
NT = (((1,), (1,)), ((), ()))
TN = (((0,), (0,)), ((), ()))

TI, TO, TL, SI, SO, FE, FR = 0, 2304, 3072, 3840, 6144, 6912, 9984
WROWS = 13056
BASE = ([96 * t for t in range(3)] + [TO, TL] + [SI + 96 * t for t in range(3)] + [SO]
        + [FE + 768 * (v // 2) + 96 * (v % 2) for v in range(4)] + [FR + 768 * t for t in range(4)])
PAIR = [576] * 3 + [192] * 2 + [576] * 3 + [192] + [192] * 4 + [192] * 4
CORE = [288] * 3 + [96] * 2 + [288] * 3 + [96] + [1536] * 4 + [96] * 4
CHUNKS = 17
GATHER_ORDER = [0, 1, 2, 3, 4, 5, 6, 7, 8, 9, 10, 13, 15, 11, 12, 14, 16]
SLOTS = 5
EPSILON = 1e-06


def dot(a, b, dims):
    return lax.dot_general(a, b, dims, preferred_element_type=F32)


class Links:
    def __init__(self, send_sem, recv_sem):
        self.send_sem, self.recv_sem = send_sem, recv_sem
        self.copies, self.used, self.sent = {}, 0, set()
        self.z = lax.axis_index("grp")
        s = self.s = lax.axis_index("seq")
        core, x, y = s % 2, (s // 2) % 2, s // 4
        xn, yn = s + 2 - 4 * x, s + 4 - 8 * y
        self.core = core
        self.sib = s + 1 - 2 * core
        self.p = yn * (1 - core) + xn * core
        self.q = xn * (1 - core) + yn * core
        self.d = xn + yn - s

    def zpeer(self, k):
        return (self.z + k) % 4

    def speer(self, k):
        return (self.s + k) % 8

    def barrier(self):
        bar = pltpu.get_barrier_semaphore()
        for k in range(1, 8):
            pl.semaphore_signal(bar, inc=1, device_id=(self.z, self.speer(k)), device_id_type=MESH)
        for k in range(1, 4):
            pl.semaphore_signal(bar, inc=1, device_id=(self.zpeer(k), self.s), device_id_type=MESH)
        pl.semaphore_wait(bar, 10)

    def send(self, key, src, dst, device):
        i = self.used
        self.used += 1
        copy = pltpu.make_async_remote_copy(
            src_ref=src, dst_ref=dst, send_sem=self.send_sem.at[i], recv_sem=self.recv_sem.at[i],
            device_id=device, device_id_type=MESH)
        copy.start()
        self.copies[key] = copy

    def sends(self, key, src, dst, seq):
        self.send(key, src, dst, (self.z, seq))

    def sendz(self, key, src, dst, z):
        self.send(key, src, dst, (z, self.s))

    def got(self, *keys):
        for key in keys:
            self.copies[key].wait_recv()

    def gone(self, *keys):
        for key in keys:
            if key not in self.sent:
                self.sent.add(key)
                self.copies[key].wait_send()

    def drain(self):
        self.gone(*self.copies)


class Local:
    def __init__(self, sem):
        self.sem, self.used, self.copies = sem, 0, {}

    def start(self, key, src, dst):
        copy = pltpu.make_async_copy(src, dst, self.sem.at[self.used])
        self.used += 1
        copy.start()
        self.copies[key] = copy

    def wait(self, *keys):
        for key in keys:
            copy = self.copies.pop(key, None)
            if copy is not None:
                copy.wait()

    def drain(self):
        self.wait(*list(self.copies))


def place(c, s):
    return pl.ds(pl.multiple_of(BASE[c] + PAIR[c] * (s // 2) + CORE[c] * (s % 2), 32), 96)


def block(ref, c, s):
    return ref.at[place(c, s)]


class Gather:
    def __init__(self, links, shard, zst, w):
        self.l, self.shard, self.zst, self.w = links, shard, zst, w
        self.next, self.flight = 0, []

    def begin(self, ahead=3):
        self.ahead = ahead
        self.zst[self.l.z] = self.shard[...]
        for i in range(ahead):
            self.zsend(i)

    def zsend(self, i):
        if i < CHUNKS:
            c = GATHER_ORDER[i]
            for k in range(1, 4):
                self.l.sendz(("z", c, k), self.shard.at[c], self.zst.at[self.l.z, c], self.l.zpeer(k))

    def step_a(self, i, c):
        l = self.l
        l.got(*[("z", c, k) for k in range(1, 4)])
        rows = place(c, l.s)
        zst, w = self.zst, self.w
        for half in range(2):
            lo, hi = zst[2 * half, c], zst[2 * half + 1, c]
            w[rows, 384 * half:384 * half + 128] = lo[:96]
            w[rows, 384 * half + 256:384 * half + 384] = hi[:96]
            blo, bhi = lo[96:], hi[96:]
            w[rows, 384 * half + 128:384 * half + 256] = jnp.concatenate([
                jnp.concatenate([blo[:, :64], bhi[:, :64]], axis=1),
                jnp.concatenate([blo[:, 64:], bhi[:, 64:]], axis=1)], axis=0)
        own = block(w, c, l.s)
        l.sends(("p", c), own, own, l.p)
        l.sends(("q", c), own, own, l.q)
        l.sends(("so", c), own, own, l.sib)
        self.zsend(i + self.ahead)

    def step_b(self, i, c):
        l = self.l
        l.got(("p", c))
        bp = block(self.w, c, l.p)
        l.sends(("d", c), bp, bp, l.q)
        l.sends(("sp", c), bp, bp, l.sib)
        l.got(("q", c))
        bq = block(self.w, c, l.q)
        l.sends(("sq", c), bq, bq, l.sib)

    def step_c(self, i, c):
        l = self.l
        l.got(("d", c))
        bd = block(self.w, c, l.d)
        l.sends(("sd", c), bd, bd, l.sib)

    def step_d(self, i, c):
        self.l.got(("so", c), ("sp", c), ("sq", c), ("sd", c))

    def tick(self):
        steps = (self.step_b, self.step_c, self.step_d)
        fresh = []
        if self.next < CHUNKS:
            self.step_a(self.next, GATHER_ORDER[self.next])
            fresh = [(self.next, 0)]
            self.next += 1
        later = []
        for i, k in self.flight[::-1]:
            steps[k](i, GATHER_ORDER[i])
            if k < 2:
                later.append((i, k + 1))
        self.flight = later[::-1] + fresh

    def until(self, chunk):
        i = GATHER_ORDER.index(chunk)
        while i >= self.next or any(j <= i for j, _ in self.flight):
            self.tick()

    def finish(self):
        while self.next < CHUNKS or self.flight:
            self.tick()


class Scatter:
    def __init__(self, links, local, g, sr, fr, ar, br, zp, zr, ob, out):
        self.l, self.local, self.g, self.sr, self.fr, self.ar, self.br = links, local, g, sr, fr, ar, br
        self.zp, self.zr, self.ob, self.out = zp, zr, ob, out
        self.ready, self.flight, self.order = [], [], []

    def step_a(self, i, c):
        l = self.l
        for j in range(4):
            l.sends(("s", c, j), block(self.g, c, 2 * j + 1 - l.core), self.sr.at[i % SLOTS, j], l.sib)

    def add(self, c, s, other):
        rows = place(c, s)
        self.g[rows, :] = (self.g[rows, :].astype(F32) + other.astype(F32)).astype(BF)

    def step_b(self, i, c):
        l, k = self.l, i % SLOTS
        l.got(*[("s", c, j) for j in range(4)])
        for s, j in ((l.d, l.d // 2), (l.p, l.p // 2), (l.q, l.q // 2), (l.s, l.s // 2)):
            self.add(c, s, self.sr[k, j])
            if s is l.d:
                l.sends(("f", c), block(self.g, c, l.d), self.fr.at[k], l.p)
            if s is l.p:
                l.sends(("a", c), block(self.g, c, l.p), self.ar.at[k], l.p)

    def step_c(self, i, c):
        l, k = self.l, i % SLOTS
        l.got(("f", c))
        self.add(c, l.q, self.fr[k])
        l.sends(("b", c), block(self.g, c, l.q), self.br.at[k], l.q)

    def step_d(self, i, c):
        l, k = self.l, i % SLOTS
        l.got(("a", c), ("b", c))
        rows = place(c, l.s)
        total = self.g[rows, :].astype(F32) + self.ar[k].astype(F32) + self.br[k].astype(F32)
        if i >= SLOTS:
            l.gone(*[("z", self.order[i - SLOTS], k) for k in range(1, 4)])
        zp = self.zp
        for half in range(2):
            lane = 384 * half
            zp[k, 2 * half, 0:96] = total[:, lane:lane + 128].astype(BF)
            zp[k, 2 * half + 1, 0:96] = total[:, lane + 256:lane + 384].astype(BF)
            mid = total[:, lane + 128:lane + 256]
            top, low = mid[:48], mid[48:]
            zp[k, 2 * half, 96:144] = jnp.concatenate([top[:, :64], low[:, :64]], axis=1).astype(BF)
            zp[k, 2 * half + 1, 96:144] = jnp.concatenate([top[:, 64:], low[:, 64:]], axis=1).astype(BF)
        for j in range(1, 4):
            z = l.zpeer(j)
            l.sendz(("z", c, j), zp.at[k, z], self.zr.at[k, j - 1], z)

    def step_e(self, i, c):
        l, k = self.l, i % SLOTS
        l.got(*[("z", c, j) for j in range(1, 4)])
        total = self.zp[k, l.z].astype(F32)
        for j in range(3):
            total += self.zr[k, j].astype(F32)
        if i >= SLOTS:
            self.local.wait(("o", self.order[i - SLOTS]))
        self.ob[k] = total
        self.local.start(("o", c), self.ob.at[k], self.out.at[c])

    def pump(self):
        steps = (self.step_b, self.step_c, self.step_d, self.step_e)
        fresh = []
        if self.ready:
            c = self.ready.pop(0)
            i = len(self.order)
            self.order.append(c)
            self.step_a(i, c)
            fresh = [(i, 0)]
        later = []
        for i, k in self.flight[::-1]:
            steps[k](i, self.order[i])
            if k < 3:
                later.append((i, k + 1))
        self.flight = later[::-1] + fresh

    def finish(self):
        while self.ready or self.flight:
            self.pump()


class VectorSum:
    def __init__(self, links, gv, vb):
        self.l, self.gv, self.vb = links, gv, vb

    def swap(self, i):
        l = self.l
        l.sends(("vs", i), self.gv.at[i], self.vb.at[i], (l.sib, l.p, l.q)[i])

    def join(self, i):
        self.l.got(("vs", i))
        self.gv[i + 1] = self.gv[i] + self.vb[i]

    def swapz(self):
        l = self.l
        self.vb[3 + l.z] = self.gv[3]
        for k in range(1, 4):
            l.sendz(("vz", k), self.gv.at[3], self.vb.at[3 + l.z], l.zpeer(k))

    def total(self):
        self.l.got(*[("vz", k) for k in range(1, 4)])
        return (self.vb[3] + self.vb[4]) + (self.vb[5] + self.vb[6])


TG, TS, TOB, TLB, SG, SS, SOB, FG, FS, FRB, TIB, SIB, FEB = 0, 1, 2, 3, 4, 5, 6, 7, 8, 9, 10, 12, 14


def assemble_vectors(vg, vec):
    vec[...] = jnp.zeros(vec.shape, F32)
    for s in range(8):
        piece = vg[s]
        vec[0:10, 96 * s:96 * s + 96] = piece[0:10, 0:96]
        for a in range(2):
            i = 2 * s + a
            for r in (TIB, SIB):
                vec[r + i // 8:r + i // 8 + 1, 96 * (i % 8):96 * (i % 8) + 96] = piece[r + a:r + a + 1, 0:96]
        for a in range(4):
            t, lane = 2 * (s % 2) + a // 2, 192 * (s // 2) + 96 * (a % 2)
            vec[FEB + t:FEB + 1 + t, lane:lane + 96] = piece[FEB + a:FEB + 1 + a, 0:96]


def split_vectors(vec, out, me):
    for s in range(8):
        @pl.when(me == s)
        def _():
            out[...] = jnp.zeros(out.shape, F32)
            out[0:10, 0:96] = vec[0:10, 96 * s:96 * s + 96]
            for a in range(2):
                i = 2 * s + a
                for r in (TIB, SIB):
                    out[r + a:r + a + 1, 0:96] = vec[r + i // 8:r + i // 8 + 1, 96 * (i % 8):96 * (i % 8) + 96]
            for a in range(4):
                t, lane = 2 * (s % 2) + a // 2, 192 * (s // 2) + 96 * (a % 2)
                out[FEB + a:FEB + 1 + a, 0:96] = vec[FEB + t:FEB + 1 + t, lane:lane + 96]


def standardize(x):
    centered = x - jnp.mean(x, axis=-1, keepdims=True)
    scale = lax.rsqrt(jnp.mean(centered * centered, axis=-1, keepdims=True) + EPSILON)
    return centered * scale, scale


def norm_back(e, gain, n, scale):
    u = e * gain
    return scale * (u - jnp.mean(u, axis=-1, keepdims=True) - n * jnp.mean(u * n, axis=-1, keepdims=True))


def column_sums(x):
    return jnp.sum(x, axis=0, keepdims=True)


def head_masks(scale):
    lane = lax.broadcasted_iota(jnp.int32, (1, 128), 1)
    return [jnp.where(lane < 64, scale, 0.0).astype(BF), jnp.where(lane < 64, 0.0, scale).astype(BF)]


def pair_columns(qkv, rows, p):
    c = pl.multiple_of(p * 128, 128)
    return [qkv[rows, pl.ds(768 * j + c, 128)] for j in range(3)]


def attend_block(b, qkv, mixed, lse, bias):
    rows = pl.ds(b * 256, 256)

    def pair(p):
        q, k, v = pair_columns(qkv, rows, p)
        scaled, plain = head_masks(0.125), head_masks(1.0)
        out = None
        for h in range(2):
            s = dot(k * scaled[h], q, NT) + bias()
            m = jnp.max(s, axis=0, keepdims=True)
            e = jnp.exp(s - m)
            total = jnp.sum(e, axis=0, keepdims=True)
            lse[pl.ds(b * 12 + p * 2 + h, 1), :] = m + jnp.log(total)
            o = dot((e * (1.0 / total)).astype(BF), v * plain[h], TN)
            out = o if out is None else out + o
        mixed[rows, pl.ds(pl.multiple_of(p * 128, 128), 128)] = out.astype(BF)

    def body(i, _):
        pair(2 * i)
        pair(2 * i + 1)
        return 0

    lax.fori_loop(0, 3, body, 0)


def attend_block_back(b, qkv, gm, lse, bias):
    rows = pl.ds(b * 256, 256)

    def pair(p):
        q, k, v = pair_columns(qkv, rows, p)
        c = pl.multiple_of(p * 128, 128)
        g = gm[rows, pl.ds(c, 128)]
        scaled, plain = head_masks(0.125), head_masks(1.0)
        sums = [None, None, None]
        for h in range(2):
            kh, vh, qh, gh = k * scaled[h], v * plain[h], q * scaled[h], g * plain[h]
            s = dot(kh, q, NT) + bias()
            chances = jnp.exp(s - lse[pl.ds(b * 12 + p * 2 + h, 1), :])
            back = dot(vh, g, NT)
            mean = jnp.sum(chances * back, axis=0, keepdims=True)
            gs = (chances * (back - mean)).astype(BF)
            for j, term in enumerate((dot(gs, kh, TN), dot(gs, qh, NN), dot(chances.astype(BF), gh, NN))):
                sums[j] = term if sums[j] is None else sums[j] + term
        for j in range(3):
            qkv[rows, pl.ds(768 * j + c, 128)] = sums[j].astype(BF)

    def body(i, _):
        pair(2 * i)
        pair(2 * i + 1)
        return 0

    lax.fori_loop(0, 3, body, 0)


def project_in(normed, w, at, qkv, rows, vec, bias_row):
    for j in range(3):
        part = dot(normed, w[at + 768 * j:at + 768 * (j + 1), :], NT)
        if j != 1:
            r = bias_row + j // 2
            part = part + vec[r:r + 1, :]
        qkv[rows, 768 * j:768 * (j + 1)] = part.astype(BF)


def flat(x):
    return x.astype(F32).reshape(256, 768)


def tiled(x):
    return x.reshape(32, 8, 768).astype(BF)


def forward_kernel(shard, vshard, tokens, tmask, smask,
                   w_o, vec, second_o, first_o, sqkv_o, smixed_o, slse, ret_o, tmixed_o, tqkv_o, tlse, xp_o,
                   w, zst, vg, x, xp, nb, tqkv, tmixed, pr, ret, ret2, first, sqkv, smixed, second,
                   local_sem, send_sem, recv_sem):
    l = Links(send_sem, recv_sem)
    here = Local(local_sem)
    here.start("x", tokens, x)
    mine = pl.ds(4 * l.s, 4)
    here.start("xp", tokens.at[:, mine], xp.at[mine])
    l.barrier()
    g = Gather(l, shard, zst, w)
    g.begin()
    vg[l.s] = vshard[...]
    for k in range(1, 8):
        peer = l.speer(k)
        l.sends(("v", k), vshard, vg.at[l.s], peer)
        l.sends(("t", k), tokens.at[:, pl.ds(4 * peer, 4)], xp.at[mine], peer)
    g.tick()
    g.tick()
    l.got(*[("v", k) for k in range(1, 8)])
    assemble_vectors(vg, vec)
    g.tick()
    l.got(*[("t", k) for k in range(1, 8)])
    here.wait("x", "xp")
    here.start("xp_o", xp, xp_o)
    for b in range(4):
        rows = pl.ds(b * 256, 256)
        n, _ = standardize(flat(xp[:, b]))
        nb[rows, :] = (n * vec[TG:TG + 1, :] + vec[TS:TS + 1, :]).astype(BF)
        if b % 2:
            g.tick()
    g.until(2)
    for b in range(4):
        project_in(nb[256 * b:256 * b + 256, :], w, TI, tqkv, pl.ds(b * 256, 256), vec, TIB)
        if b % 2:
            g.tick()
    here.start("tqkv_o", tqkv, tqkv_o)
    g.until(3)
    for b in range(4):
        attend_block(b, tqkv, tmixed, tlse, lambda: tmask[...])
        o = dot(tmixed[256 * b:256 * b + 256, :], w[TO:TO + 768, :], NT) + vec[TOB:TOB + 1, :]
        pr[:, b] = tiled(o)
        ret[:, 4 * l.s + b] = pr[mine, b]
        for k in range(1, 8):
            peer = l.speer(k)
            l.sends(("r", b, k), pr.at[pl.ds(4 * peer, 4), b], ret.at[:, 4 * l.s + b], peer)
        g.tick()
    here.start("tmixed_o", tmixed, tmixed_o)
    g.until(4)
    for b in range(4):
        l.got(*[("r", b, k) for k in range(1, 8)])
    for f in range(4):
        rows = pl.ds(256 * f, 256)
        back = flat(ret[f]).astype(BF)
        ret2[rows, :] = back
        total = flat(x[f]) + dot(back, w[TL:TL + 768, :], NT) + vec[TLB:TLB + 1, :]
        first[rows, :] = total
        n, _ = standardize(total)
        nb[rows, :] = (n * vec[SG:SG + 1, :] + vec[SS:SS + 1, :]).astype(BF)
        if f == 1:
            g.tick()
    here.start("ret_o", ret2, ret_o)
    here.start("first_o", first, first_o)
    g.until(7)
    for f in range(4):
        rows = pl.ds(256 * f, 256)
        project_in(nb[256 * f:256 * f + 256, :], w, SI, sqkv, rows, vec, SIB)
        attend_block(f, sqkv, smixed, slse, lambda: smask[f])
        g.tick()
    here.start("sqkv_o", sqkv, sqkv_o)
    here.start("smixed_o", smixed, smixed_o)
    g.until(8)
    for f in range(4):
        rows = pl.ds(256 * f, 256)
        second[rows, :] = first[rows, :] + dot(smixed[rows, :], w[SO:SO + 768, :], NT) + vec[SOB:SOB + 1, :]
    here.start("second_o", second, second_o)
    here.start("w0", w.at[0:FE], w_o.at[0:FE])
    g.finish()
    here.start("w1", w.at[FE:WROWS], w_o.at[FE:WROWS])
    l.drain()
    here.drain()


VM = pl.BlockSpec(memory_space=pltpu.VMEM)
ANY = pl.BlockSpec(memory_space=pl.ANY)
LIMIT = 63 << 20


def forward(shard, vshard, tokens, tmask, smask):
    shaped = jax.ShapeDtypeStruct
    flat_bf, flat_f32, wide = shaped((1024, 768), BF), shaped((1024, 768), F32), shaped((1024, 2304), BF)
    tokens_shape = (4, 32, 8, 768)
    n = CHUNKS * 10 + 14 + 28
    return pl.pallas_call(
        forward_kernel,
        out_shape=(shaped((WROWS, 768), BF), shaped((24, 768), F32), flat_f32, flat_f32, wide, flat_bf,
                   shaped((48, 256), F32), flat_bf, flat_bf, wide, shaped((48, 256), F32), shaped((32, 4, 8, 768), BF)),
        in_specs=[VM, VM, ANY, VM, VM],
        out_specs=(ANY, VM, ANY, ANY, ANY, ANY, VM, ANY, ANY, ANY, VM, ANY),
        scratch_shapes=[
            pltpu.VMEM((WROWS, 768), BF), pltpu.VMEM((4, CHUNKS, 144, 128), BF), pltpu.VMEM((8, 24, 128), F32),
            pltpu.VMEM(tokens_shape, BF), pltpu.VMEM((32, 4, 8, 768), BF), pltpu.VMEM((1024, 768), BF),
            pltpu.VMEM((1024, 2304), BF), pltpu.VMEM((1024, 768), BF), pltpu.VMEM((32, 4, 8, 768), BF),
            pltpu.VMEM(tokens_shape, BF), pltpu.VMEM((1024, 768), BF), pltpu.VMEM((1024, 768), F32),
            pltpu.VMEM((1024, 2304), BF), pltpu.VMEM((1024, 768), BF), pltpu.VMEM((1024, 768), F32),
            pltpu.SemaphoreType.DMA((16,)), pltpu.SemaphoreType.DMA((n,)), pltpu.SemaphoreType.DMA((n,))],
        compiler_params=pltpu.CompilerParams(collective_id=0, has_side_effects=True, vmem_limit_bytes=LIMIT),
    )(shard, vshard, tokens, tmask, smask)


def backward_kernel(w_i, vec, cot_i, second_i, first_i, sqkv_i, smixed_i, slse, ret_i, tmixed_i, tqkv_i, tlse, xp_i,
                    tmask, smask,
                    result_o, grad_o, packed_o, vout,
                    w, g, second, final, dfn, nb, act, gh, qkv, mixed, ret, xp, gp, gpp, gb, it,
                    sr, fr, ar, br, zp, zr, ob, gv, vb, vsum, local_sem, send_sem, recv_sem):
    l = Links(send_sem, recv_sem)
    here = Local(local_sem)
    here.start("second", second_i, second)
    for t in (0, 2, 1, 3):
        here.start(("fe", t), w_i.at[FE + 768 * t:FE + 768 * (t + 1)], w.at[FE + 768 * t:FE + 768 * (t + 1)])
        here.start(("fr", t), w_i.at[FR + 768 * t:FR + 768 * (t + 1)], w.at[FR + 768 * t:FR + 768 * (t + 1)])
        if t == 0:
            here.start("cot", cot_i, g)
    here.start("w", w_i.at[0:FE], w.at[0:FE])
    here.start("qkv", sqkv_i, qkv)
    here.start("mixed", smixed_i, mixed)
    here.start("ret", ret_i, ret)
    here.start("xp", xp_i, xp)
    l.barrier()
    sc = Scatter(l, here, w, sr, fr, ar, br, zp, zr, ob, packed_o)
    vs = VectorSum(l, gv, vb)
    sums = gv.at[0]
    sums[...] = jnp.zeros((24, 768), F32)

    def note(r, value):
        sums[r:r + 1, :] += value

    here.wait("second")
    for f in range(4):
        rows = pl.ds(256 * f, 256)
        value = second[rows, :]
        n, _ = standardize(value)
        nb[rows, :] = (n * vec[FG:FG + 1, :] + vec[FS:FS + 1, :]).astype(BF)
        final[rows, :] = value + vec[FRB:FRB + 1, :]
        dfn[rows, :] = jnp.zeros((256, 768), F32)
    for i, t in enumerate((0, 2, 1, 3)):
        here.wait(("fe", t), ("fr", t), "cot")
        we, wf = w.at[FE + 768 * t:FE + 768 * (t + 1)], w.at[FR + 768 * t:FR + 768 * (t + 1)]

        def unit(b, _):
            rows = pl.ds(pl.multiple_of(256 * b, 256), 256)
            u = dot(nb[rows, :], we[...], NT) + vec[FEB + t:FEB + t + 1, :]
            phi = 0.5 + 0.5 * lax.erf(u * 0.7071067811865476)
            a = (u * phi).astype(BF)
            act[rows, :] = a
            slope = phi + u * (0.3989422804014327 * jnp.exp(-0.5 * u * u))
            h = (dot(g[rows, :], wf[...], NN) * slope).astype(BF)
            gh[rows, :] = h
            final[rows, :] += dot(a, wf[...], NT)
            dfn[rows, :] += dot(h, we[...], NN)
            sums[FEB + t:FEB + t + 1, :] += column_sums(h.astype(F32))
            return 0

        lax.fori_loop(0, 2, unit, 0)
        sc.pump()
        lax.fori_loop(2, 4, unit, 0)
        sc.pump()
        wf[...] = dot(g[...], act[...], TN).astype(BF)
        sc.ready.append(13 + t)
        sc.pump()
        we[...] = dot(gh[...], nb[...], TN).astype(BF)
        if i % 2:
            sc.ready += [9, 10] if i == 1 else [11, 12]
        sc.pump()

    here.wait("w")
    for f in range(4):
        rows = pl.ds(256 * f, 256)
        nb[rows, :] = final[rows, :].astype(BF)
        n, scale = standardize(second[rows, :])
        e = dfn[rows, :]
        cot = g[rows, :].astype(F32)
        note(FRB, column_sums(cot))
        note(FG, column_sums(e * n))
        note(FS, column_sums(e))
        total = cot + norm_back(e, vec[FG:FG + 1, :], n, scale)
        final[rows, :] = total
        low = total.astype(BF)
        act[rows, :] = low
        note(SOB, column_sums(low.astype(F32)))
        gh[rows, :] = dot(low, w[SO:SO + 768, :], NN).astype(BF)
        if f % 2:
            sc.pump()
    here.start("result", nb, result_o)
    here.start("first", first_i, second)
    here.wait("mixed")
    w[SO:SO + 768, :] = dot(act[...], mixed[...], TN).astype(BF)
    here.start("mixed2", tmixed_i, mixed)
    sc.ready.append(8)
    sc.pump()
    here.wait("qkv")
    for f in range(4):
        attend_block_back(f, qkv, gh, slse, lambda: smask[f])
        sc.pump()
    here.wait("result", "first")
    for f in range(4):
        rows = pl.ds(256 * f, 256)
        n, scale = standardize(second[rows, :])
        nb[rows, :] = (n * vec[SG:SG + 1, :] + vec[SS:SS + 1, :]).astype(BF)
        joined = qkv[rows, :]
        note(SIB, column_sums(joined[:, :768].astype(F32)))
        note(SIB + 1, column_sums(joined[:, 1536:].astype(F32)))
        e = dot(joined, w[SI:SI + 2304, :], NN)
        note(SG, column_sums(e * n))
        note(SS, column_sums(e))
        total = final[rows, :] + norm_back(e, vec[SG:SG + 1, :], n, scale)
        final[rows, :] = total
        low = total.astype(BF)
        act[rows, :] = low
        note(TLB, column_sums(low.astype(F32)))
        gp[f] = tiled(dot(low, w[TL:TL + 768, :], NN))
        gpp[4 * l.s + f] = gp[f, pl.ds(4 * l.s, 4)]
        for k in range(1, 8):
            peer = l.speer(k)
            l.sends(("g", f, k), gp.at[f, pl.ds(4 * peer, 4)], gpp.at[4 * l.s + f], peer)
        if f % 2:
            sc.pump()
    for j in range(3):
        w[SI + 768 * j:SI + 768 * (j + 1), :] = dot(qkv[:, 768 * j:768 * (j + 1)], nb[...], TN).astype(BF)
    here.start("qkv2", tqkv_i, qkv)
    sc.ready += [5, 6, 7]
    sc.pump()
    here.wait("ret")
    w[TL:TL + 768, :] = dot(act[...], ret[...], TN).astype(BF)
    sc.ready.append(4)
    sc.pump()

    for f in range(4):
        l.got(*[("g", f, k) for k in range(1, 8)])
    for b in range(4):
        rows = pl.ds(256 * b, 256)
        low = flat(gpp[:, b])
        note(TOB, column_sums(low))
        low = low.astype(BF)
        act[rows, :] = low
        gh[rows, :] = dot(low, w[TO:TO + 768, :], NN).astype(BF)
    sc.pump()
    here.wait("mixed2")
    w[TO:TO + 768, :] = dot(act[...], mixed[...], TN).astype(BF)
    sc.ready.append(3)
    sc.pump()
    here.wait("qkv2", "xp")
    for b in range(4):
        rows = pl.ds(256 * b, 256)
        attend_block_back(b, qkv, gh, tlse, lambda: tmask[...])
        n, scale = standardize(flat(xp[:, b]))
        nb[rows, :] = (n * vec[TG:TG + 1, :] + vec[TS:TS + 1, :]).astype(BF)
        joined = qkv[rows, :]
        note(TIB, column_sums(joined[:, :768].astype(F32)))
        note(TIB + 1, column_sums(joined[:, 1536:].astype(F32)))
        e = dot(joined, w[TI:TI + 2304, :], NN)
        note(TG, column_sums(e * n))
        note(TS, column_sums(e))
        gb[:, b] = tiled(norm_back(e, vec[TG:TG + 1, :], n, scale))
        it[:, 4 * l.s + b] = gb[pl.ds(4 * l.s, 4), b]
        for k in range(1, 8):
            peer = l.speer(k)
            l.sends(("h", b, k), gb.at[pl.ds(4 * peer, 4), b], it.at[:, 4 * l.s + b], peer)
        sc.pump()
    for j in range(3):
        w[TI + 768 * j:TI + 768 * (j + 1), :] = dot(qkv[:, 768 * j:768 * (j + 1)], nb[...], TN).astype(BF)
    sc.ready += [0, 1, 2]
    for i in range(3):
        vs.swap(i)
        sc.pump()
        vs.join(i)
    vs.swapz()
    for b in range(4):
        l.got(*[("h", b, k) for k in range(1, 8)])
    for f in range(4):
        rows = pl.ds(256 * f, 256)
        final[rows, :] += flat(it[f])
    here.start("grad", final, grad_o)
    sc.pump()
    vsum[...] = vs.total()
    split_vectors(vsum, vout, l.s)
    sc.finish()
    l.drain()
    here.drain()


def backward(saved, cot, tmask, smask):
    w_i, vec, second, first, sqkv, smixed, slse, ret, tmixed, tqkv, tlse, xp = saved
    shaped = jax.ShapeDtypeStruct
    n = CHUNKS * 10 + 56 + 6
    vmem = pltpu.VMEM
    rows_bf, rows_f32 = vmem((1024, 768), BF), vmem((1024, 768), F32)
    by_frame, by_place = vmem((4, 32, 8, 768), BF), vmem((32, 4, 8, 768), BF)
    row_block = vmem((SLOTS, 96, 768), BF)
    return pl.pallas_call(
        backward_kernel,
        out_shape=(shaped((1024, 768), BF), shaped((1024, 768), F32), shaped((CHUNKS, 144, 128), F32), shaped((24, 128), F32)),
        in_specs=[ANY, VM, ANY, ANY, ANY, ANY, ANY, VM, ANY, ANY, ANY, VM, ANY, VM, VM],
        out_specs=(ANY, ANY, ANY, VM),
        scratch_shapes=[
            vmem((WROWS, 768), BF), rows_bf, rows_f32, rows_f32, rows_f32, rows_bf, rows_bf, rows_bf,
            vmem((1024, 2304), BF), rows_bf, rows_bf, by_place, by_frame, by_place, by_place, by_frame,
            vmem((SLOTS, 4, 96, 768), BF), row_block, row_block, row_block, vmem((SLOTS, 4, 144, 128), BF),
            vmem((SLOTS, 3, 144, 128), BF), vmem((SLOTS, 144, 128), F32), vmem((4, 24, 768), F32), vmem((7, 24, 768), F32),
            vmem((24, 768), F32), pltpu.SemaphoreType.DMA((48,)), pltpu.SemaphoreType.DMA((n,)), pltpu.SemaphoreType.DMA((n,))],
        compiler_params=pltpu.CompilerParams(collective_id=1, has_side_effects=True, vmem_limit_bytes=LIMIT),
    )(w_i, vec, cot, second, first, sqkv, smixed, slse, ret, tmixed, tqkv, tlse, xp, tmask, smask)


def pack_shards(ti, to, tl, si, so, fe, fr):
    odd = lax.axis_index("grp") % 2 == 1
    first = jnp.concatenate([ti, to, tl, si, so, fe], axis=1).astype(BF).T.reshape(13, 96, 192)
    last = fr.astype(BF).T.reshape(96, 4, 192).transpose(1, 0, 2)
    both = jnp.concatenate([first, last], axis=0)
    a = jnp.where(odd, both[..., 64:], both[..., :128])
    b = jnp.where(odd, both[..., :64], both[..., 128:])
    bp = jnp.concatenate([b[:, :48], b[:, 48:]], axis=-1)
    return jnp.concatenate([a, bp], axis=1)


def unpack_grads(packed):
    odd = lax.axis_index("grp") % 2 == 1
    a, bp = packed[:, :96], packed[:, 96:]
    b = jnp.concatenate([bp[..., :64], bp[..., 64:]], axis=1)
    both = jnp.where(odd, jnp.concatenate([b, a], axis=-1), jnp.concatenate([a, b], axis=-1))
    first = both[:13].reshape(1248, 192).T
    last = both[13:].transpose(1, 0, 2).reshape(96, 768).T
    return (first[:, :288], first[:, 288:384], first[:, 384:480], first[:, 480:768], first[:, 768:864], first[:, 864:1248], last)


def on_device_fast(
    tokens, cotangent, frame_clip, frame_valid, place_valid,
    time_gain, time_shift, time_inward, time_inward_bias, time_outward, time_outward_bias, time_linear, time_linear_bias,
    space_gain, space_shift, space_inward, space_inward_bias, space_outward, space_outward_bias,
    feed_gain, feed_shift, feed_expand, feed_expand_bias, feed_reduce, feed_reduce_bias,
):
    shard = pack_shards(time_inward, time_outward, time_linear, space_inward, space_outward, feed_expand, feed_reduce)
    vectors = jnp.concatenate([
        time_gain, time_shift, time_outward_bias, time_linear_bias, space_gain, space_shift, space_outward_bias, feed_gain,
        feed_shift, feed_reduce_bias, time_inward_bias, space_inward_bias, feed_expand_bias])
    vshard = jnp.pad(vectors.astype(BF).astype(F32).reshape(18, 96), ((0, 6), (0, 32)))
    clip_count = place_valid.shape[0]
    own_clips = lax.dynamic_slice_in_dim(frame_clip, lax.axis_index("seq") * 4, 4) % clip_count
    matches = own_clips[:, None] == jnp.arange(clip_count, dtype=jnp.int32)[None, :]
    key_places = jnp.sum(jnp.where(matches[:, :, None], place_valid[None, :, :], 0), axis=1)
    smask = jnp.where(key_places == 1, 0.0, -1e30).astype(F32)[:, :, None]
    frame, spot = jnp.arange(256) // 8, jnp.arange(256) % 8
    clip_of, valid_of = jnp.repeat(frame_clip, 8), jnp.repeat(frame_valid, 8)
    allowed = (clip_of[:, None] == clip_of[None, :]) & (spot[:, None] == spot[None, :]) & (valid_of[:, None] == 1)
    tmask = jnp.where(allowed, 0.0, -1e30).astype(F32)
    saved = forward(shard, vshard, tokens.reshape(4, 32, 8, 768), tmask, smask)
    result, grad, packed, v = backward(saved, cotangent.reshape(1024, 768), tmask, smask)
    gti, gto, gtl, gsi, gso, gfe, gfr = unpack_grads(packed)
    v = v[:, :96]
    return (result.reshape(tokens.shape), grad.reshape(tokens.shape), v[TG], v[TS], gti, v[TIB:TIB + 2].reshape(-1), gto, v[TOB],
            gtl, v[TLB], v[SG], v[SS], gsi, v[SIB:SIB + 2].reshape(-1), gso, v[SOB], v[FG], v[FS], gfe, v[FEB:FEB + 4].reshape(-1),
            gfr, v[FRB])


HEADS = 12


def normalize(inputs, scaling, offset):
    average = jnp.mean(inputs, axis=-1, keepdims=True)
    centered = inputs - average
    variance = jnp.mean(centered * centered, axis=-1, keepdims=True)
    return centered * lax.rsqrt(variance + EPSILON) * scaling + offset


def gelu_exact(inputs):
    return jax.nn.gelu(inputs, approximate=False)


def matmul(former, latter):
    return jnp.dot(former, latter, preferred_element_type=jnp.float32)


def inner(former, latter):
    return lax.dot_general(
        former, latter, (((0,), (0,)), ((), ())), preferred_element_type=jnp.float32
    )


def against(former, latter):
    return lax.dot_general(
        former, latter, (((1,), (1,)), ((), ())), preferred_element_type=jnp.float32
    )


def column_sum(delta_rows):
    return jnp.sum(delta_rows, axis=0, dtype=jnp.float32)


def packed_sum(joined_grad):
    totals = jnp.sum(joined_grad, axis=0, dtype=jnp.float32)
    model_width = totals.shape[0] // 3
    return jnp.concatenate([totals[:model_width], totals[2 * model_width :]])


def patterns(flavor):
    if flavor == "time":
        return ("fphd,gphd->phfg", "phfg,gphd->fphd", "phfg,fphd->gphd")
    return ("fphd,fqhd->fhpq", "fhpq,fqhd->fphd", "fhpq,fphd->fqhd")


def project_in_general(normed_low, weight, packed_bias, leading, head_count):
    model_width = normed_low.shape[-1]
    full_bias = jnp.concatenate(
        [
            packed_bias[:model_width],
            jnp.zeros((model_width,), jnp.float32),
            packed_bias[model_width:],
        ]
    )
    joined = (matmul(normed_low, weight) + full_bias).astype(jnp.bfloat16)
    shaped = joined.reshape(leading + (3, head_count, model_width // head_count))
    return (shaped[:, :, 0], shaped[:, :, 1], shaped[:, :, 2])


def attend(queries, keys_in, values, allowed, flavor):
    score_form, mix_form, spare_form = patterns(flavor)
    factor = queries.shape[-1] ** (-0.5)
    scores = jnp.einsum(score_form, queries, keys_in, preferred_element_type=jnp.float32) * factor
    masked = jnp.where(allowed, scores, -1e30)
    highest = jnp.max(masked, axis=-1, keepdims=True)
    raised = jnp.exp(masked - highest)
    summed = jnp.sum(raised, axis=-1, keepdims=True)
    chances = (raised / summed).astype(jnp.bfloat16)
    mixed = jnp.einsum(mix_form, chances, values, preferred_element_type=jnp.float32)
    return (mixed, highest + jnp.log(summed))


def attend_back(queries, keys_in, values, log_total, allowed, upstream, flavor):
    score_form, mix_form, spare_form = patterns(flavor)
    factor = queries.shape[-1] ** (-0.5)
    scores = jnp.einsum(score_form, queries, keys_in, preferred_element_type=jnp.float32) * factor
    chances = jnp.exp(jnp.where(allowed, scores, -1e30) - log_total)
    value_grad = jnp.einsum(
        spare_form, chances.astype(jnp.bfloat16), upstream, preferred_element_type=jnp.float32
    )
    chance_grad = jnp.einsum(score_form, upstream, values, preferred_element_type=jnp.float32)
    score_grad = (
        chances * (chance_grad - jnp.sum(chance_grad * chances, axis=-1, keepdims=True))
    ).astype(jnp.bfloat16)
    query_grad = (
        jnp.einsum(mix_form, score_grad, keys_in, preferred_element_type=jnp.float32) * factor
    )
    key_grad = (
        jnp.einsum(spare_form, score_grad, queries, preferred_element_type=jnp.float32) * factor
    )
    joined = jnp.stack([query_grad, key_grad, value_grad], axis=2)
    return joined.reshape(-1, 3 * joined.shape[-1] * joined.shape[-2]).astype(jnp.bfloat16)


def on_device_general(
    tokens,
    cotangent,
    frame_clip,
    frame_valid,
    place_valid,
    time_gain,
    time_shift,
    time_inward,
    time_inward_bias,
    time_outward,
    time_outward_bias,
    time_linear,
    time_linear_bias,
    space_gain,
    space_shift,
    space_inward,
    space_inward_bias,
    space_outward,
    space_outward_bias,
    feed_gain,
    feed_shift,
    feed_expand,
    feed_expand_bias,
    feed_reduce,
    feed_reduce_bias,
):
    frames_dev, places, model_width = tokens.shape
    head_count = HEADS
    group_frames = frame_clip.shape[0]
    clip_count = place_valid.shape[0]
    place_dev = places // lax.axis_size("seq")
    rows_part = (
        lax.all_gather(time_inward.astype(jnp.bfloat16), "grp", axis=0, tiled=True),
        lax.all_gather(time_outward.astype(jnp.bfloat16), "grp", axis=0, tiled=True),
        lax.all_gather(time_linear.astype(jnp.bfloat16), "grp", axis=0, tiled=True),
        lax.all_gather(space_inward.astype(jnp.bfloat16), "grp", axis=0, tiled=True),
        lax.all_gather(space_outward.astype(jnp.bfloat16), "grp", axis=0, tiled=True),
        lax.all_gather(feed_expand.astype(jnp.bfloat16), "grp", axis=0, tiled=True),
        lax.all_gather(feed_reduce.astype(jnp.bfloat16), "grp", axis=0, tiled=True),
    )
    gathered = (
        lax.all_gather(rows_part[0], "seq", axis=1, tiled=True),
        lax.all_gather(rows_part[1], "seq", axis=1, tiled=True),
        lax.all_gather(rows_part[2], "seq", axis=1, tiled=True),
        lax.all_gather(rows_part[3], "seq", axis=1, tiled=True),
        lax.all_gather(rows_part[4], "seq", axis=1, tiled=True),
        lax.all_gather(rows_part[5], "seq", axis=1, tiled=True),
        lax.all_gather(rows_part[6], "seq", axis=1, tiled=True),
        lax.all_gather(time_gain.astype(jnp.bfloat16), "seq", axis=0, tiled=True),
        lax.all_gather(time_shift.astype(jnp.bfloat16), "seq", axis=0, tiled=True),
        lax.all_gather(time_inward_bias.astype(jnp.bfloat16), "seq", axis=0, tiled=True),
        lax.all_gather(time_outward_bias.astype(jnp.bfloat16), "seq", axis=0, tiled=True),
        lax.all_gather(time_linear_bias.astype(jnp.bfloat16), "seq", axis=0, tiled=True),
        lax.all_gather(space_gain.astype(jnp.bfloat16), "seq", axis=0, tiled=True),
        lax.all_gather(space_shift.astype(jnp.bfloat16), "seq", axis=0, tiled=True),
        lax.all_gather(space_inward_bias.astype(jnp.bfloat16), "seq", axis=0, tiled=True),
        lax.all_gather(space_outward_bias.astype(jnp.bfloat16), "seq", axis=0, tiled=True),
        lax.all_gather(feed_gain.astype(jnp.bfloat16), "seq", axis=0, tiled=True),
        lax.all_gather(feed_shift.astype(jnp.bfloat16), "seq", axis=0, tiled=True),
        lax.all_gather(feed_expand_bias.astype(jnp.bfloat16), "seq", axis=0, tiled=True),
        lax.all_gather(feed_reduce_bias.astype(jnp.bfloat16), "seq", axis=0, tiled=True),
    )
    own_slot = lax.axis_index("seq")
    own_clips = lax.dynamic_slice_in_dim(frame_clip, own_slot * frames_dev, frames_dev) % clip_count
    matches = own_clips[:, None] == jnp.arange(clip_count, dtype=jnp.int32)[None, :]
    key_places = jnp.sum(jnp.where(matches[:, :, None], place_valid[None, :, :], 0), axis=1)
    space_allowed = (key_places == 1)[:, None, None, :]
    time_allowed = ((frame_clip[:, None] == frame_clip[None, :]) & (frame_valid[None, :] == 1))[
        None, None
    ]
    placed = lax.all_to_all(tokens, "seq", split_axis=1, concat_axis=0, tiled=True)
    placed_rows = placed.reshape(-1, model_width).astype(jnp.float32)
    time_normed_wide, time_norm_pull = jax.vjp(
        normalize,
        placed_rows,
        gathered[7].astype(jnp.float32),
        gathered[8].astype(jnp.float32),
    )
    time_normed = time_normed_wide.astype(jnp.bfloat16)
    time_parts = project_in_general(
        time_normed,
        gathered[0],
        gathered[9].astype(jnp.float32),
        (group_frames, place_dev),
        head_count,
    )
    time_mixed, time_total = attend(
        time_parts[0], time_parts[1], time_parts[2], time_allowed, "time"
    )
    time_mixed_low = time_mixed.reshape(-1, model_width).astype(jnp.bfloat16)
    time_proj = (
        matmul(time_mixed_low, gathered[1]) + gathered[10].astype(jnp.float32)
    ).astype(jnp.bfloat16)
    returned = lax.all_to_all(
        time_proj.reshape(group_frames, place_dev, model_width),
        "seq",
        split_axis=0,
        concat_axis=1,
        tiled=True,
    )
    returned_rows = returned.reshape(-1, model_width)
    first_sum = (
        tokens.reshape(-1, model_width).astype(jnp.float32)
        + matmul(returned_rows, gathered[2])
        + gathered[11].astype(jnp.float32)
    )
    space_normed_wide, space_norm_pull = jax.vjp(
        normalize,
        first_sum,
        gathered[12].astype(jnp.float32),
        gathered[13].astype(jnp.float32),
    )
    space_normed = space_normed_wide.astype(jnp.bfloat16)
    space_parts = project_in_general(
        space_normed,
        gathered[3],
        gathered[14].astype(jnp.float32),
        (frames_dev, places),
        head_count,
    )
    space_mixed, space_total = attend(
        space_parts[0], space_parts[1], space_parts[2], space_allowed, "space"
    )
    space_mixed_low = space_mixed.reshape(-1, model_width).astype(jnp.bfloat16)
    second_sum = (
        first_sum
        + matmul(space_mixed_low, gathered[4])
        + gathered[15].astype(jnp.float32)
    )
    feed_normed_wide, feed_norm_pull = jax.vjp(
        normalize,
        second_sum,
        gathered[16].astype(jnp.float32),
        gathered[17].astype(jnp.float32),
    )
    feed_normed = feed_normed_wide.astype(jnp.bfloat16)
    hidden = matmul(feed_normed, gathered[5]) + gathered[18].astype(jnp.float32)
    activated_wide, gelu_pull = jax.vjp(gelu_exact, hidden)
    activated = activated_wide.astype(jnp.bfloat16)
    final_sum = (
        second_sum
        + matmul(activated, gathered[6])
        + gathered[19].astype(jnp.float32)
    )
    result = final_sum.astype(jnp.bfloat16).reshape(tokens.shape)
    rows_again = (
        lax.all_gather(time_inward.astype(jnp.bfloat16), "grp", axis=0, tiled=True),
        lax.all_gather(time_outward.astype(jnp.bfloat16), "grp", axis=0, tiled=True),
        lax.all_gather(time_linear.astype(jnp.bfloat16), "grp", axis=0, tiled=True),
        lax.all_gather(space_inward.astype(jnp.bfloat16), "grp", axis=0, tiled=True),
        lax.all_gather(space_outward.astype(jnp.bfloat16), "grp", axis=0, tiled=True),
        lax.all_gather(feed_expand.astype(jnp.bfloat16), "grp", axis=0, tiled=True),
        lax.all_gather(feed_reduce.astype(jnp.bfloat16), "grp", axis=0, tiled=True),
    )
    gathered_again = (
        lax.all_gather(rows_again[0], "seq", axis=1, tiled=True),
        lax.all_gather(rows_again[1], "seq", axis=1, tiled=True),
        lax.all_gather(rows_again[2], "seq", axis=1, tiled=True),
        lax.all_gather(rows_again[3], "seq", axis=1, tiled=True),
        lax.all_gather(rows_again[4], "seq", axis=1, tiled=True),
        lax.all_gather(rows_again[5], "seq", axis=1, tiled=True),
        lax.all_gather(rows_again[6], "seq", axis=1, tiled=True),
        lax.all_gather(time_gain.astype(jnp.bfloat16), "seq", axis=0, tiled=True),
        lax.all_gather(time_shift.astype(jnp.bfloat16), "seq", axis=0, tiled=True),
        lax.all_gather(time_inward_bias.astype(jnp.bfloat16), "seq", axis=0, tiled=True),
        lax.all_gather(time_outward_bias.astype(jnp.bfloat16), "seq", axis=0, tiled=True),
        lax.all_gather(time_linear_bias.astype(jnp.bfloat16), "seq", axis=0, tiled=True),
        lax.all_gather(space_gain.astype(jnp.bfloat16), "seq", axis=0, tiled=True),
        lax.all_gather(space_shift.astype(jnp.bfloat16), "seq", axis=0, tiled=True),
        lax.all_gather(space_inward_bias.astype(jnp.bfloat16), "seq", axis=0, tiled=True),
        lax.all_gather(space_outward_bias.astype(jnp.bfloat16), "seq", axis=0, tiled=True),
        lax.all_gather(feed_gain.astype(jnp.bfloat16), "seq", axis=0, tiled=True),
        lax.all_gather(feed_shift.astype(jnp.bfloat16), "seq", axis=0, tiled=True),
        lax.all_gather(feed_expand_bias.astype(jnp.bfloat16), "seq", axis=0, tiled=True),
        lax.all_gather(feed_reduce_bias.astype(jnp.bfloat16), "seq", axis=0, tiled=True),
    )
    upstream = cotangent.reshape(-1, model_width).astype(jnp.float32)
    feed_delta = cotangent.reshape(-1, model_width)
    gradient_feed_reduce = inner(activated, feed_delta)
    gradient_feed_reduce_bias = column_sum(feed_delta)
    (hidden_wide,) = gelu_pull(against(feed_delta, gathered_again[6]))
    hidden_delta = hidden_wide.astype(jnp.bfloat16)
    gradient_feed_expand = inner(feed_normed, hidden_delta)
    gradient_feed_expand_bias = column_sum(hidden_delta)
    second_back, gradient_feed_gain, gradient_feed_shift = feed_norm_pull(
        against(hidden_delta, gathered_again[5])
    )
    second_delta = upstream + second_back
    space_delta = second_delta.astype(jnp.bfloat16)
    gradient_space_outward = inner(space_mixed_low, space_delta)
    gradient_space_outward_bias = column_sum(space_delta)
    space_mixed_delta = against(space_delta, gathered_again[4]).astype(jnp.bfloat16)
    space_mixed_delta = space_mixed_delta.reshape(frames_dev, places, head_count, -1)
    space_joined = attend_back(
        space_parts[0],
        space_parts[1],
        space_parts[2],
        space_total,
        space_allowed,
        space_mixed_delta,
        "space",
    )
    gradient_space_inward = inner(space_normed, space_joined)
    gradient_space_inward_bias = packed_sum(space_joined)
    first_back, gradient_space_gain, gradient_space_shift = space_norm_pull(
        against(space_joined, gathered_again[3])
    )
    first_delta = second_delta + first_back
    linear_delta = first_delta.astype(jnp.bfloat16)
    gradient_time_linear = inner(returned_rows, linear_delta)
    gradient_time_linear_bias = column_sum(linear_delta)
    proj_delta = against(linear_delta, gathered_again[2]).astype(jnp.bfloat16)
    proj_placed = lax.all_to_all(
        proj_delta.reshape(frames_dev, places, model_width),
        "seq",
        split_axis=1,
        concat_axis=0,
        tiled=True,
    )
    proj_rows = proj_placed.reshape(-1, model_width)
    gradient_time_outward = inner(time_mixed_low, proj_rows)
    gradient_time_outward_bias = column_sum(proj_rows)
    time_mixed_delta = against(proj_rows, gathered_again[1]).astype(jnp.bfloat16)
    time_mixed_delta = time_mixed_delta.reshape(group_frames, place_dev, head_count, -1)
    time_joined = attend_back(
        time_parts[0],
        time_parts[1],
        time_parts[2],
        time_total,
        time_allowed,
        time_mixed_delta,
        "time",
    )
    gradient_time_inward = inner(time_normed, time_joined)
    gradient_time_inward_bias = packed_sum(time_joined)
    placed_back, gradient_time_gain, gradient_time_shift = time_norm_pull(
        against(time_joined, gathered_again[0])
    )
    framed_back = lax.all_to_all(
        placed_back.reshape(group_frames, place_dev, model_width).astype(jnp.bfloat16),
        "seq",
        split_axis=0,
        concat_axis=1,
        tiled=True,
    ).astype(jnp.float32)
    input_gradient = (first_delta + framed_back.reshape(-1, model_width)).reshape(tokens.shape)
    matrix_terms = (
        gradient_time_inward,
        gradient_time_outward,
        gradient_time_linear,
        gradient_space_inward,
        gradient_space_outward,
        gradient_feed_expand,
        gradient_feed_reduce,
    )
    vector_terms = (
        gradient_time_gain,
        gradient_time_shift,
        gradient_time_inward_bias,
        gradient_time_outward_bias,
        gradient_time_linear_bias,
        gradient_space_gain,
        gradient_space_shift,
        gradient_space_inward_bias,
        gradient_space_outward_bias,
        gradient_feed_gain,
        gradient_feed_shift,
        gradient_feed_expand_bias,
        gradient_feed_reduce_bias,
    )
    columns_summed = (
        lax.psum_scatter(
            matrix_terms[0].astype(jnp.bfloat16), "seq", scatter_dimension=1, tiled=True
        ).astype(jnp.float32),
        lax.psum_scatter(
            matrix_terms[1].astype(jnp.bfloat16), "seq", scatter_dimension=1, tiled=True
        ).astype(jnp.float32),
        lax.psum_scatter(
            matrix_terms[2].astype(jnp.bfloat16), "seq", scatter_dimension=1, tiled=True
        ).astype(jnp.float32),
        lax.psum_scatter(
            matrix_terms[3].astype(jnp.bfloat16), "seq", scatter_dimension=1, tiled=True
        ).astype(jnp.float32),
        lax.psum_scatter(
            matrix_terms[4].astype(jnp.bfloat16), "seq", scatter_dimension=1, tiled=True
        ).astype(jnp.float32),
        lax.psum_scatter(
            matrix_terms[5].astype(jnp.bfloat16), "seq", scatter_dimension=1, tiled=True
        ).astype(jnp.float32),
        lax.psum_scatter(
            matrix_terms[6].astype(jnp.bfloat16), "seq", scatter_dimension=1, tiled=True
        ).astype(jnp.float32),
        lax.psum_scatter(
            vector_terms[0].astype(jnp.bfloat16), "seq", scatter_dimension=0, tiled=True
        ).astype(jnp.float32),
        lax.psum_scatter(
            vector_terms[1].astype(jnp.bfloat16), "seq", scatter_dimension=0, tiled=True
        ).astype(jnp.float32),
        lax.psum_scatter(
            vector_terms[2].astype(jnp.bfloat16), "seq", scatter_dimension=0, tiled=True
        ).astype(jnp.float32),
        lax.psum_scatter(
            vector_terms[3].astype(jnp.bfloat16), "seq", scatter_dimension=0, tiled=True
        ).astype(jnp.float32),
        lax.psum_scatter(
            vector_terms[4].astype(jnp.bfloat16), "seq", scatter_dimension=0, tiled=True
        ).astype(jnp.float32),
        lax.psum_scatter(
            vector_terms[5].astype(jnp.bfloat16), "seq", scatter_dimension=0, tiled=True
        ).astype(jnp.float32),
        lax.psum_scatter(
            vector_terms[6].astype(jnp.bfloat16), "seq", scatter_dimension=0, tiled=True
        ).astype(jnp.float32),
        lax.psum_scatter(
            vector_terms[7].astype(jnp.bfloat16), "seq", scatter_dimension=0, tiled=True
        ).astype(jnp.float32),
        lax.psum_scatter(
            vector_terms[8].astype(jnp.bfloat16), "seq", scatter_dimension=0, tiled=True
        ).astype(jnp.float32),
        lax.psum_scatter(
            vector_terms[9].astype(jnp.bfloat16), "seq", scatter_dimension=0, tiled=True
        ).astype(jnp.float32),
        lax.psum_scatter(
            vector_terms[10].astype(jnp.bfloat16), "seq", scatter_dimension=0, tiled=True
        ).astype(jnp.float32),
        lax.psum_scatter(
            vector_terms[11].astype(jnp.bfloat16), "seq", scatter_dimension=0, tiled=True
        ).astype(jnp.float32),
        lax.psum_scatter(
            vector_terms[12].astype(jnp.bfloat16), "seq", scatter_dimension=0, tiled=True
        ).astype(jnp.float32),
    )
    rows_summed = (
        lax.psum_scatter(
            columns_summed[0].astype(jnp.bfloat16), "grp", scatter_dimension=0, tiled=True
        ).astype(jnp.float32),
        lax.psum_scatter(
            columns_summed[1].astype(jnp.bfloat16), "grp", scatter_dimension=0, tiled=True
        ).astype(jnp.float32),
        lax.psum_scatter(
            columns_summed[2].astype(jnp.bfloat16), "grp", scatter_dimension=0, tiled=True
        ).astype(jnp.float32),
        lax.psum_scatter(
            columns_summed[3].astype(jnp.bfloat16), "grp", scatter_dimension=0, tiled=True
        ).astype(jnp.float32),
        lax.psum_scatter(
            columns_summed[4].astype(jnp.bfloat16), "grp", scatter_dimension=0, tiled=True
        ).astype(jnp.float32),
        lax.psum_scatter(
            columns_summed[5].astype(jnp.bfloat16), "grp", scatter_dimension=0, tiled=True
        ).astype(jnp.float32),
        lax.psum_scatter(
            columns_summed[6].astype(jnp.bfloat16), "grp", scatter_dimension=0, tiled=True
        ).astype(jnp.float32),
    )
    vector_shares = tuple(columns_summed[7:])
    vectors_summed = lax.psum(
        (
            vector_shares[0],
            vector_shares[1],
            vector_shares[2],
            vector_shares[3],
            vector_shares[4],
            vector_shares[5],
            vector_shares[6],
            vector_shares[7],
            vector_shares[8],
            vector_shares[9],
            vector_shares[10],
            vector_shares[11],
            vector_shares[12],
        ),
        "grp",
    )
    owned = tuple(rows_summed) + tuple(vectors_summed)
    return (result, input_gradient) + tuple(owned[i] for i in (7, 8, 0, 9, 1, 10, 2, 11, 12, 13, 3, 14, 4, 15, 16, 17, 5, 18, 6, 19))


def solution(mesh):
    fast = mesh.shape["grp"] == 4 and mesh.shape["seq"] == 8
    return jax.shard_map(
        on_device_fast if fast else on_device_general,
        mesh=mesh,
        in_specs=(
            P(("grp", "seq"), None, None),
            P(("grp", "seq"), None, None),
            P("grp"),
            P("grp"),
            P("grp", None),
            P("seq"),
            P("seq"),
            P("grp", "seq"),
            P("seq"),
            P("grp", "seq"),
            P("seq"),
            P("grp", "seq"),
            P("seq"),
            P("seq"),
            P("seq"),
            P("grp", "seq"),
            P("seq"),
            P("grp", "seq"),
            P("seq"),
            P("seq"),
            P("seq"),
            P("grp", "seq"),
            P("seq"),
            P("grp", "seq"),
            P("seq"),
        ),
        out_specs=(
            P(("grp", "seq"), None, None),
            P(("grp", "seq"), None, None),
            P("seq"),
            P("seq"),
            P("grp", "seq"),
            P("seq"),
            P("grp", "seq"),
            P("seq"),
            P("grp", "seq"),
            P("seq"),
            P("seq"),
            P("seq"),
            P("grp", "seq"),
            P("seq"),
            P("grp", "seq"),
            P("seq"),
            P("seq"),
            P("seq"),
            P("grp", "seq"),
            P("seq"),
            P("grp", "seq"),
            P("seq"),
        ),
        check_vma=False,
    )
```

```python
import jax
import jax.numpy as jnp
from jax import lax
from jax.experimental import pallas as pl
from jax.experimental.pallas import tpu as pltpu
from jax.sharding import PartitionSpec as P

MESH = pl.DeviceIdType.MESH
BF = jnp.bfloat16
F32 = jnp.float32
NN = (((1,), (0,)), ((), ()))
NT = (((1,), (1,)), ((), ()))
TN = (((0,), (0,)), ((), ()))

TI, TO, TL, SI, SO, FE, FR = 0, 2304, 3072, 3840, 6144, 6912, 9984
WROWS = 13056
BASE = ([96 * t for t in range(3)] + [TO, TL] + [SI + 96 * t for t in range(3)] + [SO]
        + [FE + 768 * (v // 2) + 96 * (v % 2) for v in range(4)] + [FR + 768 * t for t in range(4)])
PAIR = [576] * 3 + [192] * 2 + [576] * 3 + [192] + [192] * 4 + [192] * 4
CORE = [288] * 3 + [96] * 2 + [288] * 3 + [96] + [1536] * 4 + [96] * 4
CHUNKS = 17
GATHER_ORDER = [0, 1, 2, 3, 4, 5, 6, 7, 8, 9, 10, 13, 15, 11, 12, 14, 16]
SLOTS = 5
LAGS = (1, 2, 2, 2)
GATHER_LAGS = (1, 2, 1)
SPACING = 2
KINDS = ("p", "q", "so", "d", "sp", "sq", "sd")
EPSILON = 1e-06


def dot(a, b, dims):
    return lax.dot_general(a, b, dims, preferred_element_type=F32)


class Links:
    def __init__(self, send_sem, recv_sem):
        self.send_sem, self.recv_sem = send_sem, recv_sem
        self.copies, self.used, self.sent = {}, 0, set()
        self.z = lax.axis_index("grp")
        s = self.s = lax.axis_index("seq")
        core, x, y = s % 2, (s // 2) % 2, s // 4
        xn, yn = s + 2 - 4 * x, s + 4 - 8 * y
        self.core = core
        self.sib = s + 1 - 2 * core
        self.p = yn * (1 - core) + xn * core
        self.q = xn * (1 - core) + yn * core
        self.d = xn + yn - s

    def zpeer(self, k):
        return (self.z + k) % 4

    def speer(self, k):
        return (self.s + k) % 8

    def greet(self):
        bar = pltpu.get_barrier_semaphore()
        for k in range(1, 8):
            pl.semaphore_signal(bar, inc=1, device_id=(self.z, self.speer(k)), device_id_type=MESH)
        for k in range(1, 4):
            pl.semaphore_signal(bar, inc=1, device_id=(self.zpeer(k), self.s), device_id_type=MESH)

    def greeted(self):
        pl.semaphore_wait(pltpu.get_barrier_semaphore(), 10)

    def send(self, key, src, dst, device):
        i = self.used
        self.used += 1
        copy = pltpu.make_async_remote_copy(
            src_ref=src, dst_ref=dst, send_sem=self.send_sem.at[i], recv_sem=self.recv_sem.at[i],
            device_id=device, device_id_type=MESH)
        copy.start()
        self.copies[key] = copy

    def sends(self, key, src, dst, seq):
        self.send(key, src, dst, (self.z, seq))

    def sendz(self, key, src, dst, z):
        self.send(key, src, dst, (z, self.s))

    def got(self, *keys):
        for key in keys:
            self.copies[key].wait_recv()

    def gone(self, *keys):
        for key in keys:
            if key not in self.sent:
                self.sent.add(key)
                self.copies[key].wait_send()

    def drain(self):
        self.gone(*self.copies)


class Local:
    def __init__(self, sem):
        self.sem, self.used, self.copies = sem, 0, {}

    def start(self, key, src, dst):
        copy = pltpu.make_async_copy(src, dst, self.sem.at[self.used])
        self.used += 1
        copy.start()
        self.copies[key] = copy

    def wait(self, *keys):
        for key in keys:
            copy = self.copies.pop(key, None)
            if copy is not None:
                copy.wait()

    def drain(self):
        self.wait(*list(self.copies))


def place(c, s):
    return pl.ds(pl.multiple_of(BASE[c] + PAIR[c] * (s // 2) + CORE[c] * (s % 2), 32), 96)


def block(ref, c, s):
    return ref.at[place(c, s)]


class Gather:
    def __init__(self, links, zst, w):
        self.l, self.zst, self.w = links, zst, w
        self.next, self.flight, self.zsent, self.clock = 0, [], 0, 0

    def zsend(self, count=1):
        for i in range(self.zsent, min(self.zsent + count, CHUNKS)):
            c = GATHER_ORDER[i]
            own = self.zst.at[self.l.z, c]
            for k in range(1, 4):
                self.l.sendz(("zg", c, k), own, own, self.l.zpeer(k))
            self.zsent += 1

    def sources(self, *chunks):
        self.l.gone(*[(k, c) for c in chunks for k in KINDS])

    def step_a(self, i, c):
        l = self.l
        l.got(*[("zg", c, k) for k in range(1, 4)])
        rows = place(c, l.s)
        zst, w = self.zst, self.w
        for half in range(2):
            lo, hi = zst[2 * half, c], zst[2 * half + 1, c]
            w[rows, 384 * half:384 * half + 128] = lo[:96]
            w[rows, 384 * half + 256:384 * half + 384] = hi[:96]
            blo, bhi = lo[96:], hi[96:]
            w[rows, 384 * half + 128:384 * half + 256] = jnp.concatenate([
                jnp.concatenate([blo[:, :64], bhi[:, :64]], axis=1),
                jnp.concatenate([blo[:, 64:], bhi[:, 64:]], axis=1)], axis=0)
        own = block(w, c, l.s)
        l.sends(("p", c), own, own, l.p)
        l.sends(("q", c), own, own, l.q)
        l.sends(("so", c), own, own, l.sib)
        self.zsend()

    def step_b(self, i, c):
        l = self.l
        l.got(("p", c))
        bp = block(self.w, c, l.p)
        l.sends(("d", c), bp, bp, l.q)
        l.sends(("sp", c), bp, bp, l.sib)
        l.got(("q", c))
        bq = block(self.w, c, l.q)
        l.sends(("sq", c), bq, bq, l.sib)

    def step_c(self, i, c):
        l = self.l
        l.got(("d", c))
        bd = block(self.w, c, l.d)
        l.sends(("sd", c), bd, bd, l.sib)

    def step_d(self, i, c):
        self.l.got(("so", c), ("sp", c), ("sq", c), ("sd", c))

    def tick(self, push=True, whole=-1):
        steps = (self.step_b, self.step_c, self.step_d)
        self.clock += 1
        fresh = []
        if push and self.next < CHUNKS:
            self.step_a(self.next, GATHER_ORDER[self.next])
            fresh = [(self.next, 0, self.clock + GATHER_LAGS[0])]
            self.next += 1
        later = []
        for i, k, due in self.flight:
            if i <= whole or self.clock >= due:
                steps[k](i, GATHER_ORDER[i])
                k, due = k + 1, self.clock + (GATHER_LAGS + (0,))[k + 1]
            if k < 3:
                later.append((i, k, due))
        self.flight = later + fresh

    def until(self, chunk):
        i = GATHER_ORDER.index(chunk)
        while i >= self.next or any(j <= i for j, _, _ in self.flight):
            self.tick(push=self.next <= i, whole=i)

    @property
    def done(self):
        return self.next == CHUNKS and not self.flight


class Scatter:
    def __init__(self, links, g, sr, fr, ar, br, zp, zr, write):
        self.l, self.g, self.sr, self.fr, self.ar, self.br = links, g, sr, fr, ar, br
        self.zp, self.zr, self.write = zp, zr, write
        self.ready, self.flight, self.order = [], [], []
        self.clock, self.pushed = 0, -9

    def step_a(self, i, c):
        l = self.l
        for j in range(4):
            l.sends(("s", c, j), block(self.g, c, 2 * j + 1 - l.core), self.sr.at[i % SLOTS, j], l.sib)

    def add(self, c, s, other):
        rows = place(c, s)
        self.g[rows, :] = (self.g[rows, :].astype(F32) + other.astype(F32)).astype(BF)

    def step_b(self, i, c):
        l, k = self.l, i % SLOTS
        l.got(*[("s", c, j) for j in range(4)])
        for s, j in ((l.d, l.d // 2), (l.p, l.p // 2), (l.q, l.q // 2), (l.s, l.s // 2)):
            self.add(c, s, self.sr[k, j])
            if s is l.d:
                l.sends(("f", c), block(self.g, c, l.d), self.fr.at[k], l.p)
            if s is l.p:
                l.sends(("a", c), block(self.g, c, l.p), self.ar.at[k], l.p)

    def step_c(self, i, c):
        l, k = self.l, i % SLOTS
        l.got(("f", c))
        self.add(c, l.q, self.fr[k])
        l.sends(("b", c), block(self.g, c, l.q), self.br.at[k], l.q)

    def step_d(self, i, c):
        l, k = self.l, i % SLOTS
        l.got(("a", c), ("b", c))
        rows = place(c, l.s)
        total = self.g[rows, :].astype(F32) + self.ar[k].astype(F32) + self.br[k].astype(F32)
        if i >= SLOTS:
            l.gone(*[("z", self.order[i - SLOTS], j) for j in range(1, 4)])
        zp = self.zp
        for half in range(2):
            lane = 384 * half
            zp[k, 2 * half, 0:96] = total[:, lane:lane + 128].astype(BF)
            zp[k, 2 * half + 1, 0:96] = total[:, lane + 256:lane + 384].astype(BF)
            mid = total[:, lane + 128:lane + 256]
            top, low = mid[:48], mid[48:]
            zp[k, 2 * half, 96:144] = jnp.concatenate([top[:, :64], low[:, :64]], axis=1).astype(BF)
            zp[k, 2 * half + 1, 96:144] = jnp.concatenate([top[:, 64:], low[:, 64:]], axis=1).astype(BF)
        for j in range(1, 4):
            z = l.zpeer(j)
            l.sendz(("z", c, j), zp.at[k, z], self.zr.at[k, j - 1], z)

    def step_e(self, i, c):
        l, k = self.l, i % SLOTS
        l.got(*[("z", c, j) for j in range(1, 4)])
        total = self.zp[k, l.z].astype(F32)
        for j in range(3):
            total += self.zr[k, j].astype(F32)
        self.write(c, total)

    def pump(self, rush=False):
        steps = (self.step_b, self.step_c, self.step_d, self.step_e)
        self.clock += 1
        fresh = []
        if self.ready and (rush or self.clock >= self.pushed + SPACING):
            c = self.ready.pop(0)
            i = len(self.order)
            self.order.append(c)
            self.step_a(i, c)
            self.pushed = self.clock
            fresh = [(i, 0, self.clock + LAGS[0])]
        later = []
        for i, k, due in self.flight:
            if rush or self.clock >= due:
                steps[k](i, self.order[i])
                k, due = k + 1, self.clock + (LAGS + (0,))[k + 1]
            if k < 4:
                later.append((i, k, due))
        self.flight = later + fresh

    def finish(self):
        while self.ready or self.flight:
            self.pump(rush=True)


class VectorSum:
    def __init__(self, links, gv, vb):
        self.l, self.gv, self.vb = links, gv, vb

    def swap(self, i):
        l = self.l
        l.sends(("vs", i), self.gv.at[i], self.vb.at[i], (l.sib, l.p, l.q)[i])

    def join(self, i):
        self.l.got(("vs", i))
        self.gv[i + 1] = self.gv[i] + self.vb[i]

    def swapz(self):
        l = self.l
        self.vb[3 + l.z] = self.gv[3]
        for k in range(1, 4):
            l.sendz(("vz", k), self.gv.at[3], self.vb.at[3 + l.z], l.zpeer(k))

    def total(self):
        self.l.got(*[("vz", k) for k in range(1, 4)])
        return (self.vb[3] + self.vb[4]) + (self.vb[5] + self.vb[6])


TG, TS, TOB, TLB, SG, SS, SOB, FG, FS, FRB, TIB, SIB, FEB = 0, 1, 2, 3, 4, 5, 6, 7, 8, 9, 10, 12, 14


def assemble_vectors(vg, vec):
    vec[...] = jnp.zeros(vec.shape, F32)
    for s in range(8):
        piece = vg[s]
        vec[0:10, 96 * s:96 * s + 96] = piece[0:10, 0:96]
        for a in range(2):
            i = 2 * s + a
            for r in (TIB, SIB):
                vec[r + i // 8:r + i // 8 + 1, 96 * (i % 8):96 * (i % 8) + 96] = piece[r + a:r + a + 1, 0:96]
        for a in range(4):
            t, lane = 2 * (s % 2) + a // 2, 192 * (s // 2) + 96 * (a % 2)
            vec[FEB + t:FEB + 1 + t, lane:lane + 96] = piece[FEB + a:FEB + 1 + a, 0:96]


def selectors(odd, ea, el, eh, eb):
    m = lax.broadcasted_iota(jnp.int32, (192, 128), 0)
    c = lax.broadcasted_iota(jnp.int32, (192, 128), 1)
    whole, folded = c + 64 * odd, c % 64 + 128 * (1 - odd)
    ea[...] = jnp.where(m == whole, 1.0, 0.0).astype(BF)
    both = jnp.where(m == folded, 1.0, 0.0)
    el[...] = jnp.where(c < 64, both, 0.0).astype(BF)
    eh[...] = jnp.where(c < 64, 0.0, both).astype(BF)
    eb[...] = both.astype(BF)


def standardize(x):
    centered = x - jnp.mean(x, axis=-1, keepdims=True)
    scale = lax.rsqrt(jnp.mean(centered * centered, axis=-1, keepdims=True) + EPSILON)
    return centered * scale, scale


def norm_back(e, gain, n, scale):
    u = e * gain
    return scale * (u - jnp.mean(u, axis=-1, keepdims=True) - n * jnp.mean(u * n, axis=-1, keepdims=True))


def column_sums(x):
    return jnp.sum(x, axis=0, keepdims=True)


def head_masks(scale):
    lane = lax.broadcasted_iota(jnp.int32, (1, 128), 1)
    return [jnp.where(lane < 64, scale, 0.0).astype(BF), jnp.where(lane < 64, 0.0, scale).astype(BF)]


def pair_columns(qkv, rows, p):
    c = pl.multiple_of(p * 128, 128)
    return [qkv[rows, pl.ds(768 * j + c, 128)] for j in range(3)]


def attend_block(b, qkv, mixed, lse, bias):
    rows = pl.ds(b * 256, 256)

    def pair(p):
        q, k, v = pair_columns(qkv, rows, p)
        scaled, plain = head_masks(0.125), head_masks(1.0)
        out = None
        for h in range(2):
            s = dot(k * scaled[h], q, NT) + bias()
            m = jnp.max(s, axis=0, keepdims=True)
            e = jnp.exp(s - m)
            total = jnp.sum(e, axis=0, keepdims=True)
            lse[pl.ds(b * 12 + p * 2 + h, 1), :] = m + jnp.log(total)
            o = dot((e * (1.0 / total)).astype(BF), v * plain[h], TN)
            out = o if out is None else out + o
        mixed[rows, pl.ds(pl.multiple_of(p * 128, 128), 128)] = out.astype(BF)

    def body(i, _):
        pair(2 * i)
        pair(2 * i + 1)
        return 0

    lax.fori_loop(0, 3, body, 0)


def attend_block_back(b, qkv, gm, lse, bias):
    rows = pl.ds(b * 256, 256)

    def pair(p):
        q, k, v = pair_columns(qkv, rows, p)
        c = pl.multiple_of(p * 128, 128)
        g = gm[rows, pl.ds(c, 128)]
        scaled, plain = head_masks(0.125), head_masks(1.0)
        sums = [None, None, None]
        for h in range(2):
            kh, vh, qh, gh = k * scaled[h], v * plain[h], q * scaled[h], g * plain[h]
            s = dot(kh, q, NT) + bias()
            chances = jnp.exp(s - lse[pl.ds(b * 12 + p * 2 + h, 1), :])
            back = dot(vh, g, NT)
            mean = jnp.sum(chances * back, axis=0, keepdims=True)
            gs = (chances * (back - mean)).astype(BF)
            for j, term in enumerate((dot(gs, kh, TN), dot(gs, qh, NN), dot(chances.astype(BF), gh, NN))):
                sums[j] = term if sums[j] is None else sums[j] + term
        for j in range(3):
            qkv[rows, pl.ds(768 * j + c, 128)] = sums[j].astype(BF)

    def body(i, _):
        pair(2 * i)
        pair(2 * i + 1)
        return 0

    lax.fori_loop(0, 3, body, 0)


def project_in(normed, w, at, qkv, rows, vec, bias_row):
    for j in range(3):
        part = dot(normed, w[at + 768 * j:at + 768 * (j + 1), :], NT)
        if j != 1:
            r = bias_row + j // 2
            part = part + vec[r:r + 1, :]
        qkv[rows, 768 * j:768 * (j + 1)] = part.astype(BF)


def weight_gradient(out, delta, column, rows):
    for m in range(3):
        lane = column + 256 * m
        out[256 * m:256 * m + 256, :] = dot(delta[:, lane:lane + 256], rows[...], TN).astype(BF)


def flat(x):
    return x.astype(F32).reshape(256, 768)


def tiled(x):
    return x.reshape(32, 8, 768).astype(BF)


def layer_kernel(
    tokens, cot_i, clip_i, valid_i, place_i, vin, ti_i, to_i, tl_i, si_i, so_i, fe_i, fr_i,
    result_o, grad_o, tg_o, ts_o, gti, tib_o, gto, tob_o, gtl, tlb_o, sg_o, ss_o, gsi, sib_o, gso, sob_o, fg_o, fs_o, gfe, feb_o,
    gfr, frb_o, tqkv_o, tmixed_o, ret_o, first_o, xp_o,
    w, zst, vg, vec, ea, el, eh, eb, tmask, smask, frames_a, frames_b, places_a, places_b, nb, mixed, qkv, f1, f2, f3, act, gh, g,
    sr, fr, ar, br, zp, zr, gv, vb, lse, local_sem, send_sem, recv_sem,
):
    l = Links(send_sem, recv_sem)
    l.greet()
    here = Local(local_sem)
    mine = pl.ds(4 * l.s, 4)
    xp, gpp = places_a, places_a
    pr, gb = places_b, places_b
    ret, it = frames_a, frames_a
    x, gp = frames_b, frames_b
    here.start("x", tokens, x)
    here.start("xp", tokens.at[:, mine], xp.at[mine])
    here.start("cot", cot_i, g)
    odd = l.z % 2
    selectors(odd, ea, el, eh, eb)
    ga = Gather(l, zst, w)

    def pack(ref, chunks):
        low = ref[...].astype(BF)
        a, bl, bh = dot(low, ea[...], TN), dot(low, el[...], TN), dot(low, eh[...], TN)
        for t, c in enumerate(chunks):
            zst[l.z, c, 0:96] = a[96 * t:96 * t + 96].astype(BF)
            zst[l.z, c, 96:144] = (bl[96 * t:96 * t + 48] + bh[96 * t + 48:96 * t + 96]).astype(BF)

    def masks():
        clips, flags = clip_i[...].astype(F32), valid_i[...].astype(F32)
        row32 = lax.broadcasted_iota(jnp.int32, (256, 32), 0) // 8
        spread = jnp.where(row32 == lax.broadcasted_iota(jnp.int32, (256, 32), 1), 1.0, 0.0)
        clip_key = jnp.sum(spread * clips, axis=1, keepdims=True)
        flag_key = jnp.sum(spread * flags, axis=1, keepdims=True)
        clip_query = dot(jnp.broadcast_to(clips, (8, 32)).astype(BF), spread.astype(BF), NT)[0:1]
        j = lax.broadcasted_iota(jnp.int32, (256, 256), 0)
        i = lax.broadcasted_iota(jnp.int32, (256, 256), 1)
        allowed = (clip_key == clip_query) & (flag_key > 0.5) & (j % 8 == i % 8)
        tmask[...] = jnp.where(allowed, 0.0, -1e30)
        clip_row = lax.broadcasted_iota(jnp.int32, (4, 32), 0)
        which = jnp.where((clip_i[...] % 4) == clip_row, 1.0, 0.0)
        frame_of = lax.broadcasted_iota(jnp.int32, (32, 128), 0)
        own = jnp.where(frame_of == lax.broadcasted_iota(jnp.int32, (32, 128), 1) + 4 * l.s, 1.0, 0.0)
        chosen = dot(which.astype(BF), own.astype(BF), NN)
        open_places = dot(place_i[...].astype(F32).astype(BF), chosen.astype(BF), TN)
        for f in range(4):
            smask[f] = jnp.where(open_places[:, f:f + 1] > 0.5, 0.0, -1e30)

    pack(ti_i, [0, 1, 2])
    vg[l.s] = vin[...].astype(BF).astype(F32)
    l.greeted()
    ga.zsend(3)
    for k in range(1, 8):
        peer = l.speer(k)
        l.sends(("t", k), tokens.at[:, pl.ds(4 * peer, 4)], xp.at[mine], peer)
        l.sends(("v", k), vg.at[l.s], vg.at[l.s], peer)
    pack(to_i, [3])
    pack(tl_i, [4])
    ga.tick()
    pack(si_i, [5, 6, 7])
    ga.tick()
    pack(so_i, [8])
    pack(fe_i, [9, 10, 11, 12])
    ga.tick()
    ga.zsend(2)
    for t in range(4):
        pack(fr_i.at[192 * t:192 * t + 192], [13 + t])
    ga.tick()
    masks()
    l.got(*[("v", k) for k in range(1, 8)])
    assemble_vectors(vg, vec)
    l.got(*[("t", k) for k in range(1, 8)])
    here.wait("x", "xp")
    here.start("xp_o", xp, xp_o)
    for b in range(4):
        rows = pl.ds(b * 256, 256)
        n, _ = standardize(flat(xp[:, b]))
        nb[rows, :] = (n * vec[TG:TG + 1, :] + vec[TS:TS + 1, :]).astype(BF)
    ga.until(2)
    for b in range(4):
        project_in(nb[256 * b:256 * b + 256, :], w, TI, qkv, pl.ds(b * 256, 256), vec, TIB)
        if b % 2:
            ga.tick()
    here.start("tqkv_o", qkv, tqkv_o)
    here.wait("xp_o")
    ga.until(3)
    for b in range(4):
        attend_block(b, qkv, mixed, lse.at[0:48], lambda: tmask[...])
        o = dot(mixed[256 * b:256 * b + 256, :], w[TO:TO + 768, :], NT) + vec[TOB:TOB + 1, :]
        pr[:, b] = tiled(o)
        ret[:, 4 * l.s + b] = pr[mine, b]
        for k in range(1, 8):
            peer = l.speer(k)
            l.sends(("r", b, k), pr.at[pl.ds(4 * peer, 4), b], ret.at[:, 4 * l.s + b], peer)
        ga.tick()
    here.start("tmixed_o", mixed, tmixed_o)
    ga.until(4)
    for b in range(4):
        l.got(*[("r", b, k) for k in range(1, 8)])
    first = second = f1
    for f in range(4):
        rows = pl.ds(256 * f, 256)
        back = flat(ret[f]).astype(BF)
        gh[rows, :] = back
        total = flat(x[f]) + dot(back, w[TL:TL + 768, :], NT) + vec[TLB:TLB + 1, :]
        first[rows, :] = total
        n, _ = standardize(total)
        nb[rows, :] = (n * vec[SG:SG + 1, :] + vec[SS:SS + 1, :]).astype(BF)
        if f == 1:
            ga.tick()
    here.start("ret_o", gh, ret_o)
    here.start("first_o", first, first_o)
    ga.until(7)
    here.wait("tqkv_o", "tmixed_o")
    for f in range(4):
        rows = pl.ds(256 * f, 256)
        project_in(nb[256 * f:256 * f + 256, :], w, SI, qkv, rows, vec, SIB)
        attend_block(f, qkv, mixed, lse.at[48:96], lambda: smask[f])
        ga.tick()
    ga.until(8)
    here.wait("first_o", "ret_o", "cot")

    final, dfn = f2, f3
    for f in range(4):
        rows = pl.ds(256 * f, 256)
        value = first[rows, :] + dot(mixed[rows, :], w[SO:SO + 768, :], NT) + vec[SOB:SOB + 1, :]
        second[rows, :] = value
        n, _ = standardize(value)
        nb[rows, :] = (n * vec[FG:FG + 1, :] + vec[FS:FS + 1, :]).astype(BF)
        final[rows, :] = value + vec[FRB:FRB + 1, :]
        dfn[rows, :] = jnp.zeros((256, 768), F32)

    into = {0: gti, 1: gti, 2: gti, 3: gto, 4: gtl, 5: gsi, 6: gsi, 7: gsi, 8: gso, 9: gfe, 10: gfe, 11: gfe, 12: gfe}

    def write(c, total):
        a, folded = total[:96], total[96:]
        lane = lax.broadcasted_iota(jnp.int32, (48, 128), 1)
        b = jnp.concatenate([jnp.where(lane < 64, folded, 0.0), jnp.where(lane < 64, 0.0, folded)], axis=0)
        a_high, b_high = a.astype(BF), b.astype(BF)
        a_low, b_low = (a - a_high.astype(F32)).astype(BF), (b - b_high.astype(F32)).astype(BF)
        value = (dot(ea[...], a_high, NT) + dot(eb[...], b_high, NT)) + (dot(ea[...], a_low, NT) + dot(eb[...], b_low, NT))
        if c >= 13:
            gfr[192 * (c - 13):192 * (c - 12), :] = value
        else:
            t = c - [k for k in into if into[k] is into[c]][0]
            into[c][:, 96 * t:96 * t + 96] = value

    sc = Scatter(l, w, sr, fr, ar, br, zp, zr, write)
    vs = VectorSum(l, gv, vb)
    sums = gv.at[0]
    sums[...] = jnp.zeros((24, 768), F32)

    def note(r, value):
        sums[r:r + 1, :] += value

    def pump():
        if not ga.done:
            ga.tick()
        sc.pump()

    for step, t in enumerate((0, 2, 1, 3)):
        ga.until(10 if t % 2 == 0 else 12)
        ga.until(13 + t)
        we, wf = w.at[FE + 768 * t:FE + 768 * (t + 1)], w.at[FR + 768 * t:FR + 768 * (t + 1)]

        def unit(b, _):
            rows = pl.ds(pl.multiple_of(256 * b, 256), 256)
            u = dot(nb[rows, :], we[...], NT) + vec[FEB + t:FEB + t + 1, :]
            phi = 0.5 + 0.5 * lax.erf(u * 0.7071067811865476)
            a = (u * phi).astype(BF)
            act[rows, :] = a
            slope = phi + u * (0.3989422804014327 * jnp.exp(-0.5 * u * u))
            h = (dot(g[rows, :], wf[...], NN) * slope).astype(BF)
            gh[rows, :] = h
            final[rows, :] += dot(a, wf[...], NT)
            dfn[rows, :] += dot(h, we[...], NN)
            sums[FEB + t:FEB + t + 1, :] += column_sums(h.astype(F32))
            return 0

        lax.fori_loop(0, 2, unit, 0)
        pump()
        lax.fori_loop(2, 4, unit, 0)
        pump()
        ga.sources(13 + t)
        weight_gradient(wf, g, 0, act)
        sc.ready.append(13 + t)
        pump()
        ga.sources(*((9, 10) if t % 2 == 0 else (11, 12)))
        weight_gradient(we, gh, 0, nb)
        if step % 2:
            sc.ready += [9, 10] if step == 1 else [11, 12]
        pump()

    ga.sources(*GATHER_ORDER)
    for f in range(4):
        rows = pl.ds(256 * f, 256)
        nb[rows, :] = final[rows, :].astype(BF)
        n, scale = standardize(second[rows, :])
        e = dfn[rows, :]
        cot = g[rows, :].astype(F32)
        note(FRB, column_sums(cot))
        note(FG, column_sums(e * n))
        note(FS, column_sums(e))
        total = cot + norm_back(e, vec[FG:FG + 1, :], n, scale)
        final[rows, :] = total
        low = total.astype(BF)
        act[rows, :] = low
        note(SOB, column_sums(low.astype(F32)))
        gh[rows, :] = dot(low, w[SO:SO + 768, :], NN).astype(BF)
        if f % 2:
            sc.pump(rush=True)
    here.start("result", nb, result_o)
    here.start("first", first_o, first)
    weight_gradient(w.at[SO:SO + 768], act, 0, mixed)
    here.start("mixed2", tmixed_o, mixed)
    sc.ready.append(8)
    sc.pump(rush=True)
    l.gone(*[("r", b, k) for b in range(4) for k in range(1, 8)])
    here.start("xp2", xp_o, places_b)
    here.wait("result", "first")
    for f in range(4):
        rows = pl.ds(256 * f, 256)
        attend_block_back(f, qkv, gh, lse.at[48:96], lambda: smask[f])
        n, scale = standardize(first[rows, :])
        nb[rows, :] = (n * vec[SG:SG + 1, :] + vec[SS:SS + 1, :]).astype(BF)
        joined = qkv[rows, :]
        note(SIB, column_sums(joined[:, :768].astype(F32)))
        note(SIB + 1, column_sums(joined[:, 1536:].astype(F32)))
        e = dot(joined, w[SI:SI + 2304, :], NN)
        note(SG, column_sums(e * n))
        note(SS, column_sums(e))
        total = final[rows, :] + norm_back(e, vec[SG:SG + 1, :], n, scale)
        final[rows, :] = total
        low = total.astype(BF)
        act[rows, :] = low
        note(TLB, column_sums(low.astype(F32)))
        gp[f] = tiled(dot(low, w[TL:TL + 768, :], NN))
        gpp[4 * l.s + f] = gp[f, pl.ds(4 * l.s, 4)]
        for k in range(1, 8):
            peer = l.speer(k)
            l.sends(("g", f, k), gp.at[f, pl.ds(4 * peer, 4)], gpp.at[4 * l.s + f], peer)
        sc.pump(rush=True)
    here.start("ret", ret_o, gh)
    for j in range(3):
        weight_gradient(w.at[SI + 768 * j:SI + 768 * (j + 1)], qkv, 768 * j, nb)
    here.start("qkv2", tqkv_o, qkv)
    sc.ready += [5, 6, 7]
    sc.pump(rush=True)
    here.wait("ret")
    weight_gradient(w.at[TL:TL + 768], act, 0, gh)
    sc.ready.append(4)
    sc.pump(rush=True)

    for f in range(4):
        l.got(*[("g", f, k) for k in range(1, 8)])
    for b in range(4):
        rows = pl.ds(256 * b, 256)
        low = flat(gpp[:, b])
        note(TOB, column_sums(low))
        low = low.astype(BF)
        act[rows, :] = low
        gh[rows, :] = dot(low, w[TO:TO + 768, :], NN).astype(BF)
    sc.pump(rush=True)
    here.wait("mixed2")
    weight_gradient(w.at[TO:TO + 768], act, 0, mixed)
    sc.ready.append(3)
    sc.pump(rush=True)
    here.wait("qkv2", "xp2")
    for b in range(4):
        rows = pl.ds(256 * b, 256)
        attend_block_back(b, qkv, gh, lse.at[0:48], lambda: tmask[...])
        n, scale = standardize(flat(places_b[:, b]))
        nb[rows, :] = (n * vec[TG:TG + 1, :] + vec[TS:TS + 1, :]).astype(BF)
        joined = qkv[rows, :]
        note(TIB, column_sums(joined[:, :768].astype(F32)))
        note(TIB + 1, column_sums(joined[:, 1536:].astype(F32)))
        e = dot(joined, w[TI:TI + 2304, :], NN)
        note(TG, column_sums(e * n))
        note(TS, column_sums(e))
        gb[:, b] = tiled(norm_back(e, vec[TG:TG + 1, :], n, scale))
        it[:, 4 * l.s + b] = gb[mine, b]
        for k in range(1, 8):
            peer = l.speer(k)
            l.sends(("h", b, k), gb.at[pl.ds(4 * peer, 4), b], it.at[:, 4 * l.s + b], peer)
        sc.pump(rush=True)
    for j in range(3):
        weight_gradient(w.at[TI + 768 * j:TI + 768 * (j + 1)], qkv, 768 * j, nb)
    sc.ready += [0, 1, 2]
    for i in range(3):
        vs.swap(i)
        sc.pump(rush=True)
        vs.join(i)
    vs.swapz()
    for b in range(4):
        l.got(*[("h", b, k) for k in range(1, 8)])
    for f in range(4):
        rows = pl.ds(256 * f, 256)
        final[rows, :] += flat(it[f])
    here.start("grad", final, grad_o)
    sc.pump(rush=True)
    vec[...] = vs.total()
    for s in range(8):
        @pl.when(l.s == s)
        def _():
            for r, o in ((TG, tg_o), (TS, ts_o), (TOB, tob_o), (TLB, tlb_o), (SG, sg_o), (SS, ss_o), (SOB, sob_o), (FG, fg_o),
                         (FS, fs_o), (FRB, frb_o)):
                o[...] = vec[r, 96 * s:96 * s + 96]
            for r, o in ((TIB, tib_o), (SIB, sib_o)):
                o[...] = vec[r + s // 4, 192 * (s % 4):192 * (s % 4) + 192]
            t, lane = FEB + 2 * (s % 2), 192 * (s // 2)
            feb_o[...] = jnp.concatenate([vec[t:t + 1, lane:lane + 192], vec[t + 1:t + 2, lane:lane + 192]], axis=1).reshape(384)
    sc.finish()
    l.drain()
    here.drain()


LIMIT = 63 << 20
VM = pl.BlockSpec(memory_space=pltpu.VMEM)
ANY = pl.BlockSpec(memory_space=pl.ANY)


def hand_over(*refs):
    for i in range(22):
        refs[22 + i][...] = refs[i][...]


def on_device_fast(
    tokens, cotangent, frame_clip, frame_valid, place_valid,
    time_gain, time_shift, time_inward, time_inward_bias, time_outward, time_outward_bias, time_linear, time_linear_bias,
    space_gain, space_shift, space_inward, space_inward_bias, space_outward, space_outward_bias,
    feed_gain, feed_shift, feed_expand, feed_expand_bias, feed_reduce, feed_reduce_bias,
):
    vectors = jnp.concatenate([
        time_gain, time_shift, time_outward_bias, time_linear_bias, space_gain, space_shift, space_outward_bias, feed_gain,
        feed_shift, feed_reduce_bias, time_inward_bias, space_inward_bias, feed_expand_bias])
    vin = jnp.pad(vectors.reshape(18, 96), ((0, 6), (0, 32)))
    shaped, vmem = jax.ShapeDtypeStruct, pltpu.VMEM
    rows_bf, rows_f32 = vmem((1024, 768), BF), vmem((1024, 768), F32)
    by_frame, by_place = vmem((4, 32, 8, 768), BF), vmem((32, 4, 8, 768), BF)
    row_block, selector = vmem((SLOTS, 96, 768), BF), vmem((192, 128), BF)
    n = CHUNKS * 20 + 14 + 28 + 56 + 6
    parameters = (
        time_gain, time_shift, time_inward, time_inward_bias, time_outward, time_outward_bias, time_linear, time_linear_bias,
        space_gain, space_shift, space_inward, space_inward_bias, space_outward, space_outward_bias,
        feed_gain, feed_shift, feed_expand, feed_expand_bias, feed_reduce, feed_reduce_bias)
    outs = pl.pallas_call(
        layer_kernel,
        out_shape=(shaped((1024, 768), BF), shaped((1024, 768), F32)) + tuple(shaped(p.shape, F32) for p in parameters) + (
            shaped((1024, 2304), BF), shaped((1024, 768), BF), shaped((1024, 768), BF), shaped((1024, 768), F32),
            shaped((32, 4, 8, 768), BF)),
        in_specs=[ANY, ANY] + [VM] * 11,
        out_specs=(ANY, ANY) + (VM,) * 20 + (ANY,) * 5,
        scratch_shapes=[
            vmem((WROWS, 768), BF), vmem((4, CHUNKS, 144, 128), BF), vmem((8, 24, 128), F32), vmem((24, 768), F32),
            selector, selector, selector, selector, vmem((256, 256), F32), vmem((4, 256, 1), F32),
            by_frame, by_frame, by_place, by_place, rows_bf, rows_bf, vmem((1024, 2304), BF), rows_f32, rows_f32, rows_f32,
            rows_bf, rows_bf, rows_bf,
            vmem((SLOTS, 4, 96, 768), BF), row_block, row_block, row_block, vmem((SLOTS, 4, 144, 128), BF),
            vmem((SLOTS, 3, 144, 128), BF), vmem((4, 24, 768), F32), vmem((7, 24, 768), F32), vmem((96, 256), F32),
            pltpu.SemaphoreType.DMA((24,)), pltpu.SemaphoreType.DMA((n,)), pltpu.SemaphoreType.DMA((n,))],
        compiler_params=pltpu.CompilerParams(collective_id=0, has_side_effects=True, vmem_limit_bytes=LIMIT),
    )(tokens.reshape(4, 32, 8, 768), cotangent.reshape(1024, 768), frame_clip.reshape(1, 32), frame_valid.reshape(1, 32),
      place_valid, vin, time_inward, time_outward, time_linear, space_inward, space_outward, feed_expand, feed_reduce)
    outs = pl.pallas_call(
        hand_over, out_shape=tuple(shaped(o.shape, o.dtype) for o in outs[:22]), in_specs=[VM] * 22, out_specs=(VM,) * 22,
        compiler_params=pltpu.CompilerParams(vmem_limit_bytes=32 << 20))(*outs[:22])
    return (outs[0].reshape(tokens.shape), outs[1].reshape(tokens.shape)) + tuple(outs[2:])


HEADS = 12


def normalize(inputs, scaling, offset):
    average = jnp.mean(inputs, axis=-1, keepdims=True)
    centered = inputs - average
    variance = jnp.mean(centered * centered, axis=-1, keepdims=True)
    return centered * lax.rsqrt(variance + EPSILON) * scaling + offset


def gelu_exact(inputs):
    return jax.nn.gelu(inputs, approximate=False)


def matmul(former, latter):
    return jnp.dot(former, latter, preferred_element_type=jnp.float32)


def inner(former, latter):
    return lax.dot_general(
        former, latter, (((0,), (0,)), ((), ())), preferred_element_type=jnp.float32
    )


def against(former, latter):
    return lax.dot_general(
        former, latter, (((1,), (1,)), ((), ())), preferred_element_type=jnp.float32
    )


def column_sum(delta_rows):
    return jnp.sum(delta_rows, axis=0, dtype=jnp.float32)


def packed_sum(joined_grad):
    totals = jnp.sum(joined_grad, axis=0, dtype=jnp.float32)
    model_width = totals.shape[0] // 3
    return jnp.concatenate([totals[:model_width], totals[2 * model_width :]])


def patterns(flavor):
    if flavor == "time":
        return ("fphd,gphd->phfg", "phfg,gphd->fphd", "phfg,fphd->gphd")
    return ("fphd,fqhd->fhpq", "fhpq,fqhd->fphd", "fhpq,fphd->fqhd")


def project_in_general(normed_low, weight, packed_bias, leading, head_count):
    model_width = normed_low.shape[-1]
    full_bias = jnp.concatenate(
        [
            packed_bias[:model_width],
            jnp.zeros((model_width,), jnp.float32),
            packed_bias[model_width:],
        ]
    )
    joined = (matmul(normed_low, weight) + full_bias).astype(jnp.bfloat16)
    shaped = joined.reshape(leading + (3, head_count, model_width // head_count))
    return (shaped[:, :, 0], shaped[:, :, 1], shaped[:, :, 2])


def attend(queries, keys_in, values, allowed, flavor):
    score_form, mix_form, spare_form = patterns(flavor)
    factor = queries.shape[-1] ** (-0.5)
    scores = jnp.einsum(score_form, queries, keys_in, preferred_element_type=jnp.float32) * factor
    masked = jnp.where(allowed, scores, -1e30)
    highest = jnp.max(masked, axis=-1, keepdims=True)
    raised = jnp.exp(masked - highest)
    summed = jnp.sum(raised, axis=-1, keepdims=True)
    chances = (raised / summed).astype(jnp.bfloat16)
    mixed = jnp.einsum(mix_form, chances, values, preferred_element_type=jnp.float32)
    return (mixed, highest + jnp.log(summed))


def attend_back(queries, keys_in, values, log_total, allowed, upstream, flavor):
    score_form, mix_form, spare_form = patterns(flavor)
    factor = queries.shape[-1] ** (-0.5)
    scores = jnp.einsum(score_form, queries, keys_in, preferred_element_type=jnp.float32) * factor
    chances = jnp.exp(jnp.where(allowed, scores, -1e30) - log_total)
    value_grad = jnp.einsum(
        spare_form, chances.astype(jnp.bfloat16), upstream, preferred_element_type=jnp.float32
    )
    chance_grad = jnp.einsum(score_form, upstream, values, preferred_element_type=jnp.float32)
    score_grad = (
        chances * (chance_grad - jnp.sum(chance_grad * chances, axis=-1, keepdims=True))
    ).astype(jnp.bfloat16)
    query_grad = (
        jnp.einsum(mix_form, score_grad, keys_in, preferred_element_type=jnp.float32) * factor
    )
    key_grad = (
        jnp.einsum(spare_form, score_grad, queries, preferred_element_type=jnp.float32) * factor
    )
    joined = jnp.stack([query_grad, key_grad, value_grad], axis=2)
    return joined.reshape(-1, 3 * joined.shape[-1] * joined.shape[-2]).astype(jnp.bfloat16)


def on_device_general(
    tokens,
    cotangent,
    frame_clip,
    frame_valid,
    place_valid,
    time_gain,
    time_shift,
    time_inward,
    time_inward_bias,
    time_outward,
    time_outward_bias,
    time_linear,
    time_linear_bias,
    space_gain,
    space_shift,
    space_inward,
    space_inward_bias,
    space_outward,
    space_outward_bias,
    feed_gain,
    feed_shift,
    feed_expand,
    feed_expand_bias,
    feed_reduce,
    feed_reduce_bias,
):
    frames_dev, places, model_width = tokens.shape
    head_count = HEADS
    group_frames = frame_clip.shape[0]
    clip_count = place_valid.shape[0]
    place_dev = places // lax.axis_size("seq")
    rows_part = (
        lax.all_gather(time_inward.astype(jnp.bfloat16), "grp", axis=0, tiled=True),
        lax.all_gather(time_outward.astype(jnp.bfloat16), "grp", axis=0, tiled=True),
        lax.all_gather(time_linear.astype(jnp.bfloat16), "grp", axis=0, tiled=True),
        lax.all_gather(space_inward.astype(jnp.bfloat16), "grp", axis=0, tiled=True),
        lax.all_gather(space_outward.astype(jnp.bfloat16), "grp", axis=0, tiled=True),
        lax.all_gather(feed_expand.astype(jnp.bfloat16), "grp", axis=0, tiled=True),
        lax.all_gather(feed_reduce.astype(jnp.bfloat16), "grp", axis=0, tiled=True),
    )
    gathered = (
        lax.all_gather(rows_part[0], "seq", axis=1, tiled=True),
        lax.all_gather(rows_part[1], "seq", axis=1, tiled=True),
        lax.all_gather(rows_part[2], "seq", axis=1, tiled=True),
        lax.all_gather(rows_part[3], "seq", axis=1, tiled=True),
        lax.all_gather(rows_part[4], "seq", axis=1, tiled=True),
        lax.all_gather(rows_part[5], "seq", axis=1, tiled=True),
        lax.all_gather(rows_part[6], "seq", axis=1, tiled=True),
        lax.all_gather(time_gain.astype(jnp.bfloat16), "seq", axis=0, tiled=True),
        lax.all_gather(time_shift.astype(jnp.bfloat16), "seq", axis=0, tiled=True),
        lax.all_gather(time_inward_bias.astype(jnp.bfloat16), "seq", axis=0, tiled=True),
        lax.all_gather(time_outward_bias.astype(jnp.bfloat16), "seq", axis=0, tiled=True),
        lax.all_gather(time_linear_bias.astype(jnp.bfloat16), "seq", axis=0, tiled=True),
        lax.all_gather(space_gain.astype(jnp.bfloat16), "seq", axis=0, tiled=True),
        lax.all_gather(space_shift.astype(jnp.bfloat16), "seq", axis=0, tiled=True),
        lax.all_gather(space_inward_bias.astype(jnp.bfloat16), "seq", axis=0, tiled=True),
        lax.all_gather(space_outward_bias.astype(jnp.bfloat16), "seq", axis=0, tiled=True),
        lax.all_gather(feed_gain.astype(jnp.bfloat16), "seq", axis=0, tiled=True),
        lax.all_gather(feed_shift.astype(jnp.bfloat16), "seq", axis=0, tiled=True),
        lax.all_gather(feed_expand_bias.astype(jnp.bfloat16), "seq", axis=0, tiled=True),
        lax.all_gather(feed_reduce_bias.astype(jnp.bfloat16), "seq", axis=0, tiled=True),
    )
    own_slot = lax.axis_index("seq")
    own_clips = lax.dynamic_slice_in_dim(frame_clip, own_slot * frames_dev, frames_dev) % clip_count
    matches = own_clips[:, None] == jnp.arange(clip_count, dtype=jnp.int32)[None, :]
    key_places = jnp.sum(jnp.where(matches[:, :, None], place_valid[None, :, :], 0), axis=1)
    space_allowed = (key_places == 1)[:, None, None, :]
    time_allowed = ((frame_clip[:, None] == frame_clip[None, :]) & (frame_valid[None, :] == 1))[
        None, None
    ]
    placed = lax.all_to_all(tokens, "seq", split_axis=1, concat_axis=0, tiled=True)
    placed_rows = placed.reshape(-1, model_width).astype(jnp.float32)
    time_normed_wide, time_norm_pull = jax.vjp(
        normalize,
        placed_rows,
        gathered[7].astype(jnp.float32),
        gathered[8].astype(jnp.float32),
    )
    time_normed = time_normed_wide.astype(jnp.bfloat16)
    time_parts = project_in_general(
        time_normed,
        gathered[0],
        gathered[9].astype(jnp.float32),
        (group_frames, place_dev),
        head_count,
    )
    time_mixed, time_total = attend(
        time_parts[0], time_parts[1], time_parts[2], time_allowed, "time"
    )
    time_mixed_low = time_mixed.reshape(-1, model_width).astype(jnp.bfloat16)
    time_proj = (
        matmul(time_mixed_low, gathered[1]) + gathered[10].astype(jnp.float32)
    ).astype(jnp.bfloat16)
    returned = lax.all_to_all(
        time_proj.reshape(group_frames, place_dev, model_width),
        "seq",
        split_axis=0,
        concat_axis=1,
        tiled=True,
    )
    returned_rows = returned.reshape(-1, model_width)
    first_sum = (
        tokens.reshape(-1, model_width).astype(jnp.float32)
        + matmul(returned_rows, gathered[2])
        + gathered[11].astype(jnp.float32)
    )
    space_normed_wide, space_norm_pull = jax.vjp(
        normalize,
        first_sum,
        gathered[12].astype(jnp.float32),
        gathered[13].astype(jnp.float32),
    )
    space_normed = space_normed_wide.astype(jnp.bfloat16)
    space_parts = project_in_general(
        space_normed,
        gathered[3],
        gathered[14].astype(jnp.float32),
        (frames_dev, places),
        head_count,
    )
    space_mixed, space_total = attend(
        space_parts[0], space_parts[1], space_parts[2], space_allowed, "space"
    )
    space_mixed_low = space_mixed.reshape(-1, model_width).astype(jnp.bfloat16)
    second_sum = (
        first_sum
        + matmul(space_mixed_low, gathered[4])
        + gathered[15].astype(jnp.float32)
    )
    feed_normed_wide, feed_norm_pull = jax.vjp(
        normalize,
        second_sum,
        gathered[16].astype(jnp.float32),
        gathered[17].astype(jnp.float32),
    )
    feed_normed = feed_normed_wide.astype(jnp.bfloat16)
    hidden = matmul(feed_normed, gathered[5]) + gathered[18].astype(jnp.float32)
    activated_wide, gelu_pull = jax.vjp(gelu_exact, hidden)
    activated = activated_wide.astype(jnp.bfloat16)
    final_sum = (
        second_sum
        + matmul(activated, gathered[6])
        + gathered[19].astype(jnp.float32)
    )
    result = final_sum.astype(jnp.bfloat16).reshape(tokens.shape)
    rows_again = (
        lax.all_gather(time_inward.astype(jnp.bfloat16), "grp", axis=0, tiled=True),
        lax.all_gather(time_outward.astype(jnp.bfloat16), "grp", axis=0, tiled=True),
        lax.all_gather(time_linear.astype(jnp.bfloat16), "grp", axis=0, tiled=True),
        lax.all_gather(space_inward.astype(jnp.bfloat16), "grp", axis=0, tiled=True),
        lax.all_gather(space_outward.astype(jnp.bfloat16), "grp", axis=0, tiled=True),
        lax.all_gather(feed_expand.astype(jnp.bfloat16), "grp", axis=0, tiled=True),
        lax.all_gather(feed_reduce.astype(jnp.bfloat16), "grp", axis=0, tiled=True),
    )
    gathered_again = (
        lax.all_gather(rows_again[0], "seq", axis=1, tiled=True),
        lax.all_gather(rows_again[1], "seq", axis=1, tiled=True),
        lax.all_gather(rows_again[2], "seq", axis=1, tiled=True),
        lax.all_gather(rows_again[3], "seq", axis=1, tiled=True),
        lax.all_gather(rows_again[4], "seq", axis=1, tiled=True),
        lax.all_gather(rows_again[5], "seq", axis=1, tiled=True),
        lax.all_gather(rows_again[6], "seq", axis=1, tiled=True),
        lax.all_gather(time_gain.astype(jnp.bfloat16), "seq", axis=0, tiled=True),
        lax.all_gather(time_shift.astype(jnp.bfloat16), "seq", axis=0, tiled=True),
        lax.all_gather(time_inward_bias.astype(jnp.bfloat16), "seq", axis=0, tiled=True),
        lax.all_gather(time_outward_bias.astype(jnp.bfloat16), "seq", axis=0, tiled=True),
        lax.all_gather(time_linear_bias.astype(jnp.bfloat16), "seq", axis=0, tiled=True),
        lax.all_gather(space_gain.astype(jnp.bfloat16), "seq", axis=0, tiled=True),
        lax.all_gather(space_shift.astype(jnp.bfloat16), "seq", axis=0, tiled=True),
        lax.all_gather(space_inward_bias.astype(jnp.bfloat16), "seq", axis=0, tiled=True),
        lax.all_gather(space_outward_bias.astype(jnp.bfloat16), "seq", axis=0, tiled=True),
        lax.all_gather(feed_gain.astype(jnp.bfloat16), "seq", axis=0, tiled=True),
        lax.all_gather(feed_shift.astype(jnp.bfloat16), "seq", axis=0, tiled=True),
        lax.all_gather(feed_expand_bias.astype(jnp.bfloat16), "seq", axis=0, tiled=True),
        lax.all_gather(feed_reduce_bias.astype(jnp.bfloat16), "seq", axis=0, tiled=True),
    )
    upstream = cotangent.reshape(-1, model_width).astype(jnp.float32)
    feed_delta = cotangent.reshape(-1, model_width)
    gradient_feed_reduce = inner(activated, feed_delta)
    gradient_feed_reduce_bias = column_sum(feed_delta)
    (hidden_wide,) = gelu_pull(against(feed_delta, gathered_again[6]))
    hidden_delta = hidden_wide.astype(jnp.bfloat16)
    gradient_feed_expand = inner(feed_normed, hidden_delta)
    gradient_feed_expand_bias = column_sum(hidden_delta)
    second_back, gradient_feed_gain, gradient_feed_shift = feed_norm_pull(
        against(hidden_delta, gathered_again[5])
    )
    second_delta = upstream + second_back
    space_delta = second_delta.astype(jnp.bfloat16)
    gradient_space_outward = inner(space_mixed_low, space_delta)
    gradient_space_outward_bias = column_sum(space_delta)
    space_mixed_delta = against(space_delta, gathered_again[4]).astype(jnp.bfloat16)
    space_mixed_delta = space_mixed_delta.reshape(frames_dev, places, head_count, -1)
    space_joined = attend_back(
        space_parts[0],
        space_parts[1],
        space_parts[2],
        space_total,
        space_allowed,
        space_mixed_delta,
        "space",
    )
    gradient_space_inward = inner(space_normed, space_joined)
    gradient_space_inward_bias = packed_sum(space_joined)
    first_back, gradient_space_gain, gradient_space_shift = space_norm_pull(
        against(space_joined, gathered_again[3])
    )
    first_delta = second_delta + first_back
    linear_delta = first_delta.astype(jnp.bfloat16)
    gradient_time_linear = inner(returned_rows, linear_delta)
    gradient_time_linear_bias = column_sum(linear_delta)
    proj_delta = against(linear_delta, gathered_again[2]).astype(jnp.bfloat16)
    proj_placed = lax.all_to_all(
        proj_delta.reshape(frames_dev, places, model_width),
        "seq",
        split_axis=1,
        concat_axis=0,
        tiled=True,
    )
    proj_rows = proj_placed.reshape(-1, model_width)
    gradient_time_outward = inner(time_mixed_low, proj_rows)
    gradient_time_outward_bias = column_sum(proj_rows)
    time_mixed_delta = against(proj_rows, gathered_again[1]).astype(jnp.bfloat16)
    time_mixed_delta = time_mixed_delta.reshape(group_frames, place_dev, head_count, -1)
    time_joined = attend_back(
        time_parts[0],
        time_parts[1],
        time_parts[2],
        time_total,
        time_allowed,
        time_mixed_delta,
        "time",
    )
    gradient_time_inward = inner(time_normed, time_joined)
    gradient_time_inward_bias = packed_sum(time_joined)
    placed_back, gradient_time_gain, gradient_time_shift = time_norm_pull(
        against(time_joined, gathered_again[0])
    )
    framed_back = lax.all_to_all(
        placed_back.reshape(group_frames, place_dev, model_width).astype(jnp.bfloat16),
        "seq",
        split_axis=0,
        concat_axis=1,
        tiled=True,
    ).astype(jnp.float32)
    input_gradient = (first_delta + framed_back.reshape(-1, model_width)).reshape(tokens.shape)
    matrix_terms = (
        gradient_time_inward,
        gradient_time_outward,
        gradient_time_linear,
        gradient_space_inward,
        gradient_space_outward,
        gradient_feed_expand,
        gradient_feed_reduce,
    )
    vector_terms = (
        gradient_time_gain,
        gradient_time_shift,
        gradient_time_inward_bias,
        gradient_time_outward_bias,
        gradient_time_linear_bias,
        gradient_space_gain,
        gradient_space_shift,
        gradient_space_inward_bias,
        gradient_space_outward_bias,
        gradient_feed_gain,
        gradient_feed_shift,
        gradient_feed_expand_bias,
        gradient_feed_reduce_bias,
    )
    columns_summed = (
        lax.psum_scatter(
            matrix_terms[0].astype(jnp.bfloat16), "seq", scatter_dimension=1, tiled=True
        ).astype(jnp.float32),
        lax.psum_scatter(
            matrix_terms[1].astype(jnp.bfloat16), "seq", scatter_dimension=1, tiled=True
        ).astype(jnp.float32),
        lax.psum_scatter(
            matrix_terms[2].astype(jnp.bfloat16), "seq", scatter_dimension=1, tiled=True
        ).astype(jnp.float32),
        lax.psum_scatter(
            matrix_terms[3].astype(jnp.bfloat16), "seq", scatter_dimension=1, tiled=True
        ).astype(jnp.float32),
        lax.psum_scatter(
            matrix_terms[4].astype(jnp.bfloat16), "seq", scatter_dimension=1, tiled=True
        ).astype(jnp.float32),
        lax.psum_scatter(
            matrix_terms[5].astype(jnp.bfloat16), "seq", scatter_dimension=1, tiled=True
        ).astype(jnp.float32),
        lax.psum_scatter(
            matrix_terms[6].astype(jnp.bfloat16), "seq", scatter_dimension=1, tiled=True
        ).astype(jnp.float32),
        lax.psum_scatter(
            vector_terms[0].astype(jnp.bfloat16), "seq", scatter_dimension=0, tiled=True
        ).astype(jnp.float32),
        lax.psum_scatter(
            vector_terms[1].astype(jnp.bfloat16), "seq", scatter_dimension=0, tiled=True
        ).astype(jnp.float32),
        lax.psum_scatter(
            vector_terms[2].astype(jnp.bfloat16), "seq", scatter_dimension=0, tiled=True
        ).astype(jnp.float32),
        lax.psum_scatter(
            vector_terms[3].astype(jnp.bfloat16), "seq", scatter_dimension=0, tiled=True
        ).astype(jnp.float32),
        lax.psum_scatter(
            vector_terms[4].astype(jnp.bfloat16), "seq", scatter_dimension=0, tiled=True
        ).astype(jnp.float32),
        lax.psum_scatter(
            vector_terms[5].astype(jnp.bfloat16), "seq", scatter_dimension=0, tiled=True
        ).astype(jnp.float32),
        lax.psum_scatter(
            vector_terms[6].astype(jnp.bfloat16), "seq", scatter_dimension=0, tiled=True
        ).astype(jnp.float32),
        lax.psum_scatter(
            vector_terms[7].astype(jnp.bfloat16), "seq", scatter_dimension=0, tiled=True
        ).astype(jnp.float32),
        lax.psum_scatter(
            vector_terms[8].astype(jnp.bfloat16), "seq", scatter_dimension=0, tiled=True
        ).astype(jnp.float32),
        lax.psum_scatter(
            vector_terms[9].astype(jnp.bfloat16), "seq", scatter_dimension=0, tiled=True
        ).astype(jnp.float32),
        lax.psum_scatter(
            vector_terms[10].astype(jnp.bfloat16), "seq", scatter_dimension=0, tiled=True
        ).astype(jnp.float32),
        lax.psum_scatter(
            vector_terms[11].astype(jnp.bfloat16), "seq", scatter_dimension=0, tiled=True
        ).astype(jnp.float32),
        lax.psum_scatter(
            vector_terms[12].astype(jnp.bfloat16), "seq", scatter_dimension=0, tiled=True
        ).astype(jnp.float32),
    )
    rows_summed = (
        lax.psum_scatter(
            columns_summed[0].astype(jnp.bfloat16), "grp", scatter_dimension=0, tiled=True
        ).astype(jnp.float32),
        lax.psum_scatter(
            columns_summed[1].astype(jnp.bfloat16), "grp", scatter_dimension=0, tiled=True
        ).astype(jnp.float32),
        lax.psum_scatter(
            columns_summed[2].astype(jnp.bfloat16), "grp", scatter_dimension=0, tiled=True
        ).astype(jnp.float32),
        lax.psum_scatter(
            columns_summed[3].astype(jnp.bfloat16), "grp", scatter_dimension=0, tiled=True
        ).astype(jnp.float32),
        lax.psum_scatter(
            columns_summed[4].astype(jnp.bfloat16), "grp", scatter_dimension=0, tiled=True
        ).astype(jnp.float32),
        lax.psum_scatter(
            columns_summed[5].astype(jnp.bfloat16), "grp", scatter_dimension=0, tiled=True
        ).astype(jnp.float32),
        lax.psum_scatter(
            columns_summed[6].astype(jnp.bfloat16), "grp", scatter_dimension=0, tiled=True
        ).astype(jnp.float32),
    )
    vector_shares = tuple(columns_summed[7:])
    vectors_summed = lax.psum(
        (
            vector_shares[0],
            vector_shares[1],
            vector_shares[2],
            vector_shares[3],
            vector_shares[4],
            vector_shares[5],
            vector_shares[6],
            vector_shares[7],
            vector_shares[8],
            vector_shares[9],
            vector_shares[10],
            vector_shares[11],
            vector_shares[12],
        ),
        "grp",
    )
    owned = tuple(rows_summed) + tuple(vectors_summed)
    return (result, input_gradient) + tuple(owned[i] for i in (7, 8, 0, 9, 1, 10, 2, 11, 12, 13, 3, 14, 4, 15, 16, 17, 5, 18, 6, 19))


def solution(mesh):
    fast = mesh.shape["grp"] == 4 and mesh.shape["seq"] == 8
    return jax.shard_map(
        on_device_fast if fast else on_device_general,
        mesh=mesh,
        in_specs=(
            P(("grp", "seq"), None, None),
            P(("grp", "seq"), None, None),
            P("grp"),
            P("grp"),
            P("grp", None),
            P("seq"),
            P("seq"),
            P("grp", "seq"),
            P("seq"),
            P("grp", "seq"),
            P("seq"),
            P("grp", "seq"),
            P("seq"),
            P("seq"),
            P("seq"),
            P("grp", "seq"),
            P("seq"),
            P("grp", "seq"),
            P("seq"),
            P("seq"),
            P("seq"),
            P("grp", "seq"),
            P("seq"),
            P("grp", "seq"),
            P("seq"),
        ),
        out_specs=(
            P(("grp", "seq"), None, None),
            P(("grp", "seq"), None, None),
            P("seq"),
            P("seq"),
            P("grp", "seq"),
            P("seq"),
            P("grp", "seq"),
            P("seq"),
            P("grp", "seq"),
            P("seq"),
            P("seq"),
            P("seq"),
            P("grp", "seq"),
            P("seq"),
            P("grp", "seq"),
            P("seq"),
            P("seq"),
            P("seq"),
            P("grp", "seq"),
            P("seq"),
            P("grp", "seq"),
            P("seq"),
        ),
        check_vma=False,
    )
```

```python
import jax
import jax.numpy as jnp
from jax import lax
from jax.experimental import pallas as pl
from jax.experimental.pallas import tpu as pltpu
from jax.sharding import PartitionSpec as P

MESH = pl.DeviceIdType.MESH
BF = jnp.bfloat16
F32 = jnp.float32
NN = (((1,), (0,)), ((), ()))
NT = (((1,), (1,)), ((), ()))
TN = (((0,), (0,)), ((), ()))

TI, TO, TL, SI, SO, FE, FR = 0, 2304, 3072, 3840, 6144, 6912, 9984
WROWS = 13056
BASE = ([96 * t for t in range(3)] + [TO, TL] + [SI + 96 * t for t in range(3)] + [SO]
        + [FE + 768 * (v // 2) + 96 * (v % 2) for v in range(4)] + [FR + 768 * t for t in range(4)])
PAIR = [576] * 3 + [192] * 2 + [576] * 3 + [192] + [192] * 4 + [192] * 4
CORE = [288] * 3 + [96] * 2 + [288] * 3 + [96] + [1536] * 4 + [96] * 4
CHUNKS = 17
GATHER_ORDER = [0, 1, 2, 3, 4, 5, 6, 7, 8, 9, 10, 13, 15, 11, 12, 14, 16]
SLOTS = 5
LAGS = (2, 3, 3, 3)
GATHER_LAGS = (2, 3, 2)
SPACING = 2
KINDS = ("p", "q", "so", "d", "sp", "sq", "sd")
EPSILON = 1e-06


def dot(a, b, dims):
    return lax.dot_general(a, b, dims, preferred_element_type=F32)


class Links:
    def __init__(self, send_sem, recv_sem):
        self.send_sem, self.recv_sem = send_sem, recv_sem
        self.copies, self.used, self.sent = {}, 0, set()
        self.z = lax.axis_index("grp")
        s = self.s = lax.axis_index("seq")
        core, x, y = s % 2, (s // 2) % 2, s // 4
        xn, yn = s + 2 - 4 * x, s + 4 - 8 * y
        self.core = core
        self.sib = s + 1 - 2 * core
        self.p = yn * (1 - core) + xn * core
        self.q = xn * (1 - core) + yn * core
        self.d = xn + yn - s

    def zpeer(self, k):
        return (self.z + k) % 4

    def speer(self, k):
        return (self.s + k) % 8

    def greet(self):
        bar = pltpu.get_barrier_semaphore()
        for k in range(1, 8):
            pl.semaphore_signal(bar, inc=1, device_id=(self.z, self.speer(k)), device_id_type=MESH)
        for k in range(1, 4):
            pl.semaphore_signal(bar, inc=1, device_id=(self.zpeer(k), self.s), device_id_type=MESH)

    def greeted(self):
        pl.semaphore_wait(pltpu.get_barrier_semaphore(), 10)

    def send(self, key, src, dst, device):
        i = self.used
        self.used += 1
        copy = pltpu.make_async_remote_copy(
            src_ref=src, dst_ref=dst, send_sem=self.send_sem.at[i], recv_sem=self.recv_sem.at[i],
            device_id=device, device_id_type=MESH)
        copy.start()
        self.copies[key] = copy

    def sends(self, key, src, dst, seq):
        self.send(key, src, dst, (self.z, seq))

    def sendz(self, key, src, dst, z):
        self.send(key, src, dst, (z, self.s))

    def got(self, *keys):
        for key in keys:
            self.copies[key].wait_recv()

    def gone(self, *keys):
        for key in keys:
            if key not in self.sent:
                self.sent.add(key)
                self.copies[key].wait_send()

    def drain(self):
        self.gone(*self.copies)


class Local:
    def __init__(self, sem):
        self.sem, self.used, self.copies = sem, 0, {}

    def start(self, key, src, dst):
        copy = pltpu.make_async_copy(src, dst, self.sem.at[self.used])
        self.used += 1
        copy.start()
        self.copies[key] = copy

    def wait(self, *keys):
        for key in keys:
            copy = self.copies.pop(key, None)
            if copy is not None:
                copy.wait()

    def drain(self):
        self.wait(*list(self.copies))


def place(c, s):
    return pl.ds(pl.multiple_of(BASE[c] + PAIR[c] * (s // 2) + CORE[c] * (s % 2), 32), 96)


def block(ref, c, s):
    return ref.at[place(c, s)]


class Gather:
    def __init__(self, links, zst, w):
        self.l, self.zst, self.w = links, zst, w
        self.next, self.flight, self.zsent, self.clock = 0, [], 0, 0

    def zsend(self, count=1):
        for i in range(self.zsent, min(self.zsent + count, CHUNKS)):
            c = GATHER_ORDER[i]
            own = self.zst.at[self.l.z, c]
            for k in range(1, 4):
                self.l.sendz(("zg", c, k), own, own, self.l.zpeer(k))
            self.zsent += 1

    def sources(self, *chunks):
        self.l.gone(*[(k, c) for c in chunks for k in KINDS])

    def step_a(self, i, c):
        l = self.l
        l.got(*[("zg", c, k) for k in range(1, 4)])
        rows = place(c, l.s)
        zst, w = self.zst, self.w
        for half in range(2):
            lo, hi = zst[2 * half, c], zst[2 * half + 1, c]
            w[rows, 384 * half:384 * half + 128] = lo[:96]
            w[rows, 384 * half + 256:384 * half + 384] = hi[:96]
            blo, bhi = lo[96:], hi[96:]
            w[rows, 384 * half + 128:384 * half + 256] = jnp.concatenate([
                jnp.concatenate([blo[:, :64], bhi[:, :64]], axis=1),
                jnp.concatenate([blo[:, 64:], bhi[:, 64:]], axis=1)], axis=0)
        own = block(w, c, l.s)
        l.sends(("p", c), own, own, l.p)
        l.sends(("q", c), own, own, l.q)
        l.sends(("so", c), own, own, l.sib)
        self.zsend()

    def step_b(self, i, c):
        l = self.l
        l.got(("p", c))
        bp = block(self.w, c, l.p)
        l.sends(("d", c), bp, bp, l.q)
        l.sends(("sp", c), bp, bp, l.sib)
        l.got(("q", c))
        bq = block(self.w, c, l.q)
        l.sends(("sq", c), bq, bq, l.sib)

    def step_c(self, i, c):
        l = self.l
        l.got(("d", c))
        bd = block(self.w, c, l.d)
        l.sends(("sd", c), bd, bd, l.sib)

    def step_d(self, i, c):
        self.l.got(("so", c), ("sp", c), ("sq", c), ("sd", c))

    def tick(self, push=True, whole=-1):
        steps = (self.step_b, self.step_c, self.step_d)
        self.clock += 1
        fresh = []
        if push and self.next < CHUNKS:
            self.step_a(self.next, GATHER_ORDER[self.next])
            fresh = [(self.next, 0, self.clock + GATHER_LAGS[0])]
            self.next += 1
        later = []
        for i, k, due in self.flight:
            if i <= whole or self.clock >= due:
                steps[k](i, GATHER_ORDER[i])
                k, due = k + 1, self.clock + (GATHER_LAGS + (0,))[k + 1]
            if k < 3:
                later.append((i, k, due))
        self.flight = later + fresh

    def until(self, chunk):
        i = GATHER_ORDER.index(chunk)
        while i >= self.next or any(j <= i for j, _, _ in self.flight):
            self.tick(push=self.next <= i, whole=i)

    @property
    def done(self):
        return self.next == CHUNKS and not self.flight


class Scatter:
    def __init__(self, links, local, g, sr, fr, ar, br, zp, zr, ob, out):
        self.l, self.local, self.g, self.sr, self.fr, self.ar, self.br = links, local, g, sr, fr, ar, br
        self.zp, self.zr, self.ob, self.out = zp, zr, ob, out
        self.ready, self.flight, self.order = [], [], []
        self.clock, self.pushed = 0, -9

    def step_a(self, i, c):
        l = self.l
        for j in range(4):
            l.sends(("s", c, j), block(self.g, c, 2 * j + 1 - l.core), self.sr.at[i % SLOTS, j], l.sib)

    def add(self, c, s, other):
        rows = place(c, s)
        self.g[rows, :] = (self.g[rows, :].astype(F32) + other.astype(F32)).astype(BF)

    def step_b(self, i, c):
        l, k = self.l, i % SLOTS
        l.got(*[("s", c, j) for j in range(4)])
        for s, j in ((l.d, l.d // 2), (l.p, l.p // 2), (l.q, l.q // 2), (l.s, l.s // 2)):
            self.add(c, s, self.sr[k, j])
            if s is l.d:
                l.sends(("f", c), block(self.g, c, l.d), self.fr.at[k], l.p)
            if s is l.p:
                l.sends(("a", c), block(self.g, c, l.p), self.ar.at[k], l.p)

    def step_c(self, i, c):
        l, k = self.l, i % SLOTS
        l.got(("f", c))
        self.add(c, l.q, self.fr[k])
        l.sends(("b", c), block(self.g, c, l.q), self.br.at[k], l.q)

    def step_d(self, i, c):
        l, k = self.l, i % SLOTS
        l.got(("a", c), ("b", c))
        rows = place(c, l.s)
        total = self.g[rows, :].astype(F32) + self.ar[k].astype(F32) + self.br[k].astype(F32)
        if i >= SLOTS:
            l.gone(*[("z", self.order[i - SLOTS], j) for j in range(1, 4)])
        zp = self.zp
        for half in range(2):
            lane = 384 * half
            zp[k, 2 * half, 0:96] = total[:, lane:lane + 128].astype(BF)
            zp[k, 2 * half + 1, 0:96] = total[:, lane + 256:lane + 384].astype(BF)
            mid = total[:, lane + 128:lane + 256]
            top, low = mid[:48], mid[48:]
            zp[k, 2 * half, 96:144] = jnp.concatenate([top[:, :64], low[:, :64]], axis=1).astype(BF)
            zp[k, 2 * half + 1, 96:144] = jnp.concatenate([top[:, 64:], low[:, 64:]], axis=1).astype(BF)
        for j in range(1, 4):
            z = l.zpeer(j)
            l.sendz(("z", c, j), zp.at[k, z], self.zr.at[k, j - 1], z)

    def step_e(self, i, c):
        l, k = self.l, i % SLOTS
        l.got(*[("z", c, j) for j in range(1, 4)])
        total = self.zp[k, l.z].astype(F32)
        for j in range(3):
            total += self.zr[k, j].astype(F32)
        if i >= SLOTS:
            self.local.wait(("o", self.order[i - SLOTS]))
        self.ob[k] = total
        self.local.start(("o", c), self.ob.at[k], self.out.at[c])

    def pump(self, rush=False):
        steps = (self.step_b, self.step_c, self.step_d, self.step_e)
        self.clock += 1
        fresh = []
        if self.ready and (rush or self.clock >= self.pushed + SPACING):
            c = self.ready.pop(0)
            i = len(self.order)
            self.order.append(c)
            self.step_a(i, c)
            self.pushed = self.clock
            fresh = [(i, 0, self.clock + LAGS[0])]
        later = []
        for i, k, due in self.flight:
            if rush or self.clock >= due:
                steps[k](i, self.order[i])
                k, due = k + 1, self.clock + (LAGS + (0,))[k + 1]
            if k < 4:
                later.append((i, k, due))
        self.flight = later + fresh

    def finish(self):
        while self.ready or self.flight:
            self.pump(rush=True)


class VectorSum:
    def __init__(self, links, gv, vb):
        self.l, self.gv, self.vb = links, gv, vb

    def swap(self, i):
        l = self.l
        l.sends(("vs", i), self.gv.at[i], self.vb.at[i], (l.sib, l.p, l.q)[i])

    def join(self, i):
        self.l.got(("vs", i))
        self.gv[i + 1] = self.gv[i] + self.vb[i]

    def swapz(self):
        l = self.l
        self.vb[3 + l.z] = self.gv[3]
        for k in range(1, 4):
            l.sendz(("vz", k), self.gv.at[3], self.vb.at[3 + l.z], l.zpeer(k))

    def total(self):
        self.l.got(*[("vz", k) for k in range(1, 4)])
        return (self.vb[3] + self.vb[4]) + (self.vb[5] + self.vb[6])


TG, TS, TOB, TLB, SG, SS, SOB, FG, FS, FRB, TIB, SIB, FEB = 0, 1, 2, 3, 4, 5, 6, 7, 8, 9, 10, 12, 14


def assemble_vectors(vg, vec):
    vec[...] = jnp.zeros(vec.shape, F32)
    for s in range(8):
        piece = vg[s]
        vec[0:10, 96 * s:96 * s + 96] = piece[0:10, 0:96]
        for a in range(2):
            i = 2 * s + a
            for r in (TIB, SIB):
                vec[r + i // 8:r + i // 8 + 1, 96 * (i % 8):96 * (i % 8) + 96] = piece[r + a:r + a + 1, 0:96]
        for a in range(4):
            t, lane = 2 * (s % 2) + a // 2, 192 * (s // 2) + 96 * (a % 2)
            vec[FEB + t:FEB + 1 + t, lane:lane + 96] = piece[FEB + a:FEB + 1 + a, 0:96]


def selectors(odd, ea, el, eh):
    m = lax.broadcasted_iota(jnp.int32, (192, 128), 0)
    c = lax.broadcasted_iota(jnp.int32, (192, 128), 1)
    whole, folded = c + 64 * odd, c % 64 + 128 * (1 - odd)
    ea[...] = jnp.where(m == whole, 1.0, 0.0).astype(BF)
    both = jnp.where(m == folded, 1.0, 0.0)
    el[...] = jnp.where(c < 64, both, 0.0).astype(BF)
    eh[...] = jnp.where(c < 64, 0.0, both).astype(BF)


def standardize(x):
    centered = x - jnp.mean(x, axis=-1, keepdims=True)
    scale = lax.rsqrt(jnp.mean(centered * centered, axis=-1, keepdims=True) + EPSILON)
    return centered * scale, scale


def norm_back(e, gain, n, scale):
    u = e * gain
    return scale * (u - jnp.mean(u, axis=-1, keepdims=True) - n * jnp.mean(u * n, axis=-1, keepdims=True))


def column_sums(x):
    return jnp.sum(x, axis=0, keepdims=True)


def head_masks(scale):
    lane = lax.broadcasted_iota(jnp.int32, (1, 128), 1)
    return [jnp.where(lane < 64, scale, 0.0).astype(BF), jnp.where(lane < 64, 0.0, scale).astype(BF)]


def pair_columns(qkv, rows, p):
    c = pl.multiple_of(p * 128, 128)
    return [qkv[rows, pl.ds(768 * j + c, 128)] for j in range(3)]


def attend_block(b, qkv, mixed, lse, bias):
    rows = pl.ds(b * 256, 256)

    def pair(p):
        q, k, v = pair_columns(qkv, rows, p)
        scaled, plain = head_masks(0.125), head_masks(1.0)
        out = None
        for h in range(2):
            s = dot(k * scaled[h], q, NT) + bias()
            m = jnp.max(s, axis=0, keepdims=True)
            e = jnp.exp(s - m)
            total = jnp.sum(e, axis=0, keepdims=True)
            lse[pl.ds(b * 12 + p * 2 + h, 1), :] = m + jnp.log(total)
            o = dot((e * (1.0 / total)).astype(BF), v * plain[h], TN)
            out = o if out is None else out + o
        mixed[rows, pl.ds(pl.multiple_of(p * 128, 128), 128)] = out.astype(BF)

    def body(i, _):
        pair(2 * i)
        pair(2 * i + 1)
        return 0

    lax.fori_loop(0, 3, body, 0)


def attend_block_back(b, qkv, gm, lse, bias):
    rows = pl.ds(b * 256, 256)

    def pair(p):
        q, k, v = pair_columns(qkv, rows, p)
        c = pl.multiple_of(p * 128, 128)
        g = gm[rows, pl.ds(c, 128)]
        scaled, plain = head_masks(0.125), head_masks(1.0)
        sums = [None, None, None]
        for h in range(2):
            kh, vh, qh, gh = k * scaled[h], v * plain[h], q * scaled[h], g * plain[h]
            s = dot(kh, q, NT) + bias()
            chances = jnp.exp(s - lse[pl.ds(b * 12 + p * 2 + h, 1), :])
            back = dot(vh, g, NT)
            mean = jnp.sum(chances * back, axis=0, keepdims=True)
            gs = (chances * (back - mean)).astype(BF)
            for j, term in enumerate((dot(gs, kh, TN), dot(gs, qh, NN), dot(chances.astype(BF), gh, NN))):
                sums[j] = term if sums[j] is None else sums[j] + term
        for j in range(3):
            qkv[rows, pl.ds(768 * j + c, 128)] = sums[j].astype(BF)

    def body(i, _):
        pair(2 * i)
        pair(2 * i + 1)
        return 0

    lax.fori_loop(0, 3, body, 0)


def project_in(normed, w, at, qkv, rows, vec, bias_row):
    for j in range(3):
        part = dot(normed, w[at + 768 * j:at + 768 * (j + 1), :], NT)
        if j != 1:
            r = bias_row + j // 2
            part = part + vec[r:r + 1, :]
        qkv[rows, 768 * j:768 * (j + 1)] = part.astype(BF)


def weight_gradient(out, delta, column, rows):
    for m in range(3):
        lane = column + 256 * m
        out[256 * m:256 * m + 256, :] = dot(delta[:, lane:lane + 256], rows[...], TN).astype(BF)


def flat(x):
    return x.astype(F32).reshape(256, 768)


def tiled(x):
    return x.reshape(32, 8, 768).astype(BF)


def layer_kernel(
    tokens, cot_i, clip_i, valid_i, place_i, vin, ti_i, to_i, tl_i, si_i, so_i, fe_i, fr_i,
    result_o, grad_o, packed_o, total_o, tqkv_o, tmixed_o, ret_o, first_o, xp_o,
    w, zst, vg, vec, ea, el, eh, tmask, smask, frames_a, frames_b, places_a, places_b, nb, mixed, qkv, f1, f2, f3, act, gh, g,
    sr, fr, ar, br, zp, zr, ob, gv, vb, lse, local_sem, send_sem, recv_sem,
):
    l = Links(send_sem, recv_sem)
    l.greet()
    here = Local(local_sem)
    mine = pl.ds(4 * l.s, 4)
    xp, gpp = places_a, places_a
    pr, gb = places_b, places_b
    ret, it = frames_a, frames_a
    x, gp = frames_b, frames_b
    here.start("x", tokens, x)
    here.start("xp", tokens.at[:, mine], xp.at[mine])
    here.start("cot", cot_i, g)
    odd = l.z % 2
    selectors(odd, ea, el, eh)
    ga = Gather(l, zst, w)

    def pack(ref, chunks):
        low = ref[...].astype(BF)
        a, bl, bh = dot(low, ea[...], TN), dot(low, el[...], TN), dot(low, eh[...], TN)
        for t, c in enumerate(chunks):
            zst[l.z, c, 0:96] = a[96 * t:96 * t + 96].astype(BF)
            zst[l.z, c, 96:144] = (bl[96 * t:96 * t + 48] + bh[96 * t + 48:96 * t + 96]).astype(BF)

    def masks():
        clips, flags = clip_i[...].astype(F32), valid_i[...].astype(F32)
        row32 = lax.broadcasted_iota(jnp.int32, (256, 32), 0) // 8
        spread = jnp.where(row32 == lax.broadcasted_iota(jnp.int32, (256, 32), 1), 1.0, 0.0)
        clip_key = jnp.sum(spread * clips, axis=1, keepdims=True)
        flag_key = jnp.sum(spread * flags, axis=1, keepdims=True)
        clip_query = dot(jnp.broadcast_to(clips, (8, 32)).astype(BF), spread.astype(BF), NT)[0:1]
        j = lax.broadcasted_iota(jnp.int32, (256, 256), 0)
        i = lax.broadcasted_iota(jnp.int32, (256, 256), 1)
        allowed = (clip_key == clip_query) & (flag_key > 0.5) & (j % 8 == i % 8)
        tmask[...] = jnp.where(allowed, 0.0, -1e30)
        clip_row = lax.broadcasted_iota(jnp.int32, (4, 32), 0)
        which = jnp.where((clip_i[...] % 4) == clip_row, 1.0, 0.0)
        frame_of = lax.broadcasted_iota(jnp.int32, (32, 128), 0)
        own = jnp.where(frame_of == lax.broadcasted_iota(jnp.int32, (32, 128), 1) + 4 * l.s, 1.0, 0.0)
        chosen = dot(which.astype(BF), own.astype(BF), NN)
        open_places = dot(place_i[...].astype(F32).astype(BF), chosen.astype(BF), TN)
        for f in range(4):
            smask[f] = jnp.where(open_places[:, f:f + 1] > 0.5, 0.0, -1e30)

    pack(ti_i, [0, 1, 2])
    vg[l.s] = vin[...].astype(BF).astype(F32)
    l.greeted()
    ga.zsend(3)
    for k in range(1, 8):
        peer = l.speer(k)
        l.sends(("t", k), tokens.at[:, pl.ds(4 * peer, 4)], xp.at[mine], peer)
        l.sends(("v", k), vg.at[l.s], vg.at[l.s], peer)
    pack(to_i, [3])
    pack(tl_i, [4])
    ga.tick()
    pack(si_i, [5, 6, 7])
    ga.tick()
    pack(so_i, [8])
    pack(fe_i, [9, 10, 11, 12])
    ga.tick()
    ga.zsend(2)
    for t in range(4):
        low = fr_i[:, 192 * t:192 * t + 192].astype(BF)
        zst[l.z, 13 + t, 0:96] = dot(low, ea[...], NN).astype(BF)
        zst[l.z, 13 + t, 96:144] = (dot(low[:48], el[...], NN) + dot(low[48:], eh[...], NN)).astype(BF)
    ga.tick()
    masks()
    l.got(*[("v", k) for k in range(1, 8)])
    assemble_vectors(vg, vec)
    l.got(*[("t", k) for k in range(1, 8)])
    here.wait("x", "xp")
    here.start("xp_o", xp, xp_o)
    for b in range(4):
        rows = pl.ds(b * 256, 256)
        n, _ = standardize(flat(xp[:, b]))
        nb[rows, :] = (n * vec[TG:TG + 1, :] + vec[TS:TS + 1, :]).astype(BF)
    ga.until(2)
    for b in range(4):
        project_in(nb[256 * b:256 * b + 256, :], w, TI, qkv, pl.ds(b * 256, 256), vec, TIB)
        if b % 2:
            ga.tick()
    here.start("tqkv_o", qkv, tqkv_o)
    here.wait("xp_o")
    ga.until(3)
    for b in range(4):
        attend_block(b, qkv, mixed, lse.at[0:48], lambda: tmask[...])
        o = dot(mixed[256 * b:256 * b + 256, :], w[TO:TO + 768, :], NT) + vec[TOB:TOB + 1, :]
        pr[:, b] = tiled(o)
        ret[:, 4 * l.s + b] = pr[mine, b]
        for k in range(1, 8):
            peer = l.speer(k)
            l.sends(("r", b, k), pr.at[pl.ds(4 * peer, 4), b], ret.at[:, 4 * l.s + b], peer)
        ga.tick()
    here.start("tmixed_o", mixed, tmixed_o)
    ga.until(4)
    for b in range(4):
        l.got(*[("r", b, k) for k in range(1, 8)])
    first = second = f1
    for f in range(4):
        rows = pl.ds(256 * f, 256)
        back = flat(ret[f]).astype(BF)
        gh[rows, :] = back
        total = flat(x[f]) + dot(back, w[TL:TL + 768, :], NT) + vec[TLB:TLB + 1, :]
        first[rows, :] = total
        n, _ = standardize(total)
        nb[rows, :] = (n * vec[SG:SG + 1, :] + vec[SS:SS + 1, :]).astype(BF)
        if f == 1:
            ga.tick()
    here.start("ret_o", gh, ret_o)
    here.start("first_o", first, first_o)
    ga.until(7)
    here.wait("tqkv_o", "tmixed_o")
    for f in range(4):
        rows = pl.ds(256 * f, 256)
        project_in(nb[256 * f:256 * f + 256, :], w, SI, qkv, rows, vec, SIB)
        attend_block(f, qkv, mixed, lse.at[48:96], lambda: smask[f])
        ga.tick()
    ga.until(8)
    here.wait("first_o", "ret_o", "cot")

    final, dfn = f2, f3
    for f in range(4):
        rows = pl.ds(256 * f, 256)
        value = first[rows, :] + dot(mixed[rows, :], w[SO:SO + 768, :], NT) + vec[SOB:SOB + 1, :]
        second[rows, :] = value
        n, _ = standardize(value)
        nb[rows, :] = (n * vec[FG:FG + 1, :] + vec[FS:FS + 1, :]).astype(BF)
        final[rows, :] = value + vec[FRB:FRB + 1, :]
        dfn[rows, :] = jnp.zeros((256, 768), F32)

    sc = Scatter(l, here, w, sr, fr, ar, br, zp, zr, ob, packed_o)
    vs = VectorSum(l, gv, vb)
    sums = gv.at[0]
    sums[...] = jnp.zeros((24, 768), F32)

    def note(r, value):
        sums[r:r + 1, :] += value

    def pump():
        if not ga.done:
            ga.tick()
        sc.pump()

    for step, t in enumerate((0, 2, 1, 3)):
        ga.until(10 if t % 2 == 0 else 12)
        ga.until(13 + t)
        we, wf = w.at[FE + 768 * t:FE + 768 * (t + 1)], w.at[FR + 768 * t:FR + 768 * (t + 1)]

        def unit(b, _):
            rows = pl.ds(pl.multiple_of(256 * b, 256), 256)
            u = dot(nb[rows, :], we[...], NT) + vec[FEB + t:FEB + t + 1, :]
            phi = 0.5 + 0.5 * lax.erf(u * 0.7071067811865476)
            a = (u * phi).astype(BF)
            act[rows, :] = a
            slope = phi + u * (0.3989422804014327 * jnp.exp(-0.5 * u * u))
            h = (dot(g[rows, :], wf[...], NN) * slope).astype(BF)
            gh[rows, :] = h
            final[rows, :] += dot(a, wf[...], NT)
            dfn[rows, :] += dot(h, we[...], NN)
            sums[FEB + t:FEB + t + 1, :] += column_sums(h.astype(F32))
            return 0

        lax.fori_loop(0, 2, unit, 0)
        pump()
        lax.fori_loop(2, 4, unit, 0)
        pump()
        ga.sources(13 + t)
        weight_gradient(wf, g, 0, act)
        sc.ready.append(13 + t)
        pump()
        ga.sources(*((9, 10) if t % 2 == 0 else (11, 12)))
        weight_gradient(we, gh, 0, nb)
        if step % 2:
            sc.ready += [9, 10] if step == 1 else [11, 12]
        pump()

    ga.sources(*GATHER_ORDER)
    for f in range(4):
        rows = pl.ds(256 * f, 256)
        nb[rows, :] = final[rows, :].astype(BF)
        n, scale = standardize(second[rows, :])
        e = dfn[rows, :]
        cot = g[rows, :].astype(F32)
        note(FRB, column_sums(cot))
        note(FG, column_sums(e * n))
        note(FS, column_sums(e))
        total = cot + norm_back(e, vec[FG:FG + 1, :], n, scale)
        final[rows, :] = total
        low = total.astype(BF)
        act[rows, :] = low
        note(SOB, column_sums(low.astype(F32)))
        gh[rows, :] = dot(low, w[SO:SO + 768, :], NN).astype(BF)
        if f % 2:
            sc.pump(rush=True)
    here.start("result", nb, result_o)
    here.start("first", first_o, first)
    weight_gradient(w.at[SO:SO + 768], act, 0, mixed)
    here.start("mixed2", tmixed_o, mixed)
    sc.ready.append(8)
    sc.pump(rush=True)
    l.gone(*[("r", b, k) for b in range(4) for k in range(1, 8)])
    here.start("xp2", xp_o, places_b)
    here.wait("result", "first")
    for f in range(4):
        rows = pl.ds(256 * f, 256)
        attend_block_back(f, qkv, gh, lse.at[48:96], lambda: smask[f])
        n, scale = standardize(first[rows, :])
        nb[rows, :] = (n * vec[SG:SG + 1, :] + vec[SS:SS + 1, :]).astype(BF)
        joined = qkv[rows, :]
        note(SIB, column_sums(joined[:, :768].astype(F32)))
        note(SIB + 1, column_sums(joined[:, 1536:].astype(F32)))
        e = dot(joined, w[SI:SI + 2304, :], NN)
        note(SG, column_sums(e * n))
        note(SS, column_sums(e))
        total = final[rows, :] + norm_back(e, vec[SG:SG + 1, :], n, scale)
        final[rows, :] = total
        low = total.astype(BF)
        act[rows, :] = low
        note(TLB, column_sums(low.astype(F32)))
        gp[f] = tiled(dot(low, w[TL:TL + 768, :], NN))
        gpp[4 * l.s + f] = gp[f, pl.ds(4 * l.s, 4)]
        for k in range(1, 8):
            peer = l.speer(k)
            l.sends(("g", f, k), gp.at[f, pl.ds(4 * peer, 4)], gpp.at[4 * l.s + f], peer)
        sc.pump(rush=True)
    here.start("ret", ret_o, gh)
    for j in range(3):
        weight_gradient(w.at[SI + 768 * j:SI + 768 * (j + 1)], qkv, 768 * j, nb)
    here.start("qkv2", tqkv_o, qkv)
    sc.ready += [5, 6, 7]
    sc.pump(rush=True)
    here.wait("ret")
    weight_gradient(w.at[TL:TL + 768], act, 0, gh)
    sc.ready.append(4)
    sc.pump(rush=True)

    for f in range(4):
        l.got(*[("g", f, k) for k in range(1, 8)])
    for b in range(4):
        rows = pl.ds(256 * b, 256)
        low = flat(gpp[:, b])
        note(TOB, column_sums(low))
        low = low.astype(BF)
        act[rows, :] = low
        gh[rows, :] = dot(low, w[TO:TO + 768, :], NN).astype(BF)
    sc.pump(rush=True)
    here.wait("mixed2")
    weight_gradient(w.at[TO:TO + 768], act, 0, mixed)
    sc.ready.append(3)
    sc.pump(rush=True)
    here.wait("qkv2", "xp2")
    for b in range(4):
        rows = pl.ds(256 * b, 256)
        attend_block_back(b, qkv, gh, lse.at[0:48], lambda: tmask[...])
        n, scale = standardize(flat(places_b[:, b]))
        nb[rows, :] = (n * vec[TG:TG + 1, :] + vec[TS:TS + 1, :]).astype(BF)
        joined = qkv[rows, :]
        note(TIB, column_sums(joined[:, :768].astype(F32)))
        note(TIB + 1, column_sums(joined[:, 1536:].astype(F32)))
        e = dot(joined, w[TI:TI + 2304, :], NN)
        note(TG, column_sums(e * n))
        note(TS, column_sums(e))
        gb[:, b] = tiled(norm_back(e, vec[TG:TG + 1, :], n, scale))
        it[:, 4 * l.s + b] = gb[mine, b]
        for k in range(1, 8):
            peer = l.speer(k)
            l.sends(("h", b, k), gb.at[pl.ds(4 * peer, 4), b], it.at[:, 4 * l.s + b], peer)
        sc.pump(rush=True)
    for j in range(3):
        weight_gradient(w.at[TI + 768 * j:TI + 768 * (j + 1)], qkv, 768 * j, nb)
    sc.ready += [0, 1, 2]
    for i in range(3):
        vs.swap(i)
        sc.pump(rush=True)
        vs.join(i)
    vs.swapz()
    for b in range(4):
        l.got(*[("h", b, k) for k in range(1, 8)])
    for f in range(4):
        rows = pl.ds(256 * f, 256)
        final[rows, :] += flat(it[f])
    here.start("grad", final, grad_o)
    sc.pump(rush=True)
    total_o[...] = vs.total()
    sc.finish()
    l.drain()
    here.drain()


LIMIT = 63 << 20
VM = pl.BlockSpec(memory_space=pltpu.VMEM)
ANY = pl.BlockSpec(memory_space=pl.ANY)


def hand_over(
    result_i, grad_i, packed, vec,
    result_o, grad_o, tg_o, ts_o, gti, tib_o, gto, tob_o, gtl, tlb_o, sg_o, ss_o, gsi, sib_o, gso, sob_o, fg_o, fs_o, gfe, feb_o,
    gfr, frb_o, ea, el, eh,
):
    selectors(lax.axis_index("grp") % 2, ea, el, eh)
    result_o[...] = result_i[...]
    grad_o[...] = grad_i[...]
    for c in range(CHUNKS):
        total = packed[c]
        a, folded = total[:96], total[96:]
        lane = lax.broadcasted_iota(jnp.int32, (48, 128), 1)
        b = jnp.concatenate([jnp.where(lane < 64, folded, 0.0), jnp.where(lane < 64, 0.0, folded)], axis=0)
        eb = el[...] + eh[...]
        a_high, b_high = a.astype(BF), b.astype(BF)
        parts = ((ea[...], a_high), (eb, b_high), (ea[...], (a - a_high.astype(F32)).astype(BF)),
                 (eb, (b - b_high.astype(F32)).astype(BF)))
        if c >= 13:
            value = sum(dot(half, e, NT) for e, half in parts)
            gfr[:, 192 * (c - 13):192 * (c - 12)] = value
        else:
            value = sum(dot(e, half, NT) for e, half in parts)
            out = (gti, gti, gti, gto, gtl, gsi, gsi, gsi, gso, gfe, gfe, gfe, gfe)[c]
            t = (0, 1, 2, 0, 0, 0, 1, 2, 0, 0, 1, 2, 3)[c]
            out[:, 96 * t:96 * t + 96] = value
    me = lax.axis_index("seq")
    for s in range(8):
        @pl.when(me == s)
        def _():
            for r, o in ((TG, tg_o), (TS, ts_o), (TOB, tob_o), (TLB, tlb_o), (SG, sg_o), (SS, ss_o), (SOB, sob_o), (FG, fg_o),
                         (FS, fs_o), (FRB, frb_o)):
                o[...] = vec[r, 96 * s:96 * s + 96]
            for r, o in ((TIB, tib_o), (SIB, sib_o)):
                o[...] = vec[r + s // 4, 192 * (s % 4):192 * (s % 4) + 192]
            t, lane = FEB + 2 * (s % 2), 192 * (s // 2)
            feb_o[...] = jnp.concatenate([vec[t:t + 1, lane:lane + 192], vec[t + 1:t + 2, lane:lane + 192]], axis=1).reshape(384)


def on_device_fast(
    tokens, cotangent, frame_clip, frame_valid, place_valid,
    time_gain, time_shift, time_inward, time_inward_bias, time_outward, time_outward_bias, time_linear, time_linear_bias,
    space_gain, space_shift, space_inward, space_inward_bias, space_outward, space_outward_bias,
    feed_gain, feed_shift, feed_expand, feed_expand_bias, feed_reduce, feed_reduce_bias,
):
    vectors = jnp.concatenate([
        time_gain, time_shift, time_outward_bias, time_linear_bias, space_gain, space_shift, space_outward_bias, feed_gain,
        feed_shift, feed_reduce_bias, time_inward_bias, space_inward_bias, feed_expand_bias])
    vin = jnp.pad(vectors.reshape(18, 96), ((0, 6), (0, 32)))
    shaped, vmem = jax.ShapeDtypeStruct, pltpu.VMEM
    rows_bf, rows_f32 = vmem((1024, 768), BF), vmem((1024, 768), F32)
    by_frame, by_place = vmem((4, 32, 8, 768), BF), vmem((32, 4, 8, 768), BF)
    row_block, selector = vmem((SLOTS, 96, 768), BF), vmem((192, 128), BF)
    n = CHUNKS * 20 + 14 + 28 + 56 + 6
    parameters = (
        time_gain, time_shift, time_inward, time_inward_bias, time_outward, time_outward_bias, time_linear, time_linear_bias,
        space_gain, space_shift, space_inward, space_inward_bias, space_outward, space_outward_bias,
        feed_gain, feed_shift, feed_expand, feed_expand_bias, feed_reduce, feed_reduce_bias)
    outs = pl.pallas_call(
        layer_kernel,
        out_shape=(
            shaped((1024, 768), BF), shaped((1024, 768), F32), shaped((CHUNKS, 144, 128), F32), shaped((24, 768), F32),
            shaped((1024, 2304), BF), shaped((1024, 768), BF), shaped((1024, 768), BF), shaped((1024, 768), F32),
            shaped((32, 4, 8, 768), BF)),
        in_specs=[ANY, ANY] + [VM] * 11,
        out_specs=(ANY, ANY, ANY, VM) + (ANY,) * 5,
        scratch_shapes=[
            vmem((WROWS, 768), BF), vmem((4, CHUNKS, 144, 128), BF), vmem((8, 24, 128), F32), vmem((24, 768), F32),
            selector, selector, selector, vmem((256, 256), F32), vmem((4, 256, 1), F32),
            by_frame, by_frame, by_place, by_place, rows_bf, rows_bf, vmem((1024, 2304), BF), rows_f32, rows_f32, rows_f32,
            rows_bf, rows_bf, rows_bf,
            vmem((SLOTS, 4, 96, 768), BF), row_block, row_block, row_block, vmem((SLOTS, 4, 144, 128), BF),
            vmem((SLOTS, 3, 144, 128), BF), vmem((SLOTS, 144, 128), F32), vmem((4, 24, 768), F32), vmem((7, 24, 768), F32), vmem((96, 256), F32),
            pltpu.SemaphoreType.DMA((44,)), pltpu.SemaphoreType.DMA((n,)), pltpu.SemaphoreType.DMA((n,))],
        compiler_params=pltpu.CompilerParams(collective_id=0, has_side_effects=True, vmem_limit_bytes=LIMIT),
    )(tokens.reshape(4, 32, 8, 768), cotangent.reshape(1024, 768), frame_clip.reshape(1, 32), frame_valid.reshape(1, 32),
      place_valid, vin, time_inward, time_outward, time_linear, space_inward, space_outward, feed_expand, feed_reduce.T)
    shapes = [shaped(p.shape, F32) for p in parameters]
    shapes[18] = shaped(feed_reduce.T.shape, F32)
    outs = list(pl.pallas_call(
        hand_over, out_shape=(shaped((1024, 768), BF), shaped((1024, 768), F32)) + tuple(shapes),
        in_specs=[VM] * 4, out_specs=(VM,) * 22, scratch_shapes=[selector] * 3,
        compiler_params=pltpu.CompilerParams(vmem_limit_bytes=32 << 20))(*outs[:4]))
    outs[20] = outs[20].T
    return (outs[0].reshape(tokens.shape), outs[1].reshape(tokens.shape)) + tuple(outs[2:])


HEADS = 12


def normalize(inputs, scaling, offset):
    average = jnp.mean(inputs, axis=-1, keepdims=True)
    centered = inputs - average
    variance = jnp.mean(centered * centered, axis=-1, keepdims=True)
    return centered * lax.rsqrt(variance + EPSILON) * scaling + offset


def gelu_exact(inputs):
    return jax.nn.gelu(inputs, approximate=False)


def matmul(former, latter):
    return jnp.dot(former, latter, preferred_element_type=jnp.float32)


def inner(former, latter):
    return lax.dot_general(
        former, latter, (((0,), (0,)), ((), ())), preferred_element_type=jnp.float32
    )


def against(former, latter):
    return lax.dot_general(
        former, latter, (((1,), (1,)), ((), ())), preferred_element_type=jnp.float32
    )


def column_sum(delta_rows):
    return jnp.sum(delta_rows, axis=0, dtype=jnp.float32)


def packed_sum(joined_grad):
    totals = jnp.sum(joined_grad, axis=0, dtype=jnp.float32)
    model_width = totals.shape[0] // 3
    return jnp.concatenate([totals[:model_width], totals[2 * model_width :]])


def patterns(flavor):
    if flavor == "time":
        return ("fphd,gphd->phfg", "phfg,gphd->fphd", "phfg,fphd->gphd")
    return ("fphd,fqhd->fhpq", "fhpq,fqhd->fphd", "fhpq,fphd->fqhd")


def project_in_general(normed_low, weight, packed_bias, leading, head_count):
    model_width = normed_low.shape[-1]
    full_bias = jnp.concatenate(
        [
            packed_bias[:model_width],
            jnp.zeros((model_width,), jnp.float32),
            packed_bias[model_width:],
        ]
    )
    joined = (matmul(normed_low, weight) + full_bias).astype(jnp.bfloat16)
    shaped = joined.reshape(leading + (3, head_count, model_width // head_count))
    return (shaped[:, :, 0], shaped[:, :, 1], shaped[:, :, 2])


def attend(queries, keys_in, values, allowed, flavor):
    score_form, mix_form, spare_form = patterns(flavor)
    factor = queries.shape[-1] ** (-0.5)
    scores = jnp.einsum(score_form, queries, keys_in, preferred_element_type=jnp.float32) * factor
    masked = jnp.where(allowed, scores, -1e30)
    highest = jnp.max(masked, axis=-1, keepdims=True)
    raised = jnp.exp(masked - highest)
    summed = jnp.sum(raised, axis=-1, keepdims=True)
    chances = (raised / summed).astype(jnp.bfloat16)
    mixed = jnp.einsum(mix_form, chances, values, preferred_element_type=jnp.float32)
    return (mixed, highest + jnp.log(summed))


def attend_back(queries, keys_in, values, log_total, allowed, upstream, flavor):
    score_form, mix_form, spare_form = patterns(flavor)
    factor = queries.shape[-1] ** (-0.5)
    scores = jnp.einsum(score_form, queries, keys_in, preferred_element_type=jnp.float32) * factor
    chances = jnp.exp(jnp.where(allowed, scores, -1e30) - log_total)
    value_grad = jnp.einsum(
        spare_form, chances.astype(jnp.bfloat16), upstream, preferred_element_type=jnp.float32
    )
    chance_grad = jnp.einsum(score_form, upstream, values, preferred_element_type=jnp.float32)
    score_grad = (
        chances * (chance_grad - jnp.sum(chance_grad * chances, axis=-1, keepdims=True))
    ).astype(jnp.bfloat16)
    query_grad = (
        jnp.einsum(mix_form, score_grad, keys_in, preferred_element_type=jnp.float32) * factor
    )
    key_grad = (
        jnp.einsum(spare_form, score_grad, queries, preferred_element_type=jnp.float32) * factor
    )
    joined = jnp.stack([query_grad, key_grad, value_grad], axis=2)
    return joined.reshape(-1, 3 * joined.shape[-1] * joined.shape[-2]).astype(jnp.bfloat16)


def on_device_general(
    tokens,
    cotangent,
    frame_clip,
    frame_valid,
    place_valid,
    time_gain,
    time_shift,
    time_inward,
    time_inward_bias,
    time_outward,
    time_outward_bias,
    time_linear,
    time_linear_bias,
    space_gain,
    space_shift,
    space_inward,
    space_inward_bias,
    space_outward,
    space_outward_bias,
    feed_gain,
    feed_shift,
    feed_expand,
    feed_expand_bias,
    feed_reduce,
    feed_reduce_bias,
):
    frames_dev, places, model_width = tokens.shape
    head_count = HEADS
    group_frames = frame_clip.shape[0]
    clip_count = place_valid.shape[0]
    place_dev = places // lax.axis_size("seq")
    rows_part = (
        lax.all_gather(time_inward.astype(jnp.bfloat16), "grp", axis=0, tiled=True),
        lax.all_gather(time_outward.astype(jnp.bfloat16), "grp", axis=0, tiled=True),
        lax.all_gather(time_linear.astype(jnp.bfloat16), "grp", axis=0, tiled=True),
        lax.all_gather(space_inward.astype(jnp.bfloat16), "grp", axis=0, tiled=True),
        lax.all_gather(space_outward.astype(jnp.bfloat16), "grp", axis=0, tiled=True),
        lax.all_gather(feed_expand.astype(jnp.bfloat16), "grp", axis=0, tiled=True),
        lax.all_gather(feed_reduce.astype(jnp.bfloat16), "grp", axis=0, tiled=True),
    )
    gathered = (
        lax.all_gather(rows_part[0], "seq", axis=1, tiled=True),
        lax.all_gather(rows_part[1], "seq", axis=1, tiled=True),
        lax.all_gather(rows_part[2], "seq", axis=1, tiled=True),
        lax.all_gather(rows_part[3], "seq", axis=1, tiled=True),
        lax.all_gather(rows_part[4], "seq", axis=1, tiled=True),
        lax.all_gather(rows_part[5], "seq", axis=1, tiled=True),
        lax.all_gather(rows_part[6], "seq", axis=1, tiled=True),
        lax.all_gather(time_gain.astype(jnp.bfloat16), "seq", axis=0, tiled=True),
        lax.all_gather(time_shift.astype(jnp.bfloat16), "seq", axis=0, tiled=True),
        lax.all_gather(time_inward_bias.astype(jnp.bfloat16), "seq", axis=0, tiled=True),
        lax.all_gather(time_outward_bias.astype(jnp.bfloat16), "seq", axis=0, tiled=True),
        lax.all_gather(time_linear_bias.astype(jnp.bfloat16), "seq", axis=0, tiled=True),
        lax.all_gather(space_gain.astype(jnp.bfloat16), "seq", axis=0, tiled=True),
        lax.all_gather(space_shift.astype(jnp.bfloat16), "seq", axis=0, tiled=True),
        lax.all_gather(space_inward_bias.astype(jnp.bfloat16), "seq", axis=0, tiled=True),
        lax.all_gather(space_outward_bias.astype(jnp.bfloat16), "seq", axis=0, tiled=True),
        lax.all_gather(feed_gain.astype(jnp.bfloat16), "seq", axis=0, tiled=True),
        lax.all_gather(feed_shift.astype(jnp.bfloat16), "seq", axis=0, tiled=True),
        lax.all_gather(feed_expand_bias.astype(jnp.bfloat16), "seq", axis=0, tiled=True),
        lax.all_gather(feed_reduce_bias.astype(jnp.bfloat16), "seq", axis=0, tiled=True),
    )
    own_slot = lax.axis_index("seq")
    own_clips = lax.dynamic_slice_in_dim(frame_clip, own_slot * frames_dev, frames_dev) % clip_count
    matches = own_clips[:, None] == jnp.arange(clip_count, dtype=jnp.int32)[None, :]
    key_places = jnp.sum(jnp.where(matches[:, :, None], place_valid[None, :, :], 0), axis=1)
    space_allowed = (key_places == 1)[:, None, None, :]
    time_allowed = ((frame_clip[:, None] == frame_clip[None, :]) & (frame_valid[None, :] == 1))[
        None, None
    ]
    placed = lax.all_to_all(tokens, "seq", split_axis=1, concat_axis=0, tiled=True)
    placed_rows = placed.reshape(-1, model_width).astype(jnp.float32)
    time_normed_wide, time_norm_pull = jax.vjp(
        normalize,
        placed_rows,
        gathered[7].astype(jnp.float32),
        gathered[8].astype(jnp.float32),
    )
    time_normed = time_normed_wide.astype(jnp.bfloat16)
    time_parts = project_in_general(
        time_normed,
        gathered[0],
        gathered[9].astype(jnp.float32),
        (group_frames, place_dev),
        head_count,
    )
    time_mixed, time_total = attend(
        time_parts[0], time_parts[1], time_parts[2], time_allowed, "time"
    )
    time_mixed_low = time_mixed.reshape(-1, model_width).astype(jnp.bfloat16)
    time_proj = (
        matmul(time_mixed_low, gathered[1]) + gathered[10].astype(jnp.float32)
    ).astype(jnp.bfloat16)
    returned = lax.all_to_all(
        time_proj.reshape(group_frames, place_dev, model_width),
        "seq",
        split_axis=0,
        concat_axis=1,
        tiled=True,
    )
    returned_rows = returned.reshape(-1, model_width)
    first_sum = (
        tokens.reshape(-1, model_width).astype(jnp.float32)
        + matmul(returned_rows, gathered[2])
        + gathered[11].astype(jnp.float32)
    )
    space_normed_wide, space_norm_pull = jax.vjp(
        normalize,
        first_sum,
        gathered[12].astype(jnp.float32),
        gathered[13].astype(jnp.float32),
    )
    space_normed = space_normed_wide.astype(jnp.bfloat16)
    space_parts = project_in_general(
        space_normed,
        gathered[3],
        gathered[14].astype(jnp.float32),
        (frames_dev, places),
        head_count,
    )
    space_mixed, space_total = attend(
        space_parts[0], space_parts[1], space_parts[2], space_allowed, "space"
    )
    space_mixed_low = space_mixed.reshape(-1, model_width).astype(jnp.bfloat16)
    second_sum = (
        first_sum
        + matmul(space_mixed_low, gathered[4])
        + gathered[15].astype(jnp.float32)
    )
    feed_normed_wide, feed_norm_pull = jax.vjp(
        normalize,
        second_sum,
        gathered[16].astype(jnp.float32),
        gathered[17].astype(jnp.float32),
    )
    feed_normed = feed_normed_wide.astype(jnp.bfloat16)
    hidden = matmul(feed_normed, gathered[5]) + gathered[18].astype(jnp.float32)
    activated_wide, gelu_pull = jax.vjp(gelu_exact, hidden)
    activated = activated_wide.astype(jnp.bfloat16)
    final_sum = (
        second_sum
        + matmul(activated, gathered[6])
        + gathered[19].astype(jnp.float32)
    )
    result = final_sum.astype(jnp.bfloat16).reshape(tokens.shape)
    rows_again = (
        lax.all_gather(time_inward.astype(jnp.bfloat16), "grp", axis=0, tiled=True),
        lax.all_gather(time_outward.astype(jnp.bfloat16), "grp", axis=0, tiled=True),
        lax.all_gather(time_linear.astype(jnp.bfloat16), "grp", axis=0, tiled=True),
        lax.all_gather(space_inward.astype(jnp.bfloat16), "grp", axis=0, tiled=True),
        lax.all_gather(space_outward.astype(jnp.bfloat16), "grp", axis=0, tiled=True),
        lax.all_gather(feed_expand.astype(jnp.bfloat16), "grp", axis=0, tiled=True),
        lax.all_gather(feed_reduce.astype(jnp.bfloat16), "grp", axis=0, tiled=True),
    )
    gathered_again = (
        lax.all_gather(rows_again[0], "seq", axis=1, tiled=True),
        lax.all_gather(rows_again[1], "seq", axis=1, tiled=True),
        lax.all_gather(rows_again[2], "seq", axis=1, tiled=True),
        lax.all_gather(rows_again[3], "seq", axis=1, tiled=True),
        lax.all_gather(rows_again[4], "seq", axis=1, tiled=True),
        lax.all_gather(rows_again[5], "seq", axis=1, tiled=True),
        lax.all_gather(rows_again[6], "seq", axis=1, tiled=True),
        lax.all_gather(time_gain.astype(jnp.bfloat16), "seq", axis=0, tiled=True),
        lax.all_gather(time_shift.astype(jnp.bfloat16), "seq", axis=0, tiled=True),
        lax.all_gather(time_inward_bias.astype(jnp.bfloat16), "seq", axis=0, tiled=True),
        lax.all_gather(time_outward_bias.astype(jnp.bfloat16), "seq", axis=0, tiled=True),
        lax.all_gather(time_linear_bias.astype(jnp.bfloat16), "seq", axis=0, tiled=True),
        lax.all_gather(space_gain.astype(jnp.bfloat16), "seq", axis=0, tiled=True),
        lax.all_gather(space_shift.astype(jnp.bfloat16), "seq", axis=0, tiled=True),
        lax.all_gather(space_inward_bias.astype(jnp.bfloat16), "seq", axis=0, tiled=True),
        lax.all_gather(space_outward_bias.astype(jnp.bfloat16), "seq", axis=0, tiled=True),
        lax.all_gather(feed_gain.astype(jnp.bfloat16), "seq", axis=0, tiled=True),
        lax.all_gather(feed_shift.astype(jnp.bfloat16), "seq", axis=0, tiled=True),
        lax.all_gather(feed_expand_bias.astype(jnp.bfloat16), "seq", axis=0, tiled=True),
        lax.all_gather(feed_reduce_bias.astype(jnp.bfloat16), "seq", axis=0, tiled=True),
    )
    upstream = cotangent.reshape(-1, model_width).astype(jnp.float32)
    feed_delta = cotangent.reshape(-1, model_width)
    gradient_feed_reduce = inner(activated, feed_delta)
    gradient_feed_reduce_bias = column_sum(feed_delta)
    (hidden_wide,) = gelu_pull(against(feed_delta, gathered_again[6]))
    hidden_delta = hidden_wide.astype(jnp.bfloat16)
    gradient_feed_expand = inner(feed_normed, hidden_delta)
    gradient_feed_expand_bias = column_sum(hidden_delta)
    second_back, gradient_feed_gain, gradient_feed_shift = feed_norm_pull(
        against(hidden_delta, gathered_again[5])
    )
    second_delta = upstream + second_back
    space_delta = second_delta.astype(jnp.bfloat16)
    gradient_space_outward = inner(space_mixed_low, space_delta)
    gradient_space_outward_bias = column_sum(space_delta)
    space_mixed_delta = against(space_delta, gathered_again[4]).astype(jnp.bfloat16)
    space_mixed_delta = space_mixed_delta.reshape(frames_dev, places, head_count, -1)
    space_joined = attend_back(
        space_parts[0],
        space_parts[1],
        space_parts[2],
        space_total,
        space_allowed,
        space_mixed_delta,
        "space",
    )
    gradient_space_inward = inner(space_normed, space_joined)
    gradient_space_inward_bias = packed_sum(space_joined)
    first_back, gradient_space_gain, gradient_space_shift = space_norm_pull(
        against(space_joined, gathered_again[3])
    )
    first_delta = second_delta + first_back
    linear_delta = first_delta.astype(jnp.bfloat16)
    gradient_time_linear = inner(returned_rows, linear_delta)
    gradient_time_linear_bias = column_sum(linear_delta)
    proj_delta = against(linear_delta, gathered_again[2]).astype(jnp.bfloat16)
    proj_placed = lax.all_to_all(
        proj_delta.reshape(frames_dev, places, model_width),
        "seq",
        split_axis=1,
        concat_axis=0,
        tiled=True,
    )
    proj_rows = proj_placed.reshape(-1, model_width)
    gradient_time_outward = inner(time_mixed_low, proj_rows)
    gradient_time_outward_bias = column_sum(proj_rows)
    time_mixed_delta = against(proj_rows, gathered_again[1]).astype(jnp.bfloat16)
    time_mixed_delta = time_mixed_delta.reshape(group_frames, place_dev, head_count, -1)
    time_joined = attend_back(
        time_parts[0],
        time_parts[1],
        time_parts[2],
        time_total,
        time_allowed,
        time_mixed_delta,
        "time",
    )
    gradient_time_inward = inner(time_normed, time_joined)
    gradient_time_inward_bias = packed_sum(time_joined)
    placed_back, gradient_time_gain, gradient_time_shift = time_norm_pull(
        against(time_joined, gathered_again[0])
    )
    framed_back = lax.all_to_all(
        placed_back.reshape(group_frames, place_dev, model_width).astype(jnp.bfloat16),
        "seq",
        split_axis=0,
        concat_axis=1,
        tiled=True,
    ).astype(jnp.float32)
    input_gradient = (first_delta + framed_back.reshape(-1, model_width)).reshape(tokens.shape)
    matrix_terms = (
        gradient_time_inward,
        gradient_time_outward,
        gradient_time_linear,
        gradient_space_inward,
        gradient_space_outward,
        gradient_feed_expand,
        gradient_feed_reduce,
    )
    vector_terms = (
        gradient_time_gain,
        gradient_time_shift,
        gradient_time_inward_bias,
        gradient_time_outward_bias,
        gradient_time_linear_bias,
        gradient_space_gain,
        gradient_space_shift,
        gradient_space_inward_bias,
        gradient_space_outward_bias,
        gradient_feed_gain,
        gradient_feed_shift,
        gradient_feed_expand_bias,
        gradient_feed_reduce_bias,
    )
    columns_summed = (
        lax.psum_scatter(
            matrix_terms[0].astype(jnp.bfloat16), "seq", scatter_dimension=1, tiled=True
        ).astype(jnp.float32),
        lax.psum_scatter(
            matrix_terms[1].astype(jnp.bfloat16), "seq", scatter_dimension=1, tiled=True
        ).astype(jnp.float32),
        lax.psum_scatter(
            matrix_terms[2].astype(jnp.bfloat16), "seq", scatter_dimension=1, tiled=True
        ).astype(jnp.float32),
        lax.psum_scatter(
            matrix_terms[3].astype(jnp.bfloat16), "seq", scatter_dimension=1, tiled=True
        ).astype(jnp.float32),
        lax.psum_scatter(
            matrix_terms[4].astype(jnp.bfloat16), "seq", scatter_dimension=1, tiled=True
        ).astype(jnp.float32),
        lax.psum_scatter(
            matrix_terms[5].astype(jnp.bfloat16), "seq", scatter_dimension=1, tiled=True
        ).astype(jnp.float32),
        lax.psum_scatter(
            matrix_terms[6].astype(jnp.bfloat16), "seq", scatter_dimension=1, tiled=True
        ).astype(jnp.float32),
        lax.psum_scatter(
            vector_terms[0].astype(jnp.bfloat16), "seq", scatter_dimension=0, tiled=True
        ).astype(jnp.float32),
        lax.psum_scatter(
            vector_terms[1].astype(jnp.bfloat16), "seq", scatter_dimension=0, tiled=True
        ).astype(jnp.float32),
        lax.psum_scatter(
            vector_terms[2].astype(jnp.bfloat16), "seq", scatter_dimension=0, tiled=True
        ).astype(jnp.float32),
        lax.psum_scatter(
            vector_terms[3].astype(jnp.bfloat16), "seq", scatter_dimension=0, tiled=True
        ).astype(jnp.float32),
        lax.psum_scatter(
            vector_terms[4].astype(jnp.bfloat16), "seq", scatter_dimension=0, tiled=True
        ).astype(jnp.float32),
        lax.psum_scatter(
            vector_terms[5].astype(jnp.bfloat16), "seq", scatter_dimension=0, tiled=True
        ).astype(jnp.float32),
        lax.psum_scatter(
            vector_terms[6].astype(jnp.bfloat16), "seq", scatter_dimension=0, tiled=True
        ).astype(jnp.float32),
        lax.psum_scatter(
            vector_terms[7].astype(jnp.bfloat16), "seq", scatter_dimension=0, tiled=True
        ).astype(jnp.float32),
        lax.psum_scatter(
            vector_terms[8].astype(jnp.bfloat16), "seq", scatter_dimension=0, tiled=True
        ).astype(jnp.float32),
        lax.psum_scatter(
            vector_terms[9].astype(jnp.bfloat16), "seq", scatter_dimension=0, tiled=True
        ).astype(jnp.float32),
        lax.psum_scatter(
            vector_terms[10].astype(jnp.bfloat16), "seq", scatter_dimension=0, tiled=True
        ).astype(jnp.float32),
        lax.psum_scatter(
            vector_terms[11].astype(jnp.bfloat16), "seq", scatter_dimension=0, tiled=True
        ).astype(jnp.float32),
        lax.psum_scatter(
            vector_terms[12].astype(jnp.bfloat16), "seq", scatter_dimension=0, tiled=True
        ).astype(jnp.float32),
    )
    rows_summed = (
        lax.psum_scatter(
            columns_summed[0].astype(jnp.bfloat16), "grp", scatter_dimension=0, tiled=True
        ).astype(jnp.float32),
        lax.psum_scatter(
            columns_summed[1].astype(jnp.bfloat16), "grp", scatter_dimension=0, tiled=True
        ).astype(jnp.float32),
        lax.psum_scatter(
            columns_summed[2].astype(jnp.bfloat16), "grp", scatter_dimension=0, tiled=True
        ).astype(jnp.float32),
        lax.psum_scatter(
            columns_summed[3].astype(jnp.bfloat16), "grp", scatter_dimension=0, tiled=True
        ).astype(jnp.float32),
        lax.psum_scatter(
            columns_summed[4].astype(jnp.bfloat16), "grp", scatter_dimension=0, tiled=True
        ).astype(jnp.float32),
        lax.psum_scatter(
            columns_summed[5].astype(jnp.bfloat16), "grp", scatter_dimension=0, tiled=True
        ).astype(jnp.float32),
        lax.psum_scatter(
            columns_summed[6].astype(jnp.bfloat16), "grp", scatter_dimension=0, tiled=True
        ).astype(jnp.float32),
    )
    vector_shares = tuple(columns_summed[7:])
    vectors_summed = lax.psum(
        (
            vector_shares[0],
            vector_shares[1],
            vector_shares[2],
            vector_shares[3],
            vector_shares[4],
            vector_shares[5],
            vector_shares[6],
            vector_shares[7],
            vector_shares[8],
            vector_shares[9],
            vector_shares[10],
            vector_shares[11],
            vector_shares[12],
        ),
        "grp",
    )
    owned = tuple(rows_summed) + tuple(vectors_summed)
    return (result, input_gradient) + tuple(owned[i] for i in (7, 8, 0, 9, 1, 10, 2, 11, 12, 13, 3, 14, 4, 15, 16, 17, 5, 18, 6, 19))


def solution(mesh):
    fast = mesh.shape["grp"] == 4 and mesh.shape["seq"] == 8
    return jax.shard_map(
        on_device_fast if fast else on_device_general,
        mesh=mesh,
        in_specs=(
            P(("grp", "seq"), None, None),
            P(("grp", "seq"), None, None),
            P("grp"),
            P("grp"),
            P("grp", None),
            P("seq"),
            P("seq"),
            P("grp", "seq"),
            P("seq"),
            P("grp", "seq"),
            P("seq"),
            P("grp", "seq"),
            P("seq"),
            P("seq"),
            P("seq"),
            P("grp", "seq"),
            P("seq"),
            P("grp", "seq"),
            P("seq"),
            P("seq"),
            P("seq"),
            P("grp", "seq"),
            P("seq"),
            P("grp", "seq"),
            P("seq"),
        ),
        out_specs=(
            P(("grp", "seq"), None, None),
            P(("grp", "seq"), None, None),
            P("seq"),
            P("seq"),
            P("grp", "seq"),
            P("seq"),
            P("grp", "seq"),
            P("seq"),
            P("grp", "seq"),
            P("seq"),
            P("seq"),
            P("seq"),
            P("grp", "seq"),
            P("seq"),
            P("grp", "seq"),
            P("seq"),
            P("seq"),
            P("seq"),
            P("grp", "seq"),
            P("seq"),
            P("grp", "seq"),
            P("seq"),
        ),
        check_vma=False,
    )
```

```python
import jax
import jax.numpy as jnp
from jax import lax
from jax.experimental import pallas as pl
from jax.experimental.pallas import tpu as pltpu
from jax.sharding import PartitionSpec as P

MESH = pl.DeviceIdType.MESH
BF = jnp.bfloat16
F32 = jnp.float32
NN = (((1,), (0,)), ((), ()))
NT = (((1,), (1,)), ((), ()))
TN = (((0,), (0,)), ((), ()))

TI, TO, TL, SI, SO, FE, FR = 0, 2304, 3072, 3840, 6144, 6912, 9984
WROWS = 13056
BASE = ([96 * t for t in range(3)] + [TO, TL] + [SI + 96 * t for t in range(3)] + [SO]
        + [FE + 768 * (v // 2) + 96 * (v % 2) for v in range(4)] + [FR + 768 * t for t in range(4)])
PAIR = [576] * 3 + [192] * 2 + [576] * 3 + [192] + [192] * 4 + [192] * 4
CORE = [288] * 3 + [96] * 2 + [288] * 3 + [96] + [1536] * 4 + [96] * 4
CHUNKS = 17
GATHER_ORDER = [0, 1, 2, 3, 4, 5, 6, 7, 8, 9, 10, 13, 15, 11, 12, 14, 16]
SLOTS = 5
EARLY_SLOTS = 8
LAGS = (2, 3, 3, 3)
GATHER_LAGS = (3, 5, 3)
SPACING = 1
KINDS = ("p", "q", "so", "d", "sp", "sq", "sd")
EPSILON = 1e-06


def dot(a, b, dims):
    return lax.dot_general(a, b, dims, preferred_element_type=F32)


class Links:
    def __init__(self, send_sem, recv_sem):
        self.send_sem, self.recv_sem = send_sem, recv_sem
        self.copies, self.used, self.sent = {}, 0, set()
        self.z = lax.axis_index("grp")
        s = self.s = lax.axis_index("seq")
        core, x, y = s % 2, (s // 2) % 2, s // 4
        xn, yn = s + 2 - 4 * x, s + 4 - 8 * y
        self.core = core
        self.sib = s + 1 - 2 * core
        self.p = yn * (1 - core) + xn * core
        self.q = xn * (1 - core) + yn * core
        self.d = xn + yn - s

    def zpeer(self, k):
        return (self.z + k) % 4

    def speer(self, k):
        return (self.s + k) % 8

    def greet(self):
        bar = pltpu.get_barrier_semaphore()
        for k in range(1, 8):
            pl.semaphore_signal(bar, inc=1, device_id=(self.z, self.speer(k)), device_id_type=MESH)
        for k in range(1, 4):
            pl.semaphore_signal(bar, inc=1, device_id=(self.zpeer(k), self.s), device_id_type=MESH)

    def greeted(self):
        pl.semaphore_wait(pltpu.get_barrier_semaphore(), 10)

    def send(self, key, src, dst, device):
        i = self.used
        self.used += 1
        copy = pltpu.make_async_remote_copy(
            src_ref=src, dst_ref=dst, send_sem=self.send_sem.at[i], recv_sem=self.recv_sem.at[i],
            device_id=device, device_id_type=MESH)
        copy.start()
        self.copies[key] = copy

    def sends(self, key, src, dst, seq):
        self.send(key, src, dst, (self.z, seq))

    def sendz(self, key, src, dst, z):
        self.send(key, src, dst, (z, self.s))

    def got(self, *keys):
        for key in keys:
            self.copies[key].wait_recv()

    def gone(self, *keys):
        for key in keys:
            if key not in self.sent:
                self.sent.add(key)
                self.copies[key].wait_send()

    def drain(self):
        self.gone(*self.copies)


class Local:
    def __init__(self, sem):
        self.sem, self.used, self.copies = sem, 0, {}

    def start(self, key, src, dst):
        copy = pltpu.make_async_copy(src, dst, self.sem.at[self.used])
        self.used += 1
        copy.start()
        self.copies[key] = copy

    def wait(self, *keys):
        for key in keys:
            copy = self.copies.pop(key, None)
            if copy is not None:
                copy.wait()

    def drain(self):
        self.wait(*list(self.copies))


def place(c, s):
    return pl.ds(pl.multiple_of(BASE[c] + PAIR[c] * (s // 2) + CORE[c] * (s % 2), 32), 96)


def block(ref, c, s):
    return ref.at[place(c, s)]


class Gather:
    def __init__(self, links, zst, w):
        self.l, self.zst, self.w = links, zst, w
        self.next, self.flight, self.zsent, self.clock = 0, [], 0, 0

    def zsend(self, count=1):
        for i in range(self.zsent, min(self.zsent + count, CHUNKS)):
            c = GATHER_ORDER[i]
            own = self.zst.at[self.l.z, c]
            for k in range(1, 4):
                self.l.sendz(("zg", c, k), own, own, self.l.zpeer(k))
            self.zsent += 1

    def sources(self, *chunks):
        self.l.gone(*[(k, c) for c in chunks for k in KINDS])

    def step_a(self, i, c):
        l = self.l
        l.got(*[("zg", c, k) for k in range(1, 4)])
        rows = place(c, l.s)
        zst, w = self.zst, self.w
        for half in range(2):
            lo, hi = zst[2 * half, c], zst[2 * half + 1, c]
            w[rows, 384 * half:384 * half + 128] = lo[:96]
            w[rows, 384 * half + 256:384 * half + 384] = hi[:96]
            blo, bhi = lo[96:], hi[96:]
            w[rows, 384 * half + 128:384 * half + 256] = jnp.concatenate([
                jnp.concatenate([blo[:, :64], bhi[:, :64]], axis=1),
                jnp.concatenate([blo[:, 64:], bhi[:, 64:]], axis=1)], axis=0)
        own = block(w, c, l.s)
        l.sends(("p", c), own, own, l.p)
        l.sends(("q", c), own, own, l.q)
        l.sends(("so", c), own, own, l.sib)
        self.zsend()

    def step_b(self, i, c):
        l = self.l
        l.got(("p", c))
        bp = block(self.w, c, l.p)
        l.sends(("d", c), bp, bp, l.q)
        l.sends(("sp", c), bp, bp, l.sib)
        l.got(("q", c))
        bq = block(self.w, c, l.q)
        l.sends(("sq", c), bq, bq, l.sib)

    def step_c(self, i, c):
        l = self.l
        l.got(("d", c))
        bd = block(self.w, c, l.d)
        l.sends(("sd", c), bd, bd, l.sib)

    def step_d(self, i, c):
        self.l.got(("so", c), ("sp", c), ("sq", c), ("sd", c))

    def tick(self, push=True, whole=-1):
        steps = (self.step_b, self.step_c, self.step_d)
        self.clock += 1
        fresh = []
        if push and self.next < CHUNKS:
            self.step_a(self.next, GATHER_ORDER[self.next])
            fresh = [(self.next, 0, self.clock + GATHER_LAGS[0])]
            self.next += 1
        later = []
        for i, k, due in self.flight:
            if i <= whole or self.clock >= due:
                steps[k](i, GATHER_ORDER[i])
                k, due = k + 1, self.clock + (GATHER_LAGS + (0,))[k + 1]
            if k < 3:
                later.append((i, k, due))
        self.flight = later + fresh

    def until(self, chunk):
        i = GATHER_ORDER.index(chunk)
        while i >= self.next or any(j <= i for j, _, _ in self.flight):
            self.tick(push=self.next <= i, whole=i)

    @property
    def done(self):
        return self.next == CHUNKS and not self.flight


class Scatter:
    def __init__(self, links, local, g, sr, fr, ar, br, zp, zr, ob, out):
        self.l, self.local, self.g, self.sr, self.fr, self.ar, self.br = links, local, g, sr, fr, ar, br
        self.zp, self.zr, self.ob, self.out = zp, zr, ob, out
        self.ready, self.flight, self.order = [], [], []
        self.clock, self.pushed = 0, -9

    def step_a(self, i, c):
        l = self.l
        for j in range(4):
            l.sends(("s", c, j), block(self.g, c, 2 * j + 1 - l.core), self.sr.at[i % SLOTS, j], l.sib)

    def add(self, c, s, other):
        rows = place(c, s)
        self.g[rows, :] = (self.g[rows, :].astype(F32) + other.astype(F32)).astype(BF)

    def step_b(self, i, c):
        l, k = self.l, i % SLOTS
        l.got(*[("s", c, j) for j in range(4)])
        for s, j in ((l.d, l.d // 2), (l.p, l.p // 2), (l.q, l.q // 2), (l.s, l.s // 2)):
            self.add(c, s, self.sr[k, j])
            if s is l.d:
                l.sends(("f", c), block(self.g, c, l.d), self.fr.at[k], l.p)
            if s is l.p:
                l.sends(("a", c), block(self.g, c, l.p), self.ar.at[i % EARLY_SLOTS], l.p)

    def step_c(self, i, c):
        l, k = self.l, i % SLOTS
        l.got(("f", c))
        self.add(c, l.q, self.fr[k])
        l.sends(("b", c), block(self.g, c, l.q), self.br.at[k], l.q)

    def step_d(self, i, c):
        l, k = self.l, i % SLOTS
        l.got(("a", c), ("b", c))
        rows = place(c, l.s)
        total = self.g[rows, :].astype(F32) + self.ar[i % EARLY_SLOTS].astype(F32) + self.br[k].astype(F32)
        if i >= SLOTS:
            l.gone(*[("z", self.order[i - SLOTS], j) for j in range(1, 4)])
        zp = self.zp
        for half in range(2):
            lane = 384 * half
            zp[k, 2 * half, 0:96] = total[:, lane:lane + 128].astype(BF)
            zp[k, 2 * half + 1, 0:96] = total[:, lane + 256:lane + 384].astype(BF)
            mid = total[:, lane + 128:lane + 256]
            top, low = mid[:48], mid[48:]
            zp[k, 2 * half, 96:144] = jnp.concatenate([top[:, :64], low[:, :64]], axis=1).astype(BF)
            zp[k, 2 * half + 1, 96:144] = jnp.concatenate([top[:, 64:], low[:, 64:]], axis=1).astype(BF)
        for j in range(1, 4):
            z = l.zpeer(j)
            l.sendz(("z", c, j), zp.at[k, z], self.zr.at[k, j - 1], z)

    def step_e(self, i, c):
        l, k = self.l, i % SLOTS
        l.got(*[("z", c, j) for j in range(1, 4)])
        total = self.zp[k, l.z].astype(F32)
        for j in range(3):
            total += self.zr[k, j].astype(F32)
        if i >= SLOTS:
            self.local.wait(("o", self.order[i - SLOTS]))
        self.ob[k] = total
        self.local.start(("o", c), self.ob.at[k], self.out.at[c])

    def pump(self, rush=False):
        steps = (self.step_b, self.step_c, self.step_d, self.step_e)
        self.clock += 1
        fresh = []
        if self.ready and (rush or self.clock >= self.pushed + SPACING):
            c = self.ready.pop(0)
            i = len(self.order)
            self.order.append(c)
            self.step_a(i, c)
            self.pushed = self.clock
            fresh = [(i, 0, self.clock + LAGS[0])]
        later = []
        for i, k, due in self.flight:
            if rush or self.clock >= due:
                steps[k](i, self.order[i])
                k, due = k + 1, self.clock + (LAGS + (0,))[k + 1]
            if k < 4:
                later.append((i, k, due))
        self.flight = later + fresh

    def finish(self):
        while self.ready or self.flight:
            self.pump(rush=True)


class VectorSum:
    def __init__(self, links, gv, vb):
        self.l, self.gv, self.vb = links, gv, vb

    def swap(self, i):
        l = self.l
        l.sends(("vs", i), self.gv.at[i], self.vb.at[i], (l.sib, l.p, l.q)[i])

    def join(self, i):
        self.l.got(("vs", i))
        self.gv[i + 1] = self.gv[i] + self.vb[i]

    def swapz(self):
        l = self.l
        self.vb[3 + l.z] = self.gv[3]
        for k in range(1, 4):
            l.sendz(("vz", k), self.gv.at[3], self.vb.at[3 + l.z], l.zpeer(k))

    def total(self):
        self.l.got(*[("vz", k) for k in range(1, 4)])
        return (self.vb[3] + self.vb[4]) + (self.vb[5] + self.vb[6])


TG, TS, TOB, TLB, SG, SS, SOB, FG, FS, FRB, TIB, SIB, FEB = 0, 1, 2, 3, 4, 5, 6, 7, 8, 9, 10, 12, 14


def assemble_vectors(vg, vec):
    vec[...] = jnp.zeros(vec.shape, F32)
    for s in range(8):
        piece = vg[s]
        vec[0:10, 96 * s:96 * s + 96] = piece[0:10, 0:96]
        for a in range(2):
            i = 2 * s + a
            for r in (TIB, SIB):
                vec[r + i // 8:r + i // 8 + 1, 96 * (i % 8):96 * (i % 8) + 96] = piece[r + a:r + a + 1, 0:96]
        for a in range(4):
            t, lane = 2 * (s % 2) + a // 2, 192 * (s // 2) + 96 * (a % 2)
            vec[FEB + t:FEB + 1 + t, lane:lane + 96] = piece[FEB + a:FEB + 1 + a, 0:96]


def selectors(odd, ea, el, eh):
    m = lax.broadcasted_iota(jnp.int32, (192, 128), 0)
    c = lax.broadcasted_iota(jnp.int32, (192, 128), 1)
    whole, folded = c + 64 * odd, c % 64 + 128 * (1 - odd)
    ea[...] = jnp.where(m == whole, 1.0, 0.0).astype(BF)
    both = jnp.where(m == folded, 1.0, 0.0)
    el[...] = jnp.where(c < 64, both, 0.0).astype(BF)
    eh[...] = jnp.where(c < 64, 0.0, both).astype(BF)


def standardize(x):
    centered = x - jnp.mean(x, axis=-1, keepdims=True)
    scale = lax.rsqrt(jnp.mean(centered * centered, axis=-1, keepdims=True) + EPSILON)
    return centered * scale, scale


def norm_back(e, gain, n, scale):
    u = e * gain
    return scale * (u - jnp.mean(u, axis=-1, keepdims=True) - n * jnp.mean(u * n, axis=-1, keepdims=True))


def column_sums(x):
    return jnp.sum(x, axis=0, keepdims=True)


def head_masks(scale):
    lane = lax.broadcasted_iota(jnp.int32, (1, 128), 1)
    return [jnp.where(lane < 64, scale, 0.0).astype(BF), jnp.where(lane < 64, 0.0, scale).astype(BF)]


def pair_columns(qkv, rows, p):
    c = pl.multiple_of(p * 128, 128)
    return [qkv[rows, pl.ds(768 * j + c, 128)] for j in range(3)]


def attend_block(b, qkv, mixed, lse, bias):
    rows = pl.ds(b * 256, 256)

    def pair(p):
        q, k, v = pair_columns(qkv, rows, p)
        scaled, plain = head_masks(0.125), head_masks(1.0)
        out = None
        for h in range(2):
            s = dot(k * scaled[h], q, NT) + bias()
            m = jnp.max(s, axis=0, keepdims=True)
            e = jnp.exp(s - m)
            total = jnp.sum(e, axis=0, keepdims=True)
            lse[pl.ds(b * 12 + p * 2 + h, 1), :] = m + jnp.log(total)
            o = dot((e * (1.0 / total)).astype(BF), v * plain[h], TN)
            out = o if out is None else out + o
        mixed[rows, pl.ds(pl.multiple_of(p * 128, 128), 128)] = out.astype(BF)

    def body(i, _):
        pair(2 * i)
        pair(2 * i + 1)
        return 0

    lax.fori_loop(0, 3, body, 0)


def attend_block_back(b, qkv, gm, lse, bias):
    rows = pl.ds(b * 256, 256)

    def pair(p):
        q, k, v = pair_columns(qkv, rows, p)
        c = pl.multiple_of(p * 128, 128)
        g = gm[rows, pl.ds(c, 128)]
        scaled, plain = head_masks(0.125), head_masks(1.0)
        sums = [None, None, None]
        for h in range(2):
            kh, vh, qh, gh = k * scaled[h], v * plain[h], q * scaled[h], g * plain[h]
            s = dot(kh, q, NT) + bias()
            chances = jnp.exp(s - lse[pl.ds(b * 12 + p * 2 + h, 1), :])
            back = dot(vh, g, NT)
            mean = jnp.sum(chances * back, axis=0, keepdims=True)
            gs = (chances * (back - mean)).astype(BF)
            for j, term in enumerate((dot(gs, kh, TN), dot(gs, qh, NN), dot(chances.astype(BF), gh, NN))):
                sums[j] = term if sums[j] is None else sums[j] + term
        for j in range(3):
            qkv[rows, pl.ds(768 * j + c, 128)] = sums[j].astype(BF)

    def body(i, _):
        pair(2 * i)
        pair(2 * i + 1)
        return 0

    lax.fori_loop(0, 3, body, 0)


def project_in(normed, w, at, qkv, rows, vec, bias_row):
    for j in range(3):
        part = dot(normed, w[at + 768 * j:at + 768 * (j + 1), :], NT)
        if j != 1:
            r = bias_row + j // 2
            part = part + vec[r:r + 1, :]
        qkv[rows, 768 * j:768 * (j + 1)] = part.astype(BF)


def weight_gradient(out, delta, column, rows):
    for m in range(3):
        lane = column + 256 * m
        out[256 * m:256 * m + 256, :] = dot(delta[:, lane:lane + 256], rows[...], TN).astype(BF)


def flat(x):
    return x.astype(F32).reshape(256, 768)


def tiled(x):
    return x.reshape(32, 8, 768).astype(BF)


def layer_kernel(
    tokens, cot_i, clip_i, valid_i, place_i, vin, ti_i, to_i, tl_i, si_i, so_i, fe_i, fr_i,
    result_o, grad_o, packed_o, total_o, tqkv_o, tmixed_o, ret_o, first_o, xp_o,
    w, zst, vg, vec, ea, el, eh, tmask, smask, frames_a, frames_b, places_a, places_b, nb, mixed, qkv, f1, f2, f3, act, gh, g,
    sr, fr, ar, br, zp, zr, ob, gv, vb, lse, local_sem, send_sem, recv_sem,
):
    l = Links(send_sem, recv_sem)
    l.greet()
    here = Local(local_sem)
    mine = pl.ds(4 * l.s, 4)
    xp, gpp = places_a, places_a
    pr, gb = places_b, places_b
    ret, it = frames_a, frames_a
    x, gp = frames_b, frames_b
    here.start("x", tokens, x)
    here.start("xp", tokens.at[:, mine], xp.at[mine])
    here.start("cot", cot_i, g)
    odd = l.z % 2
    selectors(odd, ea, el, eh)
    ga = Gather(l, zst, w)

    def pack(ref, chunks):
        low = ref[...].astype(BF)
        a, bl, bh = dot(low, ea[...], TN), dot(low, el[...], TN), dot(low, eh[...], TN)
        for t, c in enumerate(chunks):
            zst[l.z, c, 0:96] = a[96 * t:96 * t + 96].astype(BF)
            zst[l.z, c, 96:144] = (bl[96 * t:96 * t + 48] + bh[96 * t + 48:96 * t + 96]).astype(BF)

    def masks():
        clips, flags = clip_i[...].astype(F32), valid_i[...].astype(F32)
        row32 = lax.broadcasted_iota(jnp.int32, (256, 32), 0) // 8
        spread = jnp.where(row32 == lax.broadcasted_iota(jnp.int32, (256, 32), 1), 1.0, 0.0)
        clip_key = jnp.sum(spread * clips, axis=1, keepdims=True)
        flag_key = jnp.sum(spread * flags, axis=1, keepdims=True)
        clip_query = dot(jnp.broadcast_to(clips, (8, 32)).astype(BF), spread.astype(BF), NT)[0:1]
        j = lax.broadcasted_iota(jnp.int32, (256, 256), 0)
        i = lax.broadcasted_iota(jnp.int32, (256, 256), 1)
        allowed = (clip_key == clip_query) & (flag_key > 0.5) & (j % 8 == i % 8)
        tmask[...] = jnp.where(allowed, 0.0, -1e30)
        clip_row = lax.broadcasted_iota(jnp.int32, (4, 32), 0)
        which = jnp.where((clip_i[...] % 4) == clip_row, 1.0, 0.0)
        frame_of = lax.broadcasted_iota(jnp.int32, (32, 128), 0)
        own = jnp.where(frame_of == lax.broadcasted_iota(jnp.int32, (32, 128), 1) + 4 * l.s, 1.0, 0.0)
        chosen = dot(which.astype(BF), own.astype(BF), NN)
        open_places = dot(place_i[...].astype(F32).astype(BF), chosen.astype(BF), TN)
        for f in range(4):
            smask[f] = jnp.where(open_places[:, f:f + 1] > 0.5, 0.0, -1e30)

    pack(ti_i, [0, 1, 2])
    vg[l.s] = vin[...].astype(BF).astype(F32)
    l.greeted()
    ga.zsend(3)
    for k in range(1, 8):
        peer = l.speer(k)
        l.sends(("t", k), tokens.at[:, pl.ds(4 * peer, 4)], xp.at[mine], peer)
        l.sends(("v", k), vg.at[l.s], vg.at[l.s], peer)
    pack(to_i, [3])
    pack(tl_i, [4])
    ga.tick()
    pack(si_i, [5, 6, 7])
    ga.tick()
    pack(so_i, [8])
    pack(fe_i, [9, 10, 11, 12])
    ga.tick()
    ga.zsend(2)
    for t in range(4):
        low = fr_i[:, 192 * t:192 * t + 192].astype(BF)
        zst[l.z, 13 + t, 0:96] = dot(low, ea[...], NN).astype(BF)
        zst[l.z, 13 + t, 96:144] = (dot(low[:48], el[...], NN) + dot(low[48:], eh[...], NN)).astype(BF)
    ga.tick()
    masks()
    l.got(*[("v", k) for k in range(1, 8)])
    assemble_vectors(vg, vec)
    l.got(*[("t", k) for k in range(1, 8)])
    here.wait("x", "xp")
    here.start("xp_o", xp, xp_o)
    for b in range(4):
        rows = pl.ds(b * 256, 256)
        n, _ = standardize(flat(xp[:, b]))
        nb[rows, :] = (n * vec[TG:TG + 1, :] + vec[TS:TS + 1, :]).astype(BF)
    ga.until(2)
    for b in range(4):
        project_in(nb[256 * b:256 * b + 256, :], w, TI, qkv, pl.ds(b * 256, 256), vec, TIB)
        if b % 2:
            ga.tick()
    here.start("tqkv_o", qkv, tqkv_o)
    here.wait("xp_o")
    ga.until(3)
    for b in range(4):
        attend_block(b, qkv, mixed, lse.at[0:48], lambda: tmask[...])
        o = dot(mixed[256 * b:256 * b + 256, :], w[TO:TO + 768, :], NT) + vec[TOB:TOB + 1, :]
        pr[:, b] = tiled(o)
        ret[:, 4 * l.s + b] = pr[mine, b]
        for k in range(1, 8):
            peer = l.speer(k)
            l.sends(("r", b, k), pr.at[pl.ds(4 * peer, 4), b], ret.at[:, 4 * l.s + b], peer)
        ga.tick()
    here.start("tmixed_o", mixed, tmixed_o)
    ga.until(4)
    for b in range(4):
        l.got(*[("r", b, k) for k in range(1, 8)])
    first = second = f1
    for f in range(4):
        rows = pl.ds(256 * f, 256)
        back = flat(ret[f]).astype(BF)
        gh[rows, :] = back
        total = flat(x[f]) + dot(back, w[TL:TL + 768, :], NT) + vec[TLB:TLB + 1, :]
        first[rows, :] = total
        n, _ = standardize(total)
        nb[rows, :] = (n * vec[SG:SG + 1, :] + vec[SS:SS + 1, :]).astype(BF)
        if f == 1:
            ga.tick()
    here.start("ret_o", gh, ret_o)
    here.start("first_o", first, first_o)
    ga.until(7)
    here.wait("tqkv_o", "tmixed_o")
    for f in range(4):
        rows = pl.ds(256 * f, 256)
        project_in(nb[256 * f:256 * f + 256, :], w, SI, qkv, rows, vec, SIB)
        attend_block(f, qkv, mixed, lse.at[48:96], lambda: smask[f])
        ga.tick()
    ga.until(8)
    here.wait("first_o", "ret_o", "cot")

    final, dfn = f2, f3
    for f in range(4):
        rows = pl.ds(256 * f, 256)
        value = first[rows, :] + dot(mixed[rows, :], w[SO:SO + 768, :], NT) + vec[SOB:SOB + 1, :]
        second[rows, :] = value
        n, _ = standardize(value)
        nb[rows, :] = (n * vec[FG:FG + 1, :] + vec[FS:FS + 1, :]).astype(BF)
        final[rows, :] = value + vec[FRB:FRB + 1, :]
        dfn[rows, :] = jnp.zeros((256, 768), F32)

    sc = Scatter(l, here, w, sr, fr, ar, br, zp, zr, ob, packed_o)
    vs = VectorSum(l, gv, vb)
    sums = gv.at[0]
    sums[...] = jnp.zeros((24, 768), F32)

    def note(r, value):
        sums[r:r + 1, :] += value

    def pump():
        if not ga.done:
            ga.tick()
        sc.pump()

    for step, t in enumerate((0, 2, 1, 3)):
        ga.until(10 if t % 2 == 0 else 12)
        ga.until(13 + t)
        we, wf = w.at[FE + 768 * t:FE + 768 * (t + 1)], w.at[FR + 768 * t:FR + 768 * (t + 1)]

        def unit(b, _):
            rows = pl.ds(pl.multiple_of(256 * b, 256), 256)
            u = dot(nb[rows, :], we[...], NT) + vec[FEB + t:FEB + t + 1, :]
            phi = 0.5 + 0.5 * lax.erf(u * 0.7071067811865476)
            a = (u * phi).astype(BF)
            act[rows, :] = a
            slope = phi + u * (0.3989422804014327 * jnp.exp(-0.5 * u * u))
            h = (dot(g[rows, :], wf[...], NN) * slope).astype(BF)
            gh[rows, :] = h
            final[rows, :] += dot(a, wf[...], NT)
            dfn[rows, :] += dot(h, we[...], NN)
            sums[FEB + t:FEB + t + 1, :] += column_sums(h.astype(F32))
            return 0

        lax.fori_loop(0, 2, unit, 0)
        pump()
        lax.fori_loop(2, 4, unit, 0)
        pump()
        ga.sources(13 + t)
        weight_gradient(wf, g, 0, act)
        sc.ready.append(13 + t)
        pump()
        ga.sources(*((9, 10) if t % 2 == 0 else (11, 12)))
        weight_gradient(we, gh, 0, nb)
        if step % 2:
            sc.ready += [9, 10] if step == 1 else [11, 12]
        pump()

    ga.sources(*GATHER_ORDER)
    for f in range(4):
        rows = pl.ds(256 * f, 256)
        nb[rows, :] = final[rows, :].astype(BF)
        n, scale = standardize(second[rows, :])
        e = dfn[rows, :]
        cot = g[rows, :].astype(F32)
        note(FRB, column_sums(cot))
        note(FG, column_sums(e * n))
        note(FS, column_sums(e))
        total = cot + norm_back(e, vec[FG:FG + 1, :], n, scale)
        final[rows, :] = total
        low = total.astype(BF)
        act[rows, :] = low
        note(SOB, column_sums(low.astype(F32)))
        gh[rows, :] = dot(low, w[SO:SO + 768, :], NN).astype(BF)
        sc.pump()
    here.start("result", nb, result_o)
    here.start("first", first_o, first)
    weight_gradient(w.at[SO:SO + 768], act, 0, mixed)
    here.start("mixed2", tmixed_o, mixed)
    sc.ready.append(8)
    sc.pump()
    l.gone(*[("r", b, k) for b in range(4) for k in range(1, 8)])
    here.start("xp2", xp_o, places_b)
    here.wait("result", "first")
    for f in range(4):
        rows = pl.ds(256 * f, 256)
        attend_block_back(f, qkv, gh, lse.at[48:96], lambda: smask[f])
        sc.pump()
        n, scale = standardize(first[rows, :])
        nb[rows, :] = (n * vec[SG:SG + 1, :] + vec[SS:SS + 1, :]).astype(BF)
        joined = qkv[rows, :]
        note(SIB, column_sums(joined[:, :768].astype(F32)))
        note(SIB + 1, column_sums(joined[:, 1536:].astype(F32)))
        e = dot(joined, w[SI:SI + 2304, :], NN)
        note(SG, column_sums(e * n))
        note(SS, column_sums(e))
        total = final[rows, :] + norm_back(e, vec[SG:SG + 1, :], n, scale)
        final[rows, :] = total
        low = total.astype(BF)
        act[rows, :] = low
        note(TLB, column_sums(low.astype(F32)))
        gp[f] = tiled(dot(low, w[TL:TL + 768, :], NN))
        gpp[4 * l.s + f] = gp[f, pl.ds(4 * l.s, 4)]
        for k in range(1, 8):
            peer = l.speer(k)
            l.sends(("g", f, k), gp.at[f, pl.ds(4 * peer, 4)], gpp.at[4 * l.s + f], peer)
        sc.pump()
    here.start("ret", ret_o, gh)
    for j in range(3):
        weight_gradient(w.at[SI + 768 * j:SI + 768 * (j + 1)], qkv, 768 * j, nb)
        sc.pump()
    here.start("qkv2", tqkv_o, qkv)
    sc.ready += [5, 6, 7]
    sc.pump()
    here.wait("ret")
    weight_gradient(w.at[TL:TL + 768], act, 0, gh)
    sc.ready.append(4)
    sc.pump()

    for f in range(4):
        l.got(*[("g", f, k) for k in range(1, 8)])
    for b in range(4):
        rows = pl.ds(256 * b, 256)
        low = flat(gpp[:, b])
        note(TOB, column_sums(low))
        low = low.astype(BF)
        act[rows, :] = low
        gh[rows, :] = dot(low, w[TO:TO + 768, :], NN).astype(BF)
        if b == 1:
            sc.pump()
    sc.pump()
    here.wait("mixed2")
    weight_gradient(w.at[TO:TO + 768], act, 0, mixed)
    sc.ready.append(3)
    sc.pump()
    here.wait("qkv2", "xp2")
    for b in range(4):
        rows = pl.ds(256 * b, 256)
        attend_block_back(b, qkv, gh, lse.at[0:48], lambda: tmask[...])
        sc.pump()
        n, scale = standardize(flat(places_b[:, b]))
        nb[rows, :] = (n * vec[TG:TG + 1, :] + vec[TS:TS + 1, :]).astype(BF)
        joined = qkv[rows, :]
        note(TIB, column_sums(joined[:, :768].astype(F32)))
        note(TIB + 1, column_sums(joined[:, 1536:].astype(F32)))
        e = dot(joined, w[TI:TI + 2304, :], NN)
        note(TG, column_sums(e * n))
        note(TS, column_sums(e))
        gb[:, b] = tiled(norm_back(e, vec[TG:TG + 1, :], n, scale))
        it[:, 4 * l.s + b] = gb[mine, b]
        for k in range(1, 8):
            peer = l.speer(k)
            l.sends(("h", b, k), gb.at[pl.ds(4 * peer, 4), b], it.at[:, 4 * l.s + b], peer)
        sc.pump()
    for j in range(3):
        weight_gradient(w.at[TI + 768 * j:TI + 768 * (j + 1)], qkv, 768 * j, nb)
        sc.pump()
    sc.ready += [0, 1, 2]
    for i in range(3):
        vs.swap(i)
        sc.pump(rush=True)
        vs.join(i)
    vs.swapz()
    for b in range(4):
        l.got(*[("h", b, k) for k in range(1, 8)])
    for f in range(4):
        rows = pl.ds(256 * f, 256)
        final[rows, :] += flat(it[f])
    here.start("grad", final, grad_o)
    sc.pump(rush=True)
    total_o[...] = vs.total()
    sc.finish()
    l.drain()
    here.drain()


LIMIT = 63 << 20
VM = pl.BlockSpec(memory_space=pltpu.VMEM)
ANY = pl.BlockSpec(memory_space=pl.ANY)


def hand_over(
    result_i, grad_i, packed, vec,
    result_o, grad_o, tg_o, ts_o, gti, tib_o, gto, tob_o, gtl, tlb_o, sg_o, ss_o, gsi, sib_o, gso, sob_o, fg_o, fs_o, gfe, feb_o,
    gfr, frb_o, ea, el, eh,
):
    selectors(lax.axis_index("grp") % 2, ea, el, eh)
    result_o[...] = result_i[...]
    grad_o[...] = grad_i[...]
    for c in range(CHUNKS):
        total = packed[c]
        a, folded = total[:96], total[96:]
        lane = lax.broadcasted_iota(jnp.int32, (48, 128), 1)
        b = jnp.concatenate([jnp.where(lane < 64, folded, 0.0), jnp.where(lane < 64, 0.0, folded)], axis=0)
        eb = el[...] + eh[...]
        a_high, b_high = a.astype(BF), b.astype(BF)
        parts = ((ea[...], a_high), (eb, b_high), (ea[...], (a - a_high.astype(F32)).astype(BF)),
                 (eb, (b - b_high.astype(F32)).astype(BF)))
        if c >= 13:
            value = sum(dot(half, e, NT) for e, half in parts)
            gfr[:, 192 * (c - 13):192 * (c - 12)] = value
        else:
            value = sum(dot(e, half, NT) for e, half in parts)
            out = (gti, gti, gti, gto, gtl, gsi, gsi, gsi, gso, gfe, gfe, gfe, gfe)[c]
            t = (0, 1, 2, 0, 0, 0, 1, 2, 0, 0, 1, 2, 3)[c]
            out[:, 96 * t:96 * t + 96] = value
    me = lax.axis_index("seq")
    for s in range(8):
        @pl.when(me == s)
        def _():
            for r, o in ((TG, tg_o), (TS, ts_o), (TOB, tob_o), (TLB, tlb_o), (SG, sg_o), (SS, ss_o), (SOB, sob_o), (FG, fg_o),
                         (FS, fs_o), (FRB, frb_o)):
                o[...] = vec[r, 96 * s:96 * s + 96]
            for r, o in ((TIB, tib_o), (SIB, sib_o)):
                o[...] = vec[r + s // 4, 192 * (s % 4):192 * (s % 4) + 192]
            t, lane = FEB + 2 * (s % 2), 192 * (s // 2)
            feb_o[...] = jnp.concatenate([vec[t:t + 1, lane:lane + 192], vec[t + 1:t + 2, lane:lane + 192]], axis=1).reshape(384)


def on_device_fast(
    tokens, cotangent, frame_clip, frame_valid, place_valid,
    time_gain, time_shift, time_inward, time_inward_bias, time_outward, time_outward_bias, time_linear, time_linear_bias,
    space_gain, space_shift, space_inward, space_inward_bias, space_outward, space_outward_bias,
    feed_gain, feed_shift, feed_expand, feed_expand_bias, feed_reduce, feed_reduce_bias,
):
    vectors = jnp.concatenate([
        time_gain, time_shift, time_outward_bias, time_linear_bias, space_gain, space_shift, space_outward_bias, feed_gain,
        feed_shift, feed_reduce_bias, time_inward_bias, space_inward_bias, feed_expand_bias])
    vin = jnp.pad(vectors.reshape(18, 96), ((0, 6), (0, 32)))
    shaped, vmem = jax.ShapeDtypeStruct, pltpu.VMEM
    rows_bf, rows_f32 = vmem((1024, 768), BF), vmem((1024, 768), F32)
    by_frame, by_place = vmem((4, 32, 8, 768), BF), vmem((32, 4, 8, 768), BF)
    row_block, selector = vmem((SLOTS, 96, 768), BF), vmem((192, 128), BF)
    n = CHUNKS * 20 + 14 + 28 + 56 + 6
    parameters = (
        time_gain, time_shift, time_inward, time_inward_bias, time_outward, time_outward_bias, time_linear, time_linear_bias,
        space_gain, space_shift, space_inward, space_inward_bias, space_outward, space_outward_bias,
        feed_gain, feed_shift, feed_expand, feed_expand_bias, feed_reduce, feed_reduce_bias)
    outs = pl.pallas_call(
        layer_kernel,
        out_shape=(
            shaped((1024, 768), BF), shaped((1024, 768), F32), shaped((CHUNKS, 144, 128), F32), shaped((24, 768), F32),
            shaped((1024, 2304), BF), shaped((1024, 768), BF), shaped((1024, 768), BF), shaped((1024, 768), F32),
            shaped((32, 4, 8, 768), BF)),
        in_specs=[ANY, ANY] + [VM] * 11,
        out_specs=(ANY, ANY, ANY, VM) + (ANY,) * 5,
        scratch_shapes=[
            vmem((WROWS, 768), BF), vmem((4, CHUNKS, 144, 128), BF), vmem((8, 24, 128), F32), vmem((24, 768), F32),
            selector, selector, selector, vmem((256, 256), F32), vmem((4, 256, 1), F32),
            by_frame, by_frame, by_place, by_place, rows_bf, rows_bf, vmem((1024, 2304), BF), rows_f32, rows_f32, rows_f32,
            rows_bf, rows_bf, rows_bf,
            vmem((SLOTS, 4, 96, 768), BF), row_block, vmem((EARLY_SLOTS, 96, 768), BF), row_block, vmem((SLOTS, 4, 144, 128), BF),
            vmem((SLOTS, 3, 144, 128), BF), vmem((SLOTS, 144, 128), F32), vmem((4, 24, 768), F32), vmem((7, 24, 768), F32), vmem((96, 256), F32),
            pltpu.SemaphoreType.DMA((44,)), pltpu.SemaphoreType.DMA((n,)), pltpu.SemaphoreType.DMA((n,))],
        compiler_params=pltpu.CompilerParams(collective_id=0, has_side_effects=True, vmem_limit_bytes=LIMIT),
    )(tokens.reshape(4, 32, 8, 768), cotangent.reshape(1024, 768), frame_clip.reshape(1, 32), frame_valid.reshape(1, 32),
      place_valid, vin, time_inward, time_outward, time_linear, space_inward, space_outward, feed_expand, feed_reduce.T)
    shapes = [shaped(p.shape, F32) for p in parameters]
    shapes[18] = shaped(feed_reduce.T.shape, F32)
    outs = list(pl.pallas_call(
        hand_over, out_shape=(shaped((1024, 768), BF), shaped((1024, 768), F32)) + tuple(shapes),
        in_specs=[VM] * 4, out_specs=(VM,) * 22, scratch_shapes=[selector] * 3,
        compiler_params=pltpu.CompilerParams(vmem_limit_bytes=32 << 20))(*outs[:4]))
    outs[20] = outs[20].T
    return (outs[0].reshape(tokens.shape), outs[1].reshape(tokens.shape)) + tuple(outs[2:])


HEADS = 12


def normalize(inputs, scaling, offset):
    average = jnp.mean(inputs, axis=-1, keepdims=True)
    centered = inputs - average
    variance = jnp.mean(centered * centered, axis=-1, keepdims=True)
    return centered * lax.rsqrt(variance + EPSILON) * scaling + offset


def gelu_exact(inputs):
    return jax.nn.gelu(inputs, approximate=False)


def matmul(former, latter):
    return jnp.dot(former, latter, preferred_element_type=jnp.float32)


def inner(former, latter):
    return lax.dot_general(
        former, latter, (((0,), (0,)), ((), ())), preferred_element_type=jnp.float32
    )


def against(former, latter):
    return lax.dot_general(
        former, latter, (((1,), (1,)), ((), ())), preferred_element_type=jnp.float32
    )


def column_sum(delta_rows):
    return jnp.sum(delta_rows, axis=0, dtype=jnp.float32)


def packed_sum(joined_grad):
    totals = jnp.sum(joined_grad, axis=0, dtype=jnp.float32)
    model_width = totals.shape[0] // 3
    return jnp.concatenate([totals[:model_width], totals[2 * model_width :]])


def patterns(flavor):
    if flavor == "time":
        return ("fphd,gphd->phfg", "phfg,gphd->fphd", "phfg,fphd->gphd")
    return ("fphd,fqhd->fhpq", "fhpq,fqhd->fphd", "fhpq,fphd->fqhd")


def project_in_general(normed_low, weight, packed_bias, leading, head_count):
    model_width = normed_low.shape[-1]
    full_bias = jnp.concatenate(
        [
            packed_bias[:model_width],
            jnp.zeros((model_width,), jnp.float32),
            packed_bias[model_width:],
        ]
    )
    joined = (matmul(normed_low, weight) + full_bias).astype(jnp.bfloat16)
    shaped = joined.reshape(leading + (3, head_count, model_width // head_count))
    return (shaped[:, :, 0], shaped[:, :, 1], shaped[:, :, 2])


def attend(queries, keys_in, values, allowed, flavor):
    score_form, mix_form, spare_form = patterns(flavor)
    factor = queries.shape[-1] ** (-0.5)
    scores = jnp.einsum(score_form, queries, keys_in, preferred_element_type=jnp.float32) * factor
    masked = jnp.where(allowed, scores, -1e30)
    highest = jnp.max(masked, axis=-1, keepdims=True)
    raised = jnp.exp(masked - highest)
    summed = jnp.sum(raised, axis=-1, keepdims=True)
    chances = (raised / summed).astype(jnp.bfloat16)
    mixed = jnp.einsum(mix_form, chances, values, preferred_element_type=jnp.float32)
    return (mixed, highest + jnp.log(summed))


def attend_back(queries, keys_in, values, log_total, allowed, upstream, flavor):
    score_form, mix_form, spare_form = patterns(flavor)
    factor = queries.shape[-1] ** (-0.5)
    scores = jnp.einsum(score_form, queries, keys_in, preferred_element_type=jnp.float32) * factor
    chances = jnp.exp(jnp.where(allowed, scores, -1e30) - log_total)
    value_grad = jnp.einsum(
        spare_form, chances.astype(jnp.bfloat16), upstream, preferred_element_type=jnp.float32
    )
    chance_grad = jnp.einsum(score_form, upstream, values, preferred_element_type=jnp.float32)
    score_grad = (
        chances * (chance_grad - jnp.sum(chance_grad * chances, axis=-1, keepdims=True))
    ).astype(jnp.bfloat16)
    query_grad = (
        jnp.einsum(mix_form, score_grad, keys_in, preferred_element_type=jnp.float32) * factor
    )
    key_grad = (
        jnp.einsum(spare_form, score_grad, queries, preferred_element_type=jnp.float32) * factor
    )
    joined = jnp.stack([query_grad, key_grad, value_grad], axis=2)
    return joined.reshape(-1, 3 * joined.shape[-1] * joined.shape[-2]).astype(jnp.bfloat16)


def on_device_general(
    tokens,
    cotangent,
    frame_clip,
    frame_valid,
    place_valid,
    time_gain,
    time_shift,
    time_inward,
    time_inward_bias,
    time_outward,
    time_outward_bias,
    time_linear,
    time_linear_bias,
    space_gain,
    space_shift,
    space_inward,
    space_inward_bias,
    space_outward,
    space_outward_bias,
    feed_gain,
    feed_shift,
    feed_expand,
    feed_expand_bias,
    feed_reduce,
    feed_reduce_bias,
):
    frames_dev, places, model_width = tokens.shape
    head_count = HEADS
    group_frames = frame_clip.shape[0]
    clip_count = place_valid.shape[0]
    place_dev = places // lax.axis_size("seq")
    rows_part = (
        lax.all_gather(time_inward.astype(jnp.bfloat16), "grp", axis=0, tiled=True),
        lax.all_gather(time_outward.astype(jnp.bfloat16), "grp", axis=0, tiled=True),
        lax.all_gather(time_linear.astype(jnp.bfloat16), "grp", axis=0, tiled=True),
        lax.all_gather(space_inward.astype(jnp.bfloat16), "grp", axis=0, tiled=True),
        lax.all_gather(space_outward.astype(jnp.bfloat16), "grp", axis=0, tiled=True),
        lax.all_gather(feed_expand.astype(jnp.bfloat16), "grp", axis=0, tiled=True),
        lax.all_gather(feed_reduce.astype(jnp.bfloat16), "grp", axis=0, tiled=True),
    )
    gathered = (
        lax.all_gather(rows_part[0], "seq", axis=1, tiled=True),
        lax.all_gather(rows_part[1], "seq", axis=1, tiled=True),
        lax.all_gather(rows_part[2], "seq", axis=1, tiled=True),
        lax.all_gather(rows_part[3], "seq", axis=1, tiled=True),
        lax.all_gather(rows_part[4], "seq", axis=1, tiled=True),
        lax.all_gather(rows_part[5], "seq", axis=1, tiled=True),
        lax.all_gather(rows_part[6], "seq", axis=1, tiled=True),
        lax.all_gather(time_gain.astype(jnp.bfloat16), "seq", axis=0, tiled=True),
        lax.all_gather(time_shift.astype(jnp.bfloat16), "seq", axis=0, tiled=True),
        lax.all_gather(time_inward_bias.astype(jnp.bfloat16), "seq", axis=0, tiled=True),
        lax.all_gather(time_outward_bias.astype(jnp.bfloat16), "seq", axis=0, tiled=True),
        lax.all_gather(time_linear_bias.astype(jnp.bfloat16), "seq", axis=0, tiled=True),
        lax.all_gather(space_gain.astype(jnp.bfloat16), "seq", axis=0, tiled=True),
        lax.all_gather(space_shift.astype(jnp.bfloat16), "seq", axis=0, tiled=True),
        lax.all_gather(space_inward_bias.astype(jnp.bfloat16), "seq", axis=0, tiled=True),
        lax.all_gather(space_outward_bias.astype(jnp.bfloat16), "seq", axis=0, tiled=True),
        lax.all_gather(feed_gain.astype(jnp.bfloat16), "seq", axis=0, tiled=True),
        lax.all_gather(feed_shift.astype(jnp.bfloat16), "seq", axis=0, tiled=True),
        lax.all_gather(feed_expand_bias.astype(jnp.bfloat16), "seq", axis=0, tiled=True),
        lax.all_gather(feed_reduce_bias.astype(jnp.bfloat16), "seq", axis=0, tiled=True),
    )
    own_slot = lax.axis_index("seq")
    own_clips = lax.dynamic_slice_in_dim(frame_clip, own_slot * frames_dev, frames_dev) % clip_count
    matches = own_clips[:, None] == jnp.arange(clip_count, dtype=jnp.int32)[None, :]
    key_places = jnp.sum(jnp.where(matches[:, :, None], place_valid[None, :, :], 0), axis=1)
    space_allowed = (key_places == 1)[:, None, None, :]
    time_allowed = ((frame_clip[:, None] == frame_clip[None, :]) & (frame_valid[None, :] == 1))[
        None, None
    ]
    placed = lax.all_to_all(tokens, "seq", split_axis=1, concat_axis=0, tiled=True)
    placed_rows = placed.reshape(-1, model_width).astype(jnp.float32)
    time_normed_wide, time_norm_pull = jax.vjp(
        normalize,
        placed_rows,
        gathered[7].astype(jnp.float32),
        gathered[8].astype(jnp.float32),
    )
    time_normed = time_normed_wide.astype(jnp.bfloat16)
    time_parts = project_in_general(
        time_normed,
        gathered[0],
        gathered[9].astype(jnp.float32),
        (group_frames, place_dev),
        head_count,
    )
    time_mixed, time_total = attend(
        time_parts[0], time_parts[1], time_parts[2], time_allowed, "time"
    )
    time_mixed_low = time_mixed.reshape(-1, model_width).astype(jnp.bfloat16)
    time_proj = (
        matmul(time_mixed_low, gathered[1]) + gathered[10].astype(jnp.float32)
    ).astype(jnp.bfloat16)
    returned = lax.all_to_all(
        time_proj.reshape(group_frames, place_dev, model_width),
        "seq",
        split_axis=0,
        concat_axis=1,
        tiled=True,
    )
    returned_rows = returned.reshape(-1, model_width)
    first_sum = (
        tokens.reshape(-1, model_width).astype(jnp.float32)
        + matmul(returned_rows, gathered[2])
        + gathered[11].astype(jnp.float32)
    )
    space_normed_wide, space_norm_pull = jax.vjp(
        normalize,
        first_sum,
        gathered[12].astype(jnp.float32),
        gathered[13].astype(jnp.float32),
    )
    space_normed = space_normed_wide.astype(jnp.bfloat16)
    space_parts = project_in_general(
        space_normed,
        gathered[3],
        gathered[14].astype(jnp.float32),
        (frames_dev, places),
        head_count,
    )
    space_mixed, space_total = attend(
        space_parts[0], space_parts[1], space_parts[2], space_allowed, "space"
    )
    space_mixed_low = space_mixed.reshape(-1, model_width).astype(jnp.bfloat16)
    second_sum = (
        first_sum
        + matmul(space_mixed_low, gathered[4])
        + gathered[15].astype(jnp.float32)
    )
    feed_normed_wide, feed_norm_pull = jax.vjp(
        normalize,
        second_sum,
        gathered[16].astype(jnp.float32),
        gathered[17].astype(jnp.float32),
    )
    feed_normed = feed_normed_wide.astype(jnp.bfloat16)
    hidden = matmul(feed_normed, gathered[5]) + gathered[18].astype(jnp.float32)
    activated_wide, gelu_pull = jax.vjp(gelu_exact, hidden)
    activated = activated_wide.astype(jnp.bfloat16)
    final_sum = (
        second_sum
        + matmul(activated, gathered[6])
        + gathered[19].astype(jnp.float32)
    )
    result = final_sum.astype(jnp.bfloat16).reshape(tokens.shape)
    rows_again = (
        lax.all_gather(time_inward.astype(jnp.bfloat16), "grp", axis=0, tiled=True),
        lax.all_gather(time_outward.astype(jnp.bfloat16), "grp", axis=0, tiled=True),
        lax.all_gather(time_linear.astype(jnp.bfloat16), "grp", axis=0, tiled=True),
        lax.all_gather(space_inward.astype(jnp.bfloat16), "grp", axis=0, tiled=True),
        lax.all_gather(space_outward.astype(jnp.bfloat16), "grp", axis=0, tiled=True),
        lax.all_gather(feed_expand.astype(jnp.bfloat16), "grp", axis=0, tiled=True),
        lax.all_gather(feed_reduce.astype(jnp.bfloat16), "grp", axis=0, tiled=True),
    )
    gathered_again = (
        lax.all_gather(rows_again[0], "seq", axis=1, tiled=True),
        lax.all_gather(rows_again[1], "seq", axis=1, tiled=True),
        lax.all_gather(rows_again[2], "seq", axis=1, tiled=True),
        lax.all_gather(rows_again[3], "seq", axis=1, tiled=True),
        lax.all_gather(rows_again[4], "seq", axis=1, tiled=True),
        lax.all_gather(rows_again[5], "seq", axis=1, tiled=True),
        lax.all_gather(rows_again[6], "seq", axis=1, tiled=True),
        lax.all_gather(time_gain.astype(jnp.bfloat16), "seq", axis=0, tiled=True),
        lax.all_gather(time_shift.astype(jnp.bfloat16), "seq", axis=0, tiled=True),
        lax.all_gather(time_inward_bias.astype(jnp.bfloat16), "seq", axis=0, tiled=True),
        lax.all_gather(time_outward_bias.astype(jnp.bfloat16), "seq", axis=0, tiled=True),
        lax.all_gather(time_linear_bias.astype(jnp.bfloat16), "seq", axis=0, tiled=True),
        lax.all_gather(space_gain.astype(jnp.bfloat16), "seq", axis=0, tiled=True),
        lax.all_gather(space_shift.astype(jnp.bfloat16), "seq", axis=0, tiled=True),
        lax.all_gather(space_inward_bias.astype(jnp.bfloat16), "seq", axis=0, tiled=True),
        lax.all_gather(space_outward_bias.astype(jnp.bfloat16), "seq", axis=0, tiled=True),
        lax.all_gather(feed_gain.astype(jnp.bfloat16), "seq", axis=0, tiled=True),
        lax.all_gather(feed_shift.astype(jnp.bfloat16), "seq", axis=0, tiled=True),
        lax.all_gather(feed_expand_bias.astype(jnp.bfloat16), "seq", axis=0, tiled=True),
        lax.all_gather(feed_reduce_bias.astype(jnp.bfloat16), "seq", axis=0, tiled=True),
    )
    upstream = cotangent.reshape(-1, model_width).astype(jnp.float32)
    feed_delta = cotangent.reshape(-1, model_width)
    gradient_feed_reduce = inner(activated, feed_delta)
    gradient_feed_reduce_bias = column_sum(feed_delta)
    (hidden_wide,) = gelu_pull(against(feed_delta, gathered_again[6]))
    hidden_delta = hidden_wide.astype(jnp.bfloat16)
    gradient_feed_expand = inner(feed_normed, hidden_delta)
    gradient_feed_expand_bias = column_sum(hidden_delta)
    second_back, gradient_feed_gain, gradient_feed_shift = feed_norm_pull(
        against(hidden_delta, gathered_again[5])
    )
    second_delta = upstream + second_back
    space_delta = second_delta.astype(jnp.bfloat16)
    gradient_space_outward = inner(space_mixed_low, space_delta)
    gradient_space_outward_bias = column_sum(space_delta)
    space_mixed_delta = against(space_delta, gathered_again[4]).astype(jnp.bfloat16)
    space_mixed_delta = space_mixed_delta.reshape(frames_dev, places, head_count, -1)
    space_joined = attend_back(
        space_parts[0],
        space_parts[1],
        space_parts[2],
        space_total,
        space_allowed,
        space_mixed_delta,
        "space",
    )
    gradient_space_inward = inner(space_normed, space_joined)
    gradient_space_inward_bias = packed_sum(space_joined)
    first_back, gradient_space_gain, gradient_space_shift = space_norm_pull(
        against(space_joined, gathered_again[3])
    )
    first_delta = second_delta + first_back
    linear_delta = first_delta.astype(jnp.bfloat16)
    gradient_time_linear = inner(returned_rows, linear_delta)
    gradient_time_linear_bias = column_sum(linear_delta)
    proj_delta = against(linear_delta, gathered_again[2]).astype(jnp.bfloat16)
    proj_placed = lax.all_to_all(
        proj_delta.reshape(frames_dev, places, model_width),
        "seq",
        split_axis=1,
        concat_axis=0,
        tiled=True,
    )
    proj_rows = proj_placed.reshape(-1, model_width)
    gradient_time_outward = inner(time_mixed_low, proj_rows)
    gradient_time_outward_bias = column_sum(proj_rows)
    time_mixed_delta = against(proj_rows, gathered_again[1]).astype(jnp.bfloat16)
    time_mixed_delta = time_mixed_delta.reshape(group_frames, place_dev, head_count, -1)
    time_joined = attend_back(
        time_parts[0],
        time_parts[1],
        time_parts[2],
        time_total,
        time_allowed,
        time_mixed_delta,
        "time",
    )
    gradient_time_inward = inner(time_normed, time_joined)
    gradient_time_inward_bias = packed_sum(time_joined)
    placed_back, gradient_time_gain, gradient_time_shift = time_norm_pull(
        against(time_joined, gathered_again[0])
    )
    framed_back = lax.all_to_all(
        placed_back.reshape(group_frames, place_dev, model_width).astype(jnp.bfloat16),
        "seq",
        split_axis=0,
        concat_axis=1,
        tiled=True,
    ).astype(jnp.float32)
    input_gradient = (first_delta + framed_back.reshape(-1, model_width)).reshape(tokens.shape)
    matrix_terms = (
        gradient_time_inward,
        gradient_time_outward,
        gradient_time_linear,
        gradient_space_inward,
        gradient_space_outward,
        gradient_feed_expand,
        gradient_feed_reduce,
    )
    vector_terms = (
        gradient_time_gain,
        gradient_time_shift,
        gradient_time_inward_bias,
        gradient_time_outward_bias,
        gradient_time_linear_bias,
        gradient_space_gain,
        gradient_space_shift,
        gradient_space_inward_bias,
        gradient_space_outward_bias,
        gradient_feed_gain,
        gradient_feed_shift,
        gradient_feed_expand_bias,
        gradient_feed_reduce_bias,
    )
    columns_summed = (
        lax.psum_scatter(
            matrix_terms[0].astype(jnp.bfloat16), "seq", scatter_dimension=1, tiled=True
        ).astype(jnp.float32),
        lax.psum_scatter(
            matrix_terms[1].astype(jnp.bfloat16), "seq", scatter_dimension=1, tiled=True
        ).astype(jnp.float32),
        lax.psum_scatter(
            matrix_terms[2].astype(jnp.bfloat16), "seq", scatter_dimension=1, tiled=True
        ).astype(jnp.float32),
        lax.psum_scatter(
            matrix_terms[3].astype(jnp.bfloat16), "seq", scatter_dimension=1, tiled=True
        ).astype(jnp.float32),
        lax.psum_scatter(
            matrix_terms[4].astype(jnp.bfloat16), "seq", scatter_dimension=1, tiled=True
        ).astype(jnp.float32),
        lax.psum_scatter(
            matrix_terms[5].astype(jnp.bfloat16), "seq", scatter_dimension=1, tiled=True
        ).astype(jnp.float32),
        lax.psum_scatter(
            matrix_terms[6].astype(jnp.bfloat16), "seq", scatter_dimension=1, tiled=True
        ).astype(jnp.float32),
        lax.psum_scatter(
            vector_terms[0].astype(jnp.bfloat16), "seq", scatter_dimension=0, tiled=True
        ).astype(jnp.float32),
        lax.psum_scatter(
            vector_terms[1].astype(jnp.bfloat16), "seq", scatter_dimension=0, tiled=True
        ).astype(jnp.float32),
        lax.psum_scatter(
            vector_terms[2].astype(jnp.bfloat16), "seq", scatter_dimension=0, tiled=True
        ).astype(jnp.float32),
        lax.psum_scatter(
            vector_terms[3].astype(jnp.bfloat16), "seq", scatter_dimension=0, tiled=True
        ).astype(jnp.float32),
        lax.psum_scatter(
            vector_terms[4].astype(jnp.bfloat16), "seq", scatter_dimension=0, tiled=True
        ).astype(jnp.float32),
        lax.psum_scatter(
            vector_terms[5].astype(jnp.bfloat16), "seq", scatter_dimension=0, tiled=True
        ).astype(jnp.float32),
        lax.psum_scatter(
            vector_terms[6].astype(jnp.bfloat16), "seq", scatter_dimension=0, tiled=True
        ).astype(jnp.float32),
        lax.psum_scatter(
            vector_terms[7].astype(jnp.bfloat16), "seq", scatter_dimension=0, tiled=True
        ).astype(jnp.float32),
        lax.psum_scatter(
            vector_terms[8].astype(jnp.bfloat16), "seq", scatter_dimension=0, tiled=True
        ).astype(jnp.float32),
        lax.psum_scatter(
            vector_terms[9].astype(jnp.bfloat16), "seq", scatter_dimension=0, tiled=True
        ).astype(jnp.float32),
        lax.psum_scatter(
            vector_terms[10].astype(jnp.bfloat16), "seq", scatter_dimension=0, tiled=True
        ).astype(jnp.float32),
        lax.psum_scatter(
            vector_terms[11].astype(jnp.bfloat16), "seq", scatter_dimension=0, tiled=True
        ).astype(jnp.float32),
        lax.psum_scatter(
            vector_terms[12].astype(jnp.bfloat16), "seq", scatter_dimension=0, tiled=True
        ).astype(jnp.float32),
    )
    rows_summed = (
        lax.psum_scatter(
            columns_summed[0].astype(jnp.bfloat16), "grp", scatter_dimension=0, tiled=True
        ).astype(jnp.float32),
        lax.psum_scatter(
            columns_summed[1].astype(jnp.bfloat16), "grp", scatter_dimension=0, tiled=True
        ).astype(jnp.float32),
        lax.psum_scatter(
            columns_summed[2].astype(jnp.bfloat16), "grp", scatter_dimension=0, tiled=True
        ).astype(jnp.float32),
        lax.psum_scatter(
            columns_summed[3].astype(jnp.bfloat16), "grp", scatter_dimension=0, tiled=True
        ).astype(jnp.float32),
        lax.psum_scatter(
            columns_summed[4].astype(jnp.bfloat16), "grp", scatter_dimension=0, tiled=True
        ).astype(jnp.float32),
        lax.psum_scatter(
            columns_summed[5].astype(jnp.bfloat16), "grp", scatter_dimension=0, tiled=True
        ).astype(jnp.float32),
        lax.psum_scatter(
            columns_summed[6].astype(jnp.bfloat16), "grp", scatter_dimension=0, tiled=True
        ).astype(jnp.float32),
    )
    vector_shares = tuple(columns_summed[7:])
    vectors_summed = lax.psum(
        (
            vector_shares[0],
            vector_shares[1],
            vector_shares[2],
            vector_shares[3],
            vector_shares[4],
            vector_shares[5],
            vector_shares[6],
            vector_shares[7],
            vector_shares[8],
            vector_shares[9],
            vector_shares[10],
            vector_shares[11],
            vector_shares[12],
        ),
        "grp",
    )
    owned = tuple(rows_summed) + tuple(vectors_summed)
    return (result, input_gradient) + tuple(owned[i] for i in (7, 8, 0, 9, 1, 10, 2, 11, 12, 13, 3, 14, 4, 15, 16, 17, 5, 18, 6, 19))


def solution(mesh):
    fast = mesh.shape["grp"] == 4 and mesh.shape["seq"] == 8
    return jax.shard_map(
        on_device_fast if fast else on_device_general,
        mesh=mesh,
        in_specs=(
            P(("grp", "seq"), None, None),
            P(("grp", "seq"), None, None),
            P("grp"),
            P("grp"),
            P("grp", None),
            P("seq"),
            P("seq"),
            P("grp", "seq"),
            P("seq"),
            P("grp", "seq"),
            P("seq"),
            P("grp", "seq"),
            P("seq"),
            P("seq"),
            P("seq"),
            P("grp", "seq"),
            P("seq"),
            P("grp", "seq"),
            P("seq"),
            P("seq"),
            P("seq"),
            P("grp", "seq"),
            P("seq"),
            P("grp", "seq"),
            P("seq"),
        ),
        out_specs=(
            P(("grp", "seq"), None, None),
            P(("grp", "seq"), None, None),
            P("seq"),
            P("seq"),
            P("grp", "seq"),
            P("seq"),
            P("grp", "seq"),
            P("seq"),
            P("grp", "seq"),
            P("seq"),
            P("seq"),
            P("seq"),
            P("grp", "seq"),
            P("seq"),
            P("grp", "seq"),
            P("seq"),
            P("seq"),
            P("seq"),
            P("grp", "seq"),
            P("seq"),
            P("grp", "seq"),
            P("seq"),
        ),
        check_vma=False,
    )
```

```python
import jax
import jax.numpy as jnp
from jax import lax
from jax.experimental import pallas as pl
from jax.experimental.pallas import tpu as pltpu
from jax.sharding import PartitionSpec as P

MESH = pl.DeviceIdType.MESH
BF = jnp.bfloat16
F32 = jnp.float32
NN = (((1,), (0,)), ((), ()))
NT = (((1,), (1,)), ((), ()))
TN = (((0,), (0,)), ((), ()))

TI, TO, TL, SI, SO, FE, FR = 0, 2304, 3072, 3840, 6144, 6912, 9984
WROWS = 13056
BASE = ([96 * t for t in range(3)] + [TO, TL] + [SI + 96 * t for t in range(3)] + [SO]
        + [FE + 768 * (v // 2) + 96 * (v % 2) for v in range(4)] + [FR + 768 * t for t in range(4)])
PAIR = [576] * 3 + [192] * 2 + [576] * 3 + [192] + [192] * 4 + [192] * 4
CORE = [288] * 3 + [96] * 2 + [288] * 3 + [96] + [1536] * 4 + [96] * 4
CHUNKS = 17
GATHER_ORDER = [0, 1, 2, 3, 4, 5, 6, 7, 8, 9, 10, 13, 15, 11, 12, 14, 16]
SLOTS = 5
EARLY_SLOTS = 8
LAGS = (2, 3, 3, 3)
GATHER_LAGS = (3, 5, 3)
SPACING = 1
KINDS = ("p", "q", "so", "d", "sp", "sq", "sd")
EPSILON = 1e-06


def dot(a, b, dims):
    return lax.dot_general(a, b, dims, preferred_element_type=F32)


class Links:
    def __init__(self, send_sem, recv_sem):
        self.send_sem, self.recv_sem = send_sem, recv_sem
        self.copies, self.used, self.sent = {}, 0, set()
        self.z = lax.axis_index("grp")
        s = self.s = lax.axis_index("seq")
        core, x, y = s % 2, (s // 2) % 2, s // 4
        xn, yn = s + 2 - 4 * x, s + 4 - 8 * y
        self.core = core
        self.sib = s + 1 - 2 * core
        self.p = yn * (1 - core) + xn * core
        self.q = xn * (1 - core) + yn * core
        self.d = xn + yn - s

    def zpeer(self, k):
        return (self.z + k) % 4

    def speer(self, k):
        return (self.s + k) % 8

    def greet(self):
        bar = pltpu.get_barrier_semaphore()
        for k in range(1, 8):
            pl.semaphore_signal(bar, inc=1, device_id=(self.z, self.speer(k)), device_id_type=MESH)
        for k in range(1, 4):
            pl.semaphore_signal(bar, inc=1, device_id=(self.zpeer(k), self.s), device_id_type=MESH)

    def greeted(self):
        pl.semaphore_wait(pltpu.get_barrier_semaphore(), 10)

    def send(self, key, src, dst, device):
        i = self.used
        self.used += 1
        copy = pltpu.make_async_remote_copy(
            src_ref=src, dst_ref=dst, send_sem=self.send_sem.at[i], recv_sem=self.recv_sem.at[i],
            device_id=device, device_id_type=MESH)
        copy.start()
        self.copies[key] = copy

    def sends(self, key, src, dst, seq):
        self.send(key, src, dst, (self.z, seq))

    def sendz(self, key, src, dst, z):
        self.send(key, src, dst, (z, self.s))

    def got(self, *keys):
        for key in keys:
            self.copies[key].wait_recv()

    def gone(self, *keys):
        for key in keys:
            if key not in self.sent:
                self.sent.add(key)
                self.copies[key].wait_send()

    def drain(self):
        self.gone(*self.copies)


class Local:
    def __init__(self, sem):
        self.sem, self.used, self.copies = sem, 0, {}

    def start(self, key, src, dst):
        copy = pltpu.make_async_copy(src, dst, self.sem.at[self.used])
        self.used += 1
        copy.start()
        self.copies[key] = copy

    def wait(self, *keys):
        for key in keys:
            copy = self.copies.pop(key, None)
            if copy is not None:
                copy.wait()

    def drain(self):
        self.wait(*list(self.copies))


def place(c, s):
    return pl.ds(pl.multiple_of(BASE[c] + PAIR[c] * (s // 2) + CORE[c] * (s % 2), 32), 96)


def block(ref, c, s):
    return ref.at[place(c, s)]


class Gather:
    def __init__(self, links, zst, w):
        self.l, self.zst, self.w = links, zst, w
        self.next, self.flight, self.zsent, self.clock = 0, [], 0, 0

    def zsend(self, count=1):
        for i in range(self.zsent, min(self.zsent + count, CHUNKS)):
            c = GATHER_ORDER[i]
            own = self.zst.at[self.l.z, c]
            for k in range(1, 4):
                self.l.sendz(("zg", c, k), own, own, self.l.zpeer(k))
            self.zsent += 1

    def sources(self, *chunks):
        self.l.gone(*[(k, c) for c in chunks for k in KINDS])

    def step_a(self, i, c):
        l = self.l
        l.got(*[("zg", c, k) for k in range(1, 4)])
        rows = place(c, l.s)
        zst, w = self.zst, self.w
        for half in range(2):
            lo, hi = zst[2 * half, c], zst[2 * half + 1, c]
            w[rows, 384 * half:384 * half + 128] = lo[:96]
            w[rows, 384 * half + 256:384 * half + 384] = hi[:96]
            blo, bhi = lo[96:], hi[96:]
            w[rows, 384 * half + 128:384 * half + 256] = jnp.concatenate([
                jnp.concatenate([blo[:, :64], bhi[:, :64]], axis=1),
                jnp.concatenate([blo[:, 64:], bhi[:, 64:]], axis=1)], axis=0)
        own = block(w, c, l.s)
        l.sends(("p", c), own, own, l.p)
        l.sends(("q", c), own, own, l.q)
        l.sends(("so", c), own, own, l.sib)
        self.zsend()

    def step_b(self, i, c):
        l = self.l
        l.got(("p", c))
        bp = block(self.w, c, l.p)
        l.sends(("d", c), bp, bp, l.q)
        l.sends(("sp", c), bp, bp, l.sib)
        l.got(("q", c))
        bq = block(self.w, c, l.q)
        l.sends(("sq", c), bq, bq, l.sib)

    def step_c(self, i, c):
        l = self.l
        l.got(("d", c))
        bd = block(self.w, c, l.d)
        l.sends(("sd", c), bd, bd, l.sib)

    def step_d(self, i, c):
        self.l.got(("so", c), ("sp", c), ("sq", c), ("sd", c))

    def tick(self, push=True, whole=-1):
        steps = (self.step_b, self.step_c, self.step_d)
        self.clock += 1
        fresh = []
        if push and self.next < CHUNKS:
            self.step_a(self.next, GATHER_ORDER[self.next])
            fresh = [(self.next, 0, self.clock + GATHER_LAGS[0])]
            self.next += 1
        later = []
        for i, k, due in self.flight:
            if i <= whole or self.clock >= due:
                steps[k](i, GATHER_ORDER[i])
                k, due = k + 1, self.clock + (GATHER_LAGS + (0,))[k + 1]
            if k < 3:
                later.append((i, k, due))
        self.flight = later + fresh

    def until(self, chunk):
        i = GATHER_ORDER.index(chunk)
        while i >= self.next or any(j <= i for j, _, _ in self.flight):
            self.tick(push=self.next <= i, whole=i)

    @property
    def done(self):
        return self.next == CHUNKS and not self.flight


class Scatter:
    def __init__(self, links, local, g, sr, fr, ar, br, zp, zr, ob, out):
        self.l, self.local, self.g, self.sr, self.fr, self.ar, self.br = links, local, g, sr, fr, ar, br
        self.zp, self.zr, self.ob, self.out = zp, zr, ob, out
        self.ready, self.flight, self.order = [], [], []
        self.clock, self.pushed = 0, -9

    def step_a(self, i, c):
        l = self.l
        for j in range(4):
            l.sends(("s", c, j), block(self.g, c, 2 * j + 1 - l.core), self.sr.at[i % SLOTS, j], l.sib)

    def add(self, c, s, other):
        rows = place(c, s)
        self.g[rows, :] = (self.g[rows, :].astype(F32) + other.astype(F32)).astype(BF)

    def step_b(self, i, c):
        l, k = self.l, i % SLOTS
        l.got(*[("s", c, j) for j in range(4)])
        for s, j in ((l.d, l.d // 2), (l.p, l.p // 2), (l.q, l.q // 2), (l.s, l.s // 2)):
            self.add(c, s, self.sr[k, j])
            if s is l.d:
                l.sends(("f", c), block(self.g, c, l.d), self.fr.at[k], l.p)
            if s is l.p:
                l.sends(("a", c), block(self.g, c, l.p), self.ar.at[i % EARLY_SLOTS], l.p)

    def step_c(self, i, c):
        l, k = self.l, i % SLOTS
        l.got(("f", c))
        self.add(c, l.q, self.fr[k])
        l.sends(("b", c), block(self.g, c, l.q), self.br.at[k], l.q)

    def step_d(self, i, c):
        l, k = self.l, i % SLOTS
        l.got(("a", c), ("b", c))
        rows = place(c, l.s)
        total = self.g[rows, :].astype(F32) + self.ar[i % EARLY_SLOTS].astype(F32) + self.br[k].astype(F32)
        if i >= SLOTS:
            l.gone(*[("z", self.order[i - SLOTS], j) for j in range(1, 4)])
        zp = self.zp
        for half in range(2):
            lane = 384 * half
            zp[k, 2 * half, 0:96] = total[:, lane:lane + 128].astype(BF)
            zp[k, 2 * half + 1, 0:96] = total[:, lane + 256:lane + 384].astype(BF)
            mid = total[:, lane + 128:lane + 256]
            top, low = mid[:48], mid[48:]
            zp[k, 2 * half, 96:144] = jnp.concatenate([top[:, :64], low[:, :64]], axis=1).astype(BF)
            zp[k, 2 * half + 1, 96:144] = jnp.concatenate([top[:, 64:], low[:, 64:]], axis=1).astype(BF)
        for j in range(1, 4):
            z = l.zpeer(j)
            l.sendz(("z", c, j), zp.at[k, z], self.zr.at[k, j - 1], z)

    def step_e(self, i, c):
        l, k = self.l, i % SLOTS
        l.got(*[("z", c, j) for j in range(1, 4)])
        total = self.zp[k, l.z].astype(F32)
        for j in range(3):
            total += self.zr[k, j].astype(F32)
        if i >= SLOTS:
            self.local.wait(("o", self.order[i - SLOTS]))
        self.ob[k] = total
        self.local.start(("o", c), self.ob.at[k], self.out.at[c])

    def pump(self, rush=False):
        steps = (self.step_b, self.step_c, self.step_d, self.step_e)
        self.clock += 1
        fresh = []
        if self.ready and (rush or self.clock >= self.pushed + SPACING):
            c = self.ready.pop(0)
            i = len(self.order)
            self.order.append(c)
            self.step_a(i, c)
            self.pushed = self.clock
            fresh = [(i, 0, self.clock + LAGS[0])]
        later = []
        for i, k, due in self.flight:
            if rush or self.clock >= due:
                steps[k](i, self.order[i])
                k, due = k + 1, self.clock + (LAGS + (0,))[k + 1]
            if k < 4:
                later.append((i, k, due))
        self.flight = later + fresh

    def finish(self):
        while self.ready or self.flight:
            self.pump(rush=True)


class VectorSum:
    def __init__(self, links, gv, vb):
        self.l, self.gv, self.vb = links, gv, vb

    def swap(self, i):
        l = self.l
        l.sends(("vs", i), self.gv.at[i], self.vb.at[i], (l.sib, l.p, l.q)[i])

    def join(self, i):
        self.l.got(("vs", i))
        self.gv[i + 1] = self.gv[i] + self.vb[i]

    def swapz(self):
        l = self.l
        self.vb[3 + l.z] = self.gv[3]
        for k in range(1, 4):
            l.sendz(("vz", k), self.gv.at[3], self.vb.at[3 + l.z], l.zpeer(k))

    def total(self):
        self.l.got(*[("vz", k) for k in range(1, 4)])
        return (self.vb[3] + self.vb[4]) + (self.vb[5] + self.vb[6])


TG, TS, TOB, TLB, SG, SS, SOB, FG, FS, FRB, TIB, SIB, FEB = 0, 1, 2, 3, 4, 5, 6, 7, 8, 9, 10, 12, 14


def assemble_vectors(vg, vec):
    vec[...] = jnp.zeros(vec.shape, F32)
    for s in range(8):
        piece = vg[s]
        vec[0:10, 96 * s:96 * s + 96] = piece[0:10, 0:96]
        for a in range(2):
            i = 2 * s + a
            for r in (TIB, SIB):
                vec[r + i // 8:r + i // 8 + 1, 96 * (i % 8):96 * (i % 8) + 96] = piece[r + a:r + a + 1, 0:96]
        for a in range(4):
            t, lane = 2 * (s % 2) + a // 2, 192 * (s // 2) + 96 * (a % 2)
            vec[FEB + t:FEB + 1 + t, lane:lane + 96] = piece[FEB + a:FEB + 1 + a, 0:96]


def selectors(odd, ea, el, eh):
    m = lax.broadcasted_iota(jnp.int32, (192, 128), 0)
    c = lax.broadcasted_iota(jnp.int32, (192, 128), 1)
    whole, folded = c + 64 * odd, c % 64 + 128 * (1 - odd)
    ea[...] = jnp.where(m == whole, 1.0, 0.0).astype(BF)
    both = jnp.where(m == folded, 1.0, 0.0)
    el[...] = jnp.where(c < 64, both, 0.0).astype(BF)
    eh[...] = jnp.where(c < 64, 0.0, both).astype(BF)


def standardize(x):
    centered = x - jnp.mean(x, axis=-1, keepdims=True)
    scale = lax.rsqrt(jnp.mean(centered * centered, axis=-1, keepdims=True) + EPSILON)
    return centered * scale, scale


def norm_back(e, gain, n, scale):
    u = e * gain
    return scale * (u - jnp.mean(u, axis=-1, keepdims=True) - n * jnp.mean(u * n, axis=-1, keepdims=True))


def column_sums(x):
    return jnp.sum(x, axis=0, keepdims=True)


def head_masks(scale):
    lane = lax.broadcasted_iota(jnp.int32, (1, 128), 1)
    return [jnp.where(lane < 64, scale, 0.0).astype(BF), jnp.where(lane < 64, 0.0, scale).astype(BF)]


def pair_columns(qkv, rows, p):
    c = pl.multiple_of(p * 128, 128)
    return [qkv[rows, pl.ds(768 * j + c, 128)] for j in range(3)]


def attend_block(b, qkv, mixed, lse, bias):
    rows = pl.ds(b * 256, 256)

    def pair(p):
        q, k, v = pair_columns(qkv, rows, p)
        scaled, plain = head_masks(0.125), head_masks(1.0)
        out = None
        for h in range(2):
            s = dot(k * scaled[h], q, NT) + bias()
            m = jnp.max(s, axis=0, keepdims=True)
            e = jnp.exp(s - m)
            total = jnp.sum(e, axis=0, keepdims=True)
            lse[pl.ds(b * 12 + p * 2 + h, 1), :] = m + jnp.log(total)
            o = dot((e * (1.0 / total)).astype(BF), v * plain[h], TN)
            out = o if out is None else out + o
        mixed[rows, pl.ds(pl.multiple_of(p * 128, 128), 128)] = out.astype(BF)

    def body(i, _):
        pair(2 * i)
        pair(2 * i + 1)
        return 0

    lax.fori_loop(0, 3, body, 0)


def attend_block_back(b, qkv, gm, lse, bias):
    rows = pl.ds(b * 256, 256)

    def pair(p):
        q, k, v = pair_columns(qkv, rows, p)
        c = pl.multiple_of(p * 128, 128)
        g = gm[rows, pl.ds(c, 128)]
        scaled, plain = head_masks(0.125), head_masks(1.0)
        sums = [None, None, None]
        for h in range(2):
            kh, vh, qh, gh = k * scaled[h], v * plain[h], q * scaled[h], g * plain[h]
            s = dot(kh, q, NT) + bias()
            chances = jnp.exp(s - lse[pl.ds(b * 12 + p * 2 + h, 1), :])
            back = dot(vh, g, NT)
            mean = jnp.sum(chances * back, axis=0, keepdims=True)
            gs = (chances * (back - mean)).astype(BF)
            for j, term in enumerate((dot(gs, kh, TN), dot(gs, qh, NN), dot(chances.astype(BF), gh, NN))):
                sums[j] = term if sums[j] is None else sums[j] + term
        for j in range(3):
            qkv[rows, pl.ds(768 * j + c, 128)] = sums[j].astype(BF)

    def body(i, _):
        pair(2 * i)
        pair(2 * i + 1)
        return 0

    lax.fori_loop(0, 3, body, 0)


def project_in(normed, w, at, qkv, rows, vec, bias_row):
    for j in range(3):
        part = dot(normed, w[at + 768 * j:at + 768 * (j + 1), :], NT)
        if j != 1:
            r = bias_row + j // 2
            part = part + vec[r:r + 1, :]
        qkv[rows, 768 * j:768 * (j + 1)] = part.astype(BF)


def weight_gradient(out, delta, column, rows):
    for m in range(3):
        lane = column + 256 * m
        out[256 * m:256 * m + 256, :] = dot(delta[:, lane:lane + 256], rows[...], TN).astype(BF)


def flat(x):
    return x.astype(F32).reshape(256, 768)


def tiled(x):
    return x.reshape(32, 8, 768).astype(BF)


def layer_kernel(
    tokens, cot_i, clip_i, valid_i, place_i, vin, ti_i, to_i, tl_i, si_i, so_i, fe_i, fr_i,
    result_o, grad_o, packed_o, total_o, tqkv_o, tmixed_o, ret_o, first_o, xp_o,
    w, zst, vg, vec, ea, el, eh, tmask, smask, frames_a, frames_b, places_a, places_b, nb, mixed, qkv, f1, f2, f3, act, gh, g,
    sr, fr, ar, br, zp, zr, ob, gv, vb, lse, local_sem, send_sem, recv_sem,
):
    l = Links(send_sem, recv_sem)
    l.greet()
    here = Local(local_sem)
    mine = pl.ds(4 * l.s, 4)
    xp, gpp = places_a, places_a
    pr, gb = places_b, places_b
    ret, it = frames_a, frames_a
    x, gp = frames_b, frames_b
    here.start("x", tokens, x)
    here.start("xp", tokens.at[:, mine], xp.at[mine])
    here.start("cot", cot_i, g)
    odd = l.z % 2
    selectors(odd, ea, el, eh)
    ga = Gather(l, zst, w)

    def pack(ref, chunks):
        low = ref[...].astype(BF)
        a, bl, bh = dot(low, ea[...], TN), dot(low, el[...], TN), dot(low, eh[...], TN)
        for t, c in enumerate(chunks):
            zst[l.z, c, 0:96] = a[96 * t:96 * t + 96].astype(BF)
            zst[l.z, c, 96:144] = (bl[96 * t:96 * t + 48] + bh[96 * t + 48:96 * t + 96]).astype(BF)

    def masks():
        clips, flags = clip_i[...].astype(F32), valid_i[...].astype(F32)
        row32 = lax.broadcasted_iota(jnp.int32, (256, 32), 0) // 8
        spread = jnp.where(row32 == lax.broadcasted_iota(jnp.int32, (256, 32), 1), 1.0, 0.0)
        clip_key = jnp.sum(spread * clips, axis=1, keepdims=True)
        flag_key = jnp.sum(spread * flags, axis=1, keepdims=True)
        clip_query = dot(jnp.broadcast_to(clips, (8, 32)).astype(BF), spread.astype(BF), NT)[0:1]
        j = lax.broadcasted_iota(jnp.int32, (256, 256), 0)
        i = lax.broadcasted_iota(jnp.int32, (256, 256), 1)
        allowed = (clip_key == clip_query) & (flag_key > 0.5) & (j % 8 == i % 8)
        tmask[...] = jnp.where(allowed, 0.0, -1e30)
        clip_row = lax.broadcasted_iota(jnp.int32, (4, 32), 0)
        which = jnp.where((clip_i[...] % 4) == clip_row, 1.0, 0.0)
        frame_of = lax.broadcasted_iota(jnp.int32, (32, 128), 0)
        own = jnp.where(frame_of == lax.broadcasted_iota(jnp.int32, (32, 128), 1) + 4 * l.s, 1.0, 0.0)
        chosen = dot(which.astype(BF), own.astype(BF), NN)
        open_places = dot(place_i[...].astype(F32).astype(BF), chosen.astype(BF), TN)
        for f in range(4):
            smask[f] = jnp.where(open_places[:, f:f + 1] > 0.5, 0.0, -1e30)

    pack(ti_i, [0, 1, 2])
    vg[l.s] = vin[...].astype(BF).astype(F32)
    l.greeted()
    ga.zsend(3)
    for k in range(1, 8):
        peer = l.speer(k)
        l.sends(("t", k), tokens.at[:, pl.ds(4 * peer, 4)], xp.at[mine], peer)
        l.sends(("v", k), vg.at[l.s], vg.at[l.s], peer)
    pack(to_i, [3])
    pack(tl_i, [4])
    ga.tick()
    pack(si_i, [5, 6, 7])
    ga.tick()
    pack(so_i, [8])
    pack(fe_i, [9, 10, 11, 12])
    ga.tick()
    ga.zsend(2)
    for t in range(4):
        low = fr_i[:, 192 * t:192 * t + 192].astype(BF)
        zst[l.z, 13 + t, 0:96] = dot(low, ea[...], NN).astype(BF)
        zst[l.z, 13 + t, 96:144] = (dot(low[:48], el[...], NN) + dot(low[48:], eh[...], NN)).astype(BF)
    ga.tick()
    masks()
    l.got(*[("v", k) for k in range(1, 8)])
    assemble_vectors(vg, vec)
    l.got(*[("t", k) for k in range(1, 8)])
    here.wait("x", "xp")
    here.start("xp_o", xp, xp_o)
    for b in range(4):
        rows = pl.ds(b * 256, 256)
        n, _ = standardize(flat(xp[:, b]))
        nb[rows, :] = (n * vec[TG:TG + 1, :] + vec[TS:TS + 1, :]).astype(BF)
    ga.until(2)
    for b in range(4):
        project_in(nb[256 * b:256 * b + 256, :], w, TI, qkv, pl.ds(b * 256, 256), vec, TIB)
        if b % 2:
            ga.tick()
    here.start("tqkv_o", qkv, tqkv_o)
    here.wait("xp_o")
    ga.until(3)
    for b in range(4):
        attend_block(b, qkv, mixed, lse.at[0:48], lambda: tmask[...])
        o = dot(mixed[256 * b:256 * b + 256, :], w[TO:TO + 768, :], NT) + vec[TOB:TOB + 1, :]
        pr[:, b] = tiled(o)
        ret[:, 4 * l.s + b] = pr[mine, b]
        for k in range(1, 8):
            peer = l.speer(k)
            l.sends(("r", b, k), pr.at[pl.ds(4 * peer, 4), b], ret.at[:, 4 * l.s + b], peer)
        ga.tick()
    here.start("tmixed_o", mixed, tmixed_o)
    ga.until(4)
    for b in range(4):
        l.got(*[("r", b, k) for k in range(1, 8)])
    first = second = f1
    for f in range(4):
        rows = pl.ds(256 * f, 256)
        back = flat(ret[f]).astype(BF)
        gh[rows, :] = back
        total = flat(x[f]) + dot(back, w[TL:TL + 768, :], NT) + vec[TLB:TLB + 1, :]
        first[rows, :] = total
        n, _ = standardize(total)
        nb[rows, :] = (n * vec[SG:SG + 1, :] + vec[SS:SS + 1, :]).astype(BF)
        if f == 1:
            ga.tick()
    here.start("ret_o", gh, ret_o)
    here.start("first_o", first, first_o)
    ga.until(7)
    here.wait("tqkv_o", "tmixed_o")
    for f in range(4):
        rows = pl.ds(256 * f, 256)
        project_in(nb[256 * f:256 * f + 256, :], w, SI, qkv, rows, vec, SIB)
        attend_block(f, qkv, mixed, lse.at[48:96], lambda: smask[f])
        ga.tick()
    ga.until(8)
    here.wait("first_o", "ret_o", "cot")

    final, dfn = f2, f3
    for f in range(4):
        rows = pl.ds(256 * f, 256)
        value = first[rows, :] + dot(mixed[rows, :], w[SO:SO + 768, :], NT) + vec[SOB:SOB + 1, :]
        second[rows, :] = value
        n, _ = standardize(value)
        nb[rows, :] = (n * vec[FG:FG + 1, :] + vec[FS:FS + 1, :]).astype(BF)
        final[rows, :] = value + vec[FRB:FRB + 1, :]
        dfn[rows, :] = jnp.zeros((256, 768), F32)

    sc = Scatter(l, here, w, sr, fr, ar, br, zp, zr, ob, packed_o)
    vs = VectorSum(l, gv, vb)
    sums = gv.at[0]
    sums[...] = jnp.zeros((24, 768), F32)

    def note(r, value):
        sums[r:r + 1, :] += value

    def pump():
        if not ga.done:
            ga.tick()
        sc.pump()

    for step, t in enumerate((0, 2, 1, 3)):
        ga.until(10 if t % 2 == 0 else 12)
        ga.until(13 + t)
        we, wf = w.at[FE + 768 * t:FE + 768 * (t + 1)], w.at[FR + 768 * t:FR + 768 * (t + 1)]

        def unit(b, _):
            rows = pl.ds(pl.multiple_of(256 * b, 256), 256)
            u = dot(nb[rows, :], we[...], NT) + vec[FEB + t:FEB + t + 1, :]
            phi = 0.5 + 0.5 * lax.erf(u * 0.7071067811865476)
            a = (u * phi).astype(BF)
            act[rows, :] = a
            slope = phi + u * (0.3989422804014327 * jnp.exp(-0.5 * u * u))
            h = (dot(g[rows, :], wf[...], NN) * slope).astype(BF)
            gh[rows, :] = h
            final[rows, :] += dot(a, wf[...], NT)
            dfn[rows, :] += dot(h, we[...], NN)
            sums[FEB + t:FEB + t + 1, :] += column_sums(h.astype(F32))
            return 0

        lax.fori_loop(0, 2, unit, 0)
        pump()
        lax.fori_loop(2, 4, unit, 0)
        pump()
        ga.sources(13 + t)
        weight_gradient(wf, g, 0, act)
        sc.ready.append(13 + t)
        pump()
        ga.sources(*((9, 10) if t % 2 == 0 else (11, 12)))
        weight_gradient(we, gh, 0, nb)
        if step % 2:
            sc.ready += [9, 10] if step == 1 else [11, 12]
        pump()

    ga.sources(*GATHER_ORDER)
    for f in range(4):
        rows = pl.ds(256 * f, 256)
        nb[rows, :] = final[rows, :].astype(BF)
        n, scale = standardize(second[rows, :])
        e = dfn[rows, :]
        cot = g[rows, :].astype(F32)
        note(FRB, column_sums(cot))
        note(FG, column_sums(e * n))
        note(FS, column_sums(e))
        total = cot + norm_back(e, vec[FG:FG + 1, :], n, scale)
        final[rows, :] = total
        low = total.astype(BF)
        act[rows, :] = low
        note(SOB, column_sums(low.astype(F32)))
        gh[rows, :] = dot(low, w[SO:SO + 768, :], NN).astype(BF)
        sc.pump()
    here.start("result", nb, result_o)
    here.start("first", first_o, first)
    weight_gradient(w.at[SO:SO + 768], act, 0, mixed)
    here.start("mixed2", tmixed_o, mixed)
    sc.ready.append(8)
    sc.pump()
    l.gone(*[("r", b, k) for b in range(4) for k in range(1, 8)])
    here.start("xp2", xp_o, places_b)
    here.wait("result", "first")
    for f in range(4):
        rows = pl.ds(256 * f, 256)
        attend_block_back(f, qkv, gh, lse.at[48:96], lambda: smask[f])
        sc.pump()
        n, scale = standardize(first[rows, :])
        nb[rows, :] = (n * vec[SG:SG + 1, :] + vec[SS:SS + 1, :]).astype(BF)
        joined = qkv[rows, :]
        note(SIB, column_sums(joined[:, :768].astype(F32)))
        note(SIB + 1, column_sums(joined[:, 1536:].astype(F32)))
        e = dot(joined, w[SI:SI + 2304, :], NN)
        note(SG, column_sums(e * n))
        note(SS, column_sums(e))
        total = final[rows, :] + norm_back(e, vec[SG:SG + 1, :], n, scale)
        final[rows, :] = total
        low = total.astype(BF)
        act[rows, :] = low
        note(TLB, column_sums(low.astype(F32)))
        gp[f] = tiled(dot(low, w[TL:TL + 768, :], NN))
        gpp[4 * l.s + f] = gp[f, pl.ds(4 * l.s, 4)]
        for k in range(1, 8):
            peer = l.speer(k)
            l.sends(("g", f, k), gp.at[f, pl.ds(4 * peer, 4)], gpp.at[4 * l.s + f], peer)
        sc.pump()
    here.start("ret", ret_o, gh)
    for j in range(3):
        weight_gradient(w.at[SI + 768 * j:SI + 768 * (j + 1)], qkv, 768 * j, nb)
        sc.pump()
    here.start("qkv2", tqkv_o, qkv)
    sc.ready += [5, 6, 7]
    sc.pump()
    here.wait("ret")
    weight_gradient(w.at[TL:TL + 768], act, 0, gh)
    sc.ready.append(4)
    sc.pump()

    for f in range(4):
        l.got(*[("g", f, k) for k in range(1, 8)])
    for b in range(4):
        rows = pl.ds(256 * b, 256)
        low = flat(gpp[:, b])
        note(TOB, column_sums(low))
        low = low.astype(BF)
        act[rows, :] = low
        gh[rows, :] = dot(low, w[TO:TO + 768, :], NN).astype(BF)
        if b == 1:
            sc.pump()
    sc.pump()
    here.wait("mixed2")
    weight_gradient(w.at[TO:TO + 768], act, 0, mixed)
    sc.ready.append(3)
    sc.pump()
    here.wait("qkv2", "xp2")
    for b in range(4):
        rows = pl.ds(256 * b, 256)
        attend_block_back(b, qkv, gh, lse.at[0:48], lambda: tmask[...])
        sc.pump()
        n, scale = standardize(flat(places_b[:, b]))
        nb[rows, :] = (n * vec[TG:TG + 1, :] + vec[TS:TS + 1, :]).astype(BF)
        joined = qkv[rows, :]
        note(TIB, column_sums(joined[:, :768].astype(F32)))
        note(TIB + 1, column_sums(joined[:, 1536:].astype(F32)))
        e = dot(joined, w[TI:TI + 2304, :], NN)
        note(TG, column_sums(e * n))
        note(TS, column_sums(e))
        gb[:, b] = tiled(norm_back(e, vec[TG:TG + 1, :], n, scale))
        it[:, 4 * l.s + b] = gb[mine, b]
        for k in range(1, 8):
            peer = l.speer(k)
            l.sends(("h", b, k), gb.at[pl.ds(4 * peer, 4), b], it.at[:, 4 * l.s + b], peer)
        sc.pump()
    for j in range(3):
        weight_gradient(w.at[TI + 768 * j:TI + 768 * (j + 1)], qkv, 768 * j, nb)
        sc.pump()
    sc.ready += [0, 1, 2]
    for i in range(3):
        vs.swap(i)
        sc.pump(rush=True)
        vs.join(i)
    vs.swapz()
    for b in range(4):
        l.got(*[("h", b, k) for k in range(1, 8)])
    for f in range(4):
        rows = pl.ds(256 * f, 256)
        final[rows, :] += flat(it[f])
    here.start("grad", final, grad_o)
    sc.pump(rush=True)
    total_o[...] = vs.total()
    sc.finish()
    l.drain()
    here.drain()


LIMIT = 63 << 20
VM = pl.BlockSpec(memory_space=pltpu.VMEM)
ANY = pl.BlockSpec(memory_space=pl.ANY)


def hand_over(
    result_i, grad_i, packed_i, vec_i,
    result_o, grad_o, tg_o, ts_o, gti, tib_o, gto, tob_o, gtl, tlb_o, sg_o, ss_o, gsi, sib_o, gso, sob_o, fg_o, fs_o, gfe, feb_o,
    gfr, frb_o, ea, el, eh, packed, vec, sem,
):
    pairs = ((packed_i, packed), (vec_i, vec), (result_i, result_o), (grad_i, grad_o))
    copies = [pltpu.make_async_copy(src, dst, sem.at[i]) for i, (src, dst) in enumerate(pairs)]
    for copy in copies:
        copy.start()
    selectors(lax.axis_index("grp") % 2, ea, el, eh)
    copies[0].wait()
    for c in range(CHUNKS):
        total = packed[c]
        a, folded = total[:96], total[96:]
        lane = lax.broadcasted_iota(jnp.int32, (48, 128), 1)
        b = jnp.concatenate([jnp.where(lane < 64, folded, 0.0), jnp.where(lane < 64, 0.0, folded)], axis=0)
        eb = el[...] + eh[...]
        a_high, b_high = a.astype(BF), b.astype(BF)
        parts = ((ea[...], a_high), (eb, b_high), (ea[...], (a - a_high.astype(F32)).astype(BF)),
                 (eb, (b - b_high.astype(F32)).astype(BF)))
        if c >= 13:
            value = sum(dot(half, e, NT) for e, half in parts)
            gfr[:, 192 * (c - 13):192 * (c - 12)] = value
        else:
            value = sum(dot(e, half, NT) for e, half in parts)
            out = (gti, gti, gti, gto, gtl, gsi, gsi, gsi, gso, gfe, gfe, gfe, gfe)[c]
            t = (0, 1, 2, 0, 0, 0, 1, 2, 0, 0, 1, 2, 3)[c]
            out[:, 96 * t:96 * t + 96] = value
    me = lax.axis_index("seq")
    for copy in copies[1:]:
        copy.wait()
    for s in range(8):
        @pl.when(me == s)
        def _():
            for r, o in ((TG, tg_o), (TS, ts_o), (TOB, tob_o), (TLB, tlb_o), (SG, sg_o), (SS, ss_o), (SOB, sob_o), (FG, fg_o),
                         (FS, fs_o), (FRB, frb_o)):
                o[...] = vec[r, 96 * s:96 * s + 96]
            for r, o in ((TIB, tib_o), (SIB, sib_o)):
                o[...] = vec[r + s // 4, 192 * (s % 4):192 * (s % 4) + 192]
            t, lane = FEB + 2 * (s % 2), 192 * (s // 2)
            feb_o[...] = jnp.concatenate([vec[t:t + 1, lane:lane + 192], vec[t + 1:t + 2, lane:lane + 192]], axis=1).reshape(384)


def on_device_fast(
    tokens, cotangent, frame_clip, frame_valid, place_valid,
    time_gain, time_shift, time_inward, time_inward_bias, time_outward, time_outward_bias, time_linear, time_linear_bias,
    space_gain, space_shift, space_inward, space_inward_bias, space_outward, space_outward_bias,
    feed_gain, feed_shift, feed_expand, feed_expand_bias, feed_reduce, feed_reduce_bias,
):
    vectors = jnp.concatenate([
        time_gain, time_shift, time_outward_bias, time_linear_bias, space_gain, space_shift, space_outward_bias, feed_gain,
        feed_shift, feed_reduce_bias, time_inward_bias, space_inward_bias, feed_expand_bias])
    vin = jnp.pad(vectors.reshape(18, 96), ((0, 6), (0, 32)))
    shaped, vmem = jax.ShapeDtypeStruct, pltpu.VMEM
    rows_bf, rows_f32 = vmem((1024, 768), BF), vmem((1024, 768), F32)
    by_frame, by_place = vmem((4, 32, 8, 768), BF), vmem((32, 4, 8, 768), BF)
    row_block, selector = vmem((SLOTS, 96, 768), BF), vmem((192, 128), BF)
    n = CHUNKS * 20 + 14 + 28 + 56 + 6
    parameters = (
        time_gain, time_shift, time_inward, time_inward_bias, time_outward, time_outward_bias, time_linear, time_linear_bias,
        space_gain, space_shift, space_inward, space_inward_bias, space_outward, space_outward_bias,
        feed_gain, feed_shift, feed_expand, feed_expand_bias, feed_reduce, feed_reduce_bias)
    outs = pl.pallas_call(
        layer_kernel,
        out_shape=(
            shaped((1024, 768), BF), shaped((1024, 768), F32), shaped((CHUNKS, 144, 128), F32), shaped((24, 768), F32),
            shaped((1024, 2304), BF), shaped((1024, 768), BF), shaped((1024, 768), BF), shaped((1024, 768), F32),
            shaped((32, 4, 8, 768), BF)),
        in_specs=[ANY, ANY] + [VM] * 11,
        out_specs=(ANY, ANY, ANY, VM) + (ANY,) * 5,
        scratch_shapes=[
            vmem((WROWS, 768), BF), vmem((4, CHUNKS, 144, 128), BF), vmem((8, 24, 128), F32), vmem((24, 768), F32),
            selector, selector, selector, vmem((256, 256), F32), vmem((4, 256, 1), F32),
            by_frame, by_frame, by_place, by_place, rows_bf, rows_bf, vmem((1024, 2304), BF), rows_f32, rows_f32, rows_f32,
            rows_bf, rows_bf, rows_bf,
            vmem((SLOTS, 4, 96, 768), BF), row_block, vmem((EARLY_SLOTS, 96, 768), BF), row_block, vmem((SLOTS, 4, 144, 128), BF),
            vmem((SLOTS, 3, 144, 128), BF), vmem((SLOTS, 144, 128), F32), vmem((4, 24, 768), F32), vmem((7, 24, 768), F32), vmem((96, 256), F32),
            pltpu.SemaphoreType.DMA((44,)), pltpu.SemaphoreType.DMA((n,)), pltpu.SemaphoreType.DMA((n,))],
        compiler_params=pltpu.CompilerParams(collective_id=0, has_side_effects=True, vmem_limit_bytes=LIMIT),
    )(tokens.reshape(4, 32, 8, 768), cotangent.reshape(1024, 768), frame_clip.reshape(1, 32), frame_valid.reshape(1, 32),
      place_valid, vin, time_inward, time_outward, time_linear, space_inward, space_outward, feed_expand, feed_reduce.T)
    shapes = [shaped(p.shape, F32) for p in parameters]
    shapes[18] = shaped(feed_reduce.T.shape, F32)
    outs = list(pl.pallas_call(
        hand_over, out_shape=(shaped((1024, 768), BF), shaped((1024, 768), F32)) + tuple(shapes),
        in_specs=[ANY] * 4, out_specs=(VM,) * 22,
        scratch_shapes=[selector] * 3 + [vmem((CHUNKS, 144, 128), F32), vmem((24, 768), F32), pltpu.SemaphoreType.DMA((4,))],
        compiler_params=pltpu.CompilerParams(vmem_limit_bytes=32 << 20))(*outs[:4]))
    outs[20] = outs[20].T
    return (outs[0].reshape(tokens.shape), outs[1].reshape(tokens.shape)) + tuple(outs[2:])


HEADS = 12


def normalize(inputs, scaling, offset):
    average = jnp.mean(inputs, axis=-1, keepdims=True)
    centered = inputs - average
    variance = jnp.mean(centered * centered, axis=-1, keepdims=True)
    return centered * lax.rsqrt(variance + EPSILON) * scaling + offset


def gelu_exact(inputs):
    return jax.nn.gelu(inputs, approximate=False)


def matmul(former, latter):
    return jnp.dot(former, latter, preferred_element_type=jnp.float32)


def inner(former, latter):
    return lax.dot_general(
        former, latter, (((0,), (0,)), ((), ())), preferred_element_type=jnp.float32
    )


def against(former, latter):
    return lax.dot_general(
        former, latter, (((1,), (1,)), ((), ())), preferred_element_type=jnp.float32
    )


def column_sum(delta_rows):
    return jnp.sum(delta_rows, axis=0, dtype=jnp.float32)


def packed_sum(joined_grad):
    totals = jnp.sum(joined_grad, axis=0, dtype=jnp.float32)
    model_width = totals.shape[0] // 3
    return jnp.concatenate([totals[:model_width], totals[2 * model_width :]])


def patterns(flavor):
    if flavor == "time":
        return ("fphd,gphd->phfg", "phfg,gphd->fphd", "phfg,fphd->gphd")
    return ("fphd,fqhd->fhpq", "fhpq,fqhd->fphd", "fhpq,fphd->fqhd")


def project_in_general(normed_low, weight, packed_bias, leading, head_count):
    model_width = normed_low.shape[-1]
    full_bias = jnp.concatenate(
        [
            packed_bias[:model_width],
            jnp.zeros((model_width,), jnp.float32),
            packed_bias[model_width:],
        ]
    )
    joined = (matmul(normed_low, weight) + full_bias).astype(jnp.bfloat16)
    shaped = joined.reshape(leading + (3, head_count, model_width // head_count))
    return (shaped[:, :, 0], shaped[:, :, 1], shaped[:, :, 2])


def attend(queries, keys_in, values, allowed, flavor):
    score_form, mix_form, spare_form = patterns(flavor)
    factor = queries.shape[-1] ** (-0.5)
    scores = jnp.einsum(score_form, queries, keys_in, preferred_element_type=jnp.float32) * factor
    masked = jnp.where(allowed, scores, -1e30)
    highest = jnp.max(masked, axis=-1, keepdims=True)
    raised = jnp.exp(masked - highest)
    summed = jnp.sum(raised, axis=-1, keepdims=True)
    chances = (raised / summed).astype(jnp.bfloat16)
    mixed = jnp.einsum(mix_form, chances, values, preferred_element_type=jnp.float32)
    return (mixed, highest + jnp.log(summed))


def attend_back(queries, keys_in, values, log_total, allowed, upstream, flavor):
    score_form, mix_form, spare_form = patterns(flavor)
    factor = queries.shape[-1] ** (-0.5)
    scores = jnp.einsum(score_form, queries, keys_in, preferred_element_type=jnp.float32) * factor
    chances = jnp.exp(jnp.where(allowed, scores, -1e30) - log_total)
    value_grad = jnp.einsum(
        spare_form, chances.astype(jnp.bfloat16), upstream, preferred_element_type=jnp.float32
    )
    chance_grad = jnp.einsum(score_form, upstream, values, preferred_element_type=jnp.float32)
    score_grad = (
        chances * (chance_grad - jnp.sum(chance_grad * chances, axis=-1, keepdims=True))
    ).astype(jnp.bfloat16)
    query_grad = (
        jnp.einsum(mix_form, score_grad, keys_in, preferred_element_type=jnp.float32) * factor
    )
    key_grad = (
        jnp.einsum(spare_form, score_grad, queries, preferred_element_type=jnp.float32) * factor
    )
    joined = jnp.stack([query_grad, key_grad, value_grad], axis=2)
    return joined.reshape(-1, 3 * joined.shape[-1] * joined.shape[-2]).astype(jnp.bfloat16)


def on_device_general(
    tokens,
    cotangent,
    frame_clip,
    frame_valid,
    place_valid,
    time_gain,
    time_shift,
    time_inward,
    time_inward_bias,
    time_outward,
    time_outward_bias,
    time_linear,
    time_linear_bias,
    space_gain,
    space_shift,
    space_inward,
    space_inward_bias,
    space_outward,
    space_outward_bias,
    feed_gain,
    feed_shift,
    feed_expand,
    feed_expand_bias,
    feed_reduce,
    feed_reduce_bias,
):
    frames_dev, places, model_width = tokens.shape
    head_count = HEADS
    group_frames = frame_clip.shape[0]
    clip_count = place_valid.shape[0]
    place_dev = places // lax.axis_size("seq")
    rows_part = (
        lax.all_gather(time_inward.astype(jnp.bfloat16), "grp", axis=0, tiled=True),
        lax.all_gather(time_outward.astype(jnp.bfloat16), "grp", axis=0, tiled=True),
        lax.all_gather(time_linear.astype(jnp.bfloat16), "grp", axis=0, tiled=True),
        lax.all_gather(space_inward.astype(jnp.bfloat16), "grp", axis=0, tiled=True),
        lax.all_gather(space_outward.astype(jnp.bfloat16), "grp", axis=0, tiled=True),
        lax.all_gather(feed_expand.astype(jnp.bfloat16), "grp", axis=0, tiled=True),
        lax.all_gather(feed_reduce.astype(jnp.bfloat16), "grp", axis=0, tiled=True),
    )
    gathered = (
        lax.all_gather(rows_part[0], "seq", axis=1, tiled=True),
        lax.all_gather(rows_part[1], "seq", axis=1, tiled=True),
        lax.all_gather(rows_part[2], "seq", axis=1, tiled=True),
        lax.all_gather(rows_part[3], "seq", axis=1, tiled=True),
        lax.all_gather(rows_part[4], "seq", axis=1, tiled=True),
        lax.all_gather(rows_part[5], "seq", axis=1, tiled=True),
        lax.all_gather(rows_part[6], "seq", axis=1, tiled=True),
        lax.all_gather(time_gain.astype(jnp.bfloat16), "seq", axis=0, tiled=True),
        lax.all_gather(time_shift.astype(jnp.bfloat16), "seq", axis=0, tiled=True),
        lax.all_gather(time_inward_bias.astype(jnp.bfloat16), "seq", axis=0, tiled=True),
        lax.all_gather(time_outward_bias.astype(jnp.bfloat16), "seq", axis=0, tiled=True),
        lax.all_gather(time_linear_bias.astype(jnp.bfloat16), "seq", axis=0, tiled=True),
        lax.all_gather(space_gain.astype(jnp.bfloat16), "seq", axis=0, tiled=True),
        lax.all_gather(space_shift.astype(jnp.bfloat16), "seq", axis=0, tiled=True),
        lax.all_gather(space_inward_bias.astype(jnp.bfloat16), "seq", axis=0, tiled=True),
        lax.all_gather(space_outward_bias.astype(jnp.bfloat16), "seq", axis=0, tiled=True),
        lax.all_gather(feed_gain.astype(jnp.bfloat16), "seq", axis=0, tiled=True),
        lax.all_gather(feed_shift.astype(jnp.bfloat16), "seq", axis=0, tiled=True),
        lax.all_gather(feed_expand_bias.astype(jnp.bfloat16), "seq", axis=0, tiled=True),
        lax.all_gather(feed_reduce_bias.astype(jnp.bfloat16), "seq", axis=0, tiled=True),
    )
    own_slot = lax.axis_index("seq")
    own_clips = lax.dynamic_slice_in_dim(frame_clip, own_slot * frames_dev, frames_dev) % clip_count
    matches = own_clips[:, None] == jnp.arange(clip_count, dtype=jnp.int32)[None, :]
    key_places = jnp.sum(jnp.where(matches[:, :, None], place_valid[None, :, :], 0), axis=1)
    space_allowed = (key_places == 1)[:, None, None, :]
    time_allowed = ((frame_clip[:, None] == frame_clip[None, :]) & (frame_valid[None, :] == 1))[
        None, None
    ]
    placed = lax.all_to_all(tokens, "seq", split_axis=1, concat_axis=0, tiled=True)
    placed_rows = placed.reshape(-1, model_width).astype(jnp.float32)
    time_normed_wide, time_norm_pull = jax.vjp(
        normalize,
        placed_rows,
        gathered[7].astype(jnp.float32),
        gathered[8].astype(jnp.float32),
    )
    time_normed = time_normed_wide.astype(jnp.bfloat16)
    time_parts = project_in_general(
        time_normed,
        gathered[0],
        gathered[9].astype(jnp.float32),
        (group_frames, place_dev),
        head_count,
    )
    time_mixed, time_total = attend(
        time_parts[0], time_parts[1], time_parts[2], time_allowed, "time"
    )
    time_mixed_low = time_mixed.reshape(-1, model_width).astype(jnp.bfloat16)
    time_proj = (
        matmul(time_mixed_low, gathered[1]) + gathered[10].astype(jnp.float32)
    ).astype(jnp.bfloat16)
    returned = lax.all_to_all(
        time_proj.reshape(group_frames, place_dev, model_width),
        "seq",
        split_axis=0,
        concat_axis=1,
        tiled=True,
    )
    returned_rows = returned.reshape(-1, model_width)
    first_sum = (
        tokens.reshape(-1, model_width).astype(jnp.float32)
        + matmul(returned_rows, gathered[2])
        + gathered[11].astype(jnp.float32)
    )
    space_normed_wide, space_norm_pull = jax.vjp(
        normalize,
        first_sum,
        gathered[12].astype(jnp.float32),
        gathered[13].astype(jnp.float32),
    )
    space_normed = space_normed_wide.astype(jnp.bfloat16)
    space_parts = project_in_general(
        space_normed,
        gathered[3],
        gathered[14].astype(jnp.float32),
        (frames_dev, places),
        head_count,
    )
    space_mixed, space_total = attend(
        space_parts[0], space_parts[1], space_parts[2], space_allowed, "space"
    )
    space_mixed_low = space_mixed.reshape(-1, model_width).astype(jnp.bfloat16)
    second_sum = (
        first_sum
        + matmul(space_mixed_low, gathered[4])
        + gathered[15].astype(jnp.float32)
    )
    feed_normed_wide, feed_norm_pull = jax.vjp(
        normalize,
        second_sum,
        gathered[16].astype(jnp.float32),
        gathered[17].astype(jnp.float32),
    )
    feed_normed = feed_normed_wide.astype(jnp.bfloat16)
    hidden = matmul(feed_normed, gathered[5]) + gathered[18].astype(jnp.float32)
    activated_wide, gelu_pull = jax.vjp(gelu_exact, hidden)
    activated = activated_wide.astype(jnp.bfloat16)
    final_sum = (
        second_sum
        + matmul(activated, gathered[6])
        + gathered[19].astype(jnp.float32)
    )
    result = final_sum.astype(jnp.bfloat16).reshape(tokens.shape)
    rows_again = (
        lax.all_gather(time_inward.astype(jnp.bfloat16), "grp", axis=0, tiled=True),
        lax.all_gather(time_outward.astype(jnp.bfloat16), "grp", axis=0, tiled=True),
        lax.all_gather(time_linear.astype(jnp.bfloat16), "grp", axis=0, tiled=True),
        lax.all_gather(space_inward.astype(jnp.bfloat16), "grp", axis=0, tiled=True),
        lax.all_gather(space_outward.astype(jnp.bfloat16), "grp", axis=0, tiled=True),
        lax.all_gather(feed_expand.astype(jnp.bfloat16), "grp", axis=0, tiled=True),
        lax.all_gather(feed_reduce.astype(jnp.bfloat16), "grp", axis=0, tiled=True),
    )
    gathered_again = (
        lax.all_gather(rows_again[0], "seq", axis=1, tiled=True),
        lax.all_gather(rows_again[1], "seq", axis=1, tiled=True),
        lax.all_gather(rows_again[2], "seq", axis=1, tiled=True),
        lax.all_gather(rows_again[3], "seq", axis=1, tiled=True),
        lax.all_gather(rows_again[4], "seq", axis=1, tiled=True),
        lax.all_gather(rows_again[5], "seq", axis=1, tiled=True),
        lax.all_gather(rows_again[6], "seq", axis=1, tiled=True),
        lax.all_gather(time_gain.astype(jnp.bfloat16), "seq", axis=0, tiled=True),
        lax.all_gather(time_shift.astype(jnp.bfloat16), "seq", axis=0, tiled=True),
        lax.all_gather(time_inward_bias.astype(jnp.bfloat16), "seq", axis=0, tiled=True),
        lax.all_gather(time_outward_bias.astype(jnp.bfloat16), "seq", axis=0, tiled=True),
        lax.all_gather(time_linear_bias.astype(jnp.bfloat16), "seq", axis=0, tiled=True),
        lax.all_gather(space_gain.astype(jnp.bfloat16), "seq", axis=0, tiled=True),
        lax.all_gather(space_shift.astype(jnp.bfloat16), "seq", axis=0, tiled=True),
        lax.all_gather(space_inward_bias.astype(jnp.bfloat16), "seq", axis=0, tiled=True),
        lax.all_gather(space_outward_bias.astype(jnp.bfloat16), "seq", axis=0, tiled=True),
        lax.all_gather(feed_gain.astype(jnp.bfloat16), "seq", axis=0, tiled=True),
        lax.all_gather(feed_shift.astype(jnp.bfloat16), "seq", axis=0, tiled=True),
        lax.all_gather(feed_expand_bias.astype(jnp.bfloat16), "seq", axis=0, tiled=True),
        lax.all_gather(feed_reduce_bias.astype(jnp.bfloat16), "seq", axis=0, tiled=True),
    )
    upstream = cotangent.reshape(-1, model_width).astype(jnp.float32)
    feed_delta = cotangent.reshape(-1, model_width)
    gradient_feed_reduce = inner(activated, feed_delta)
    gradient_feed_reduce_bias = column_sum(feed_delta)
    (hidden_wide,) = gelu_pull(against(feed_delta, gathered_again[6]))
    hidden_delta = hidden_wide.astype(jnp.bfloat16)
    gradient_feed_expand = inner(feed_normed, hidden_delta)
    gradient_feed_expand_bias = column_sum(hidden_delta)
    second_back, gradient_feed_gain, gradient_feed_shift = feed_norm_pull(
        against(hidden_delta, gathered_again[5])
    )
    second_delta = upstream + second_back
    space_delta = second_delta.astype(jnp.bfloat16)
    gradient_space_outward = inner(space_mixed_low, space_delta)
    gradient_space_outward_bias = column_sum(space_delta)
    space_mixed_delta = against(space_delta, gathered_again[4]).astype(jnp.bfloat16)
    space_mixed_delta = space_mixed_delta.reshape(frames_dev, places, head_count, -1)
    space_joined = attend_back(
        space_parts[0],
        space_parts[1],
        space_parts[2],
        space_total,
        space_allowed,
        space_mixed_delta,
        "space",
    )
    gradient_space_inward = inner(space_normed, space_joined)
    gradient_space_inward_bias = packed_sum(space_joined)
    first_back, gradient_space_gain, gradient_space_shift = space_norm_pull(
        against(space_joined, gathered_again[3])
    )
    first_delta = second_delta + first_back
    linear_delta = first_delta.astype(jnp.bfloat16)
    gradient_time_linear = inner(returned_rows, linear_delta)
    gradient_time_linear_bias = column_sum(linear_delta)
    proj_delta = against(linear_delta, gathered_again[2]).astype(jnp.bfloat16)
    proj_placed = lax.all_to_all(
        proj_delta.reshape(frames_dev, places, model_width),
        "seq",
        split_axis=1,
        concat_axis=0,
        tiled=True,
    )
    proj_rows = proj_placed.reshape(-1, model_width)
    gradient_time_outward = inner(time_mixed_low, proj_rows)
    gradient_time_outward_bias = column_sum(proj_rows)
    time_mixed_delta = against(proj_rows, gathered_again[1]).astype(jnp.bfloat16)
    time_mixed_delta = time_mixed_delta.reshape(group_frames, place_dev, head_count, -1)
    time_joined = attend_back(
        time_parts[0],
        time_parts[1],
        time_parts[2],
        time_total,
        time_allowed,
        time_mixed_delta,
        "time",
    )
    gradient_time_inward = inner(time_normed, time_joined)
    gradient_time_inward_bias = packed_sum(time_joined)
    placed_back, gradient_time_gain, gradient_time_shift = time_norm_pull(
        against(time_joined, gathered_again[0])
    )
    framed_back = lax.all_to_all(
        placed_back.reshape(group_frames, place_dev, model_width).astype(jnp.bfloat16),
        "seq",
        split_axis=0,
        concat_axis=1,
        tiled=True,
    ).astype(jnp.float32)
    input_gradient = (first_delta + framed_back.reshape(-1, model_width)).reshape(tokens.shape)
    matrix_terms = (
        gradient_time_inward,
        gradient_time_outward,
        gradient_time_linear,
        gradient_space_inward,
        gradient_space_outward,
        gradient_feed_expand,
        gradient_feed_reduce,
    )
    vector_terms = (
        gradient_time_gain,
        gradient_time_shift,
        gradient_time_inward_bias,
        gradient_time_outward_bias,
        gradient_time_linear_bias,
        gradient_space_gain,
        gradient_space_shift,
        gradient_space_inward_bias,
        gradient_space_outward_bias,
        gradient_feed_gain,
        gradient_feed_shift,
        gradient_feed_expand_bias,
        gradient_feed_reduce_bias,
    )
    columns_summed = (
        lax.psum_scatter(
            matrix_terms[0].astype(jnp.bfloat16), "seq", scatter_dimension=1, tiled=True
        ).astype(jnp.float32),
        lax.psum_scatter(
            matrix_terms[1].astype(jnp.bfloat16), "seq", scatter_dimension=1, tiled=True
        ).astype(jnp.float32),
        lax.psum_scatter(
            matrix_terms[2].astype(jnp.bfloat16), "seq", scatter_dimension=1, tiled=True
        ).astype(jnp.float32),
        lax.psum_scatter(
            matrix_terms[3].astype(jnp.bfloat16), "seq", scatter_dimension=1, tiled=True
        ).astype(jnp.float32),
        lax.psum_scatter(
            matrix_terms[4].astype(jnp.bfloat16), "seq", scatter_dimension=1, tiled=True
        ).astype(jnp.float32),
        lax.psum_scatter(
            matrix_terms[5].astype(jnp.bfloat16), "seq", scatter_dimension=1, tiled=True
        ).astype(jnp.float32),
        lax.psum_scatter(
            matrix_terms[6].astype(jnp.bfloat16), "seq", scatter_dimension=1, tiled=True
        ).astype(jnp.float32),
        lax.psum_scatter(
            vector_terms[0].astype(jnp.bfloat16), "seq", scatter_dimension=0, tiled=True
        ).astype(jnp.float32),
        lax.psum_scatter(
            vector_terms[1].astype(jnp.bfloat16), "seq", scatter_dimension=0, tiled=True
        ).astype(jnp.float32),
        lax.psum_scatter(
            vector_terms[2].astype(jnp.bfloat16), "seq", scatter_dimension=0, tiled=True
        ).astype(jnp.float32),
        lax.psum_scatter(
            vector_terms[3].astype(jnp.bfloat16), "seq", scatter_dimension=0, tiled=True
        ).astype(jnp.float32),
        lax.psum_scatter(
            vector_terms[4].astype(jnp.bfloat16), "seq", scatter_dimension=0, tiled=True
        ).astype(jnp.float32),
        lax.psum_scatter(
            vector_terms[5].astype(jnp.bfloat16), "seq", scatter_dimension=0, tiled=True
        ).astype(jnp.float32),
        lax.psum_scatter(
            vector_terms[6].astype(jnp.bfloat16), "seq", scatter_dimension=0, tiled=True
        ).astype(jnp.float32),
        lax.psum_scatter(
            vector_terms[7].astype(jnp.bfloat16), "seq", scatter_dimension=0, tiled=True
        ).astype(jnp.float32),
        lax.psum_scatter(
            vector_terms[8].astype(jnp.bfloat16), "seq", scatter_dimension=0, tiled=True
        ).astype(jnp.float32),
        lax.psum_scatter(
            vector_terms[9].astype(jnp.bfloat16), "seq", scatter_dimension=0, tiled=True
        ).astype(jnp.float32),
        lax.psum_scatter(
            vector_terms[10].astype(jnp.bfloat16), "seq", scatter_dimension=0, tiled=True
        ).astype(jnp.float32),
        lax.psum_scatter(
            vector_terms[11].astype(jnp.bfloat16), "seq", scatter_dimension=0, tiled=True
        ).astype(jnp.float32),
        lax.psum_scatter(
            vector_terms[12].astype(jnp.bfloat16), "seq", scatter_dimension=0, tiled=True
        ).astype(jnp.float32),
    )
    rows_summed = (
        lax.psum_scatter(
            columns_summed[0].astype(jnp.bfloat16), "grp", scatter_dimension=0, tiled=True
        ).astype(jnp.float32),
        lax.psum_scatter(
            columns_summed[1].astype(jnp.bfloat16), "grp", scatter_dimension=0, tiled=True
        ).astype(jnp.float32),
        lax.psum_scatter(
            columns_summed[2].astype(jnp.bfloat16), "grp", scatter_dimension=0, tiled=True
        ).astype(jnp.float32),
        lax.psum_scatter(
            columns_summed[3].astype(jnp.bfloat16), "grp", scatter_dimension=0, tiled=True
        ).astype(jnp.float32),
        lax.psum_scatter(
            columns_summed[4].astype(jnp.bfloat16), "grp", scatter_dimension=0, tiled=True
        ).astype(jnp.float32),
        lax.psum_scatter(
            columns_summed[5].astype(jnp.bfloat16), "grp", scatter_dimension=0, tiled=True
        ).astype(jnp.float32),
        lax.psum_scatter(
            columns_summed[6].astype(jnp.bfloat16), "grp", scatter_dimension=0, tiled=True
        ).astype(jnp.float32),
    )
    vector_shares = tuple(columns_summed[7:])
    vectors_summed = lax.psum(
        (
            vector_shares[0],
            vector_shares[1],
            vector_shares[2],
            vector_shares[3],
            vector_shares[4],
            vector_shares[5],
            vector_shares[6],
            vector_shares[7],
            vector_shares[8],
            vector_shares[9],
            vector_shares[10],
            vector_shares[11],
            vector_shares[12],
        ),
        "grp",
    )
    owned = tuple(rows_summed) + tuple(vectors_summed)
    return (result, input_gradient) + tuple(owned[i] for i in (7, 8, 0, 9, 1, 10, 2, 11, 12, 13, 3, 14, 4, 15, 16, 17, 5, 18, 6, 19))


def solution(mesh):
    fast = mesh.shape["grp"] == 4 and mesh.shape["seq"] == 8
    return jax.shard_map(
        on_device_fast if fast else on_device_general,
        mesh=mesh,
        in_specs=(
            P(("grp", "seq"), None, None),
            P(("grp", "seq"), None, None),
            P("grp"),
            P("grp"),
            P("grp", None),
            P("seq"),
            P("seq"),
            P("grp", "seq"),
            P("seq"),
            P("grp", "seq"),
            P("seq"),
            P("grp", "seq"),
            P("seq"),
            P("seq"),
            P("seq"),
            P("grp", "seq"),
            P("seq"),
            P("grp", "seq"),
            P("seq"),
            P("seq"),
            P("seq"),
            P("grp", "seq"),
            P("seq"),
            P("grp", "seq"),
            P("seq"),
        ),
        out_specs=(
            P(("grp", "seq"), None, None),
            P(("grp", "seq"), None, None),
            P("seq"),
            P("seq"),
            P("grp", "seq"),
            P("seq"),
            P("grp", "seq"),
            P("seq"),
            P("grp", "seq"),
            P("seq"),
            P("seq"),
            P("seq"),
            P("grp", "seq"),
            P("seq"),
            P("grp", "seq"),
            P("seq"),
            P("seq"),
            P("seq"),
            P("grp", "seq"),
            P("seq"),
            P("grp", "seq"),
            P("seq"),
        ),
        check_vma=False,
    )
```
